32 devices in a mesh: groups: 2 (over y), mom: 4 (over z), tm: 4 (over x, core).
Axes of the slice: x: 2, y: 2, z: 4, core: 2. Of those that a mesh axis runs over, the one named last changes fastest.
Arguments:
- panel_start: float32 [256, 4, 64, 512], P('mom', 'groups', None, 'tm'), parts along dimension 1, may hold values from -6 to 6
- block_guess: float32 [256, 4, 64, 128], P('mom', 'groups', 'tm'), parts along dimension 1, may hold values from -6 to 6
- coupling: float32 [2], P('groups'), parts along dimension 0, may hold values from 0.3 to 0.6
- slab_owner: int32 [8], P('groups'), parts along dimension 0, may hold values from 0 to 3, each once
- expiring: int32 [2], P('groups'), parts along dimension 0, may hold values from 0 to 3
- ordering: int32 [256], replicated, may hold values from 0 to 255, each once
Outputs:
- history_out: float32 [256, 4, 64, 512], P('mom', 'groups', None, 'tm'), parts along dimension 1
The draws below stay inside these ranges and needn't reach their ends.
There are 2 independent parts, one for each index of `groups`. The reference program is written for one: setup_inputs(seed, part) draws one part's arguments, and reference() takes and returns one part's arrays. A program takes and returns all parts, laid end to end along the dimension named above; an argument that names none is the same for every part. Nothing has to cross between parts.
Inputs may be any that keep to these rules, and one draw needn't show every extreme that they name: `slab_owner`: entry s is the column block that holds history slab s; each block once. `ordering`: entry j is qx * 16 + qy for the momentum of stored row j; each momentum once.
All inputs are finite; a program needn't handle non-finite values.
Results may differ from the reference program's by a relative error of at most 0.0001.
Values sent between devices are 32-bit elements; how exact they have to be, the bound alone decides.
A program may use at most 128 MiB of HBM per device.

```python
import math
import jax
import jax.numpy as jnp
from jax import lax

LSIDE = 16
K = 256
SPIN = 2
PANEL = 64
PASSES = 2
HIST = 256
N_TM = 4


def block_levels(key, shape, cuts, smallest, largest):
    gain, own = 1.0, jax.random.fold_in(key, 6)
    for axis_at, shards_of in cuts:
        heights = jnp.exp(jax.random.uniform(jax.random.fold_in(own, axis_at), (shards_of,), jnp.float32, smallest / len(cuts), largest / len(cuts)))
        gain = gain * jnp.repeat(heights, shape[axis_at] // shards_of).reshape([-1 if axis == axis_at else 1 for axis in range(len(shape))])
    return gain


def normal_values(stream_key, extent, width, most, cuts=(), kind=jnp.bfloat16):
    values = jax.random.normal(stream_key, extent, jnp.float32) * width
    if len(cuts) > 0:
        values = block_levels(stream_key, extent, cuts, -0.22, 0.18) * values
    return jnp.clip(values, min=-most, max=most).astype(kind)


def setup_inputs(seed: int = 0, part: int = 0) -> dict:
    keys = jax.random.split(jax.random.key(seed), 7)
    part_keys = jax.random.split(jax.random.fold_in(keys[6], part), 7)
    panel_start = normal_values(part_keys[0], (K, SPIN, PANEL, 2 * HIST), 1.0, 6.0, ((0, 4), (3, 4)), jnp.float32)
    block_guess = normal_values(part_keys[1], (K, SPIN, PANEL, 2 * PANEL), 1.0, 6.0, ((0, 4), (2, 4)), jnp.float32)
    coupling = jnp.clip(jnp.exp(jax.random.uniform(part_keys[2], (1,), jnp.float32, math.log(0.3), math.log(0.6))), 0.3, 0.6)
    slab_owner = jax.random.permutation(part_keys[3], N_TM).astype(jnp.int32)
    expiring = jax.random.randint(part_keys[4], (1,), 0, N_TM).astype(jnp.int32)
    ordering = jax.random.permutation(keys[5], K).astype(jnp.int32)
    return dict(panel_start=panel_start, block_guess=block_guess, coupling=coupling, slab_owner=slab_owner, expiring=expiring, ordering=ordering)


def product(left, right):
    return jnp.dot(left, right, precision=lax.Precision.HIGHEST, preferred_element_type=jnp.float32)

def contract(pattern, left, right):
    return jnp.einsum(pattern, left, right, precision=lax.Precision.HIGHEST, preferred_element_type=jnp.float32)

def tables(ordering):
    site_index = jnp.arange(K, dtype=jnp.int32)
    site_x = site_index // LSIDE
    site_y = site_index % LSIDE
    mom_x = ordering // LSIDE
    mom_y = ordering % LSIDE
    phases = (site_x[:, None] * mom_x[None, :] + site_y[:, None] * mom_y[None, :]) % LSIDE
    angles = phases.astype(jnp.float32) * (2.0 * math.pi / LSIDE)
    mirror = (-site_x % LSIDE * LSIDE + -site_y % LSIDE).astype(jnp.int32)
    return (jnp.cos(angles) / LSIDE, jnp.sin(angles) / LSIDE, mirror)

def site_sigma(mom_re, mom_im, cos_table, sin_table, mirror, strength):
    layout = mom_re.shape
    flat_re = mom_re.reshape(K, -1)
    flat_im = mom_im.reshape(K, -1)
    site_re = (product(cos_table, flat_re) - product(sin_table, flat_im)).reshape(layout)
    site_im = (product(cos_table, flat_im) + product(sin_table, flat_re)).reshape(layout)
    other_re = site_re[:, ::-1]
    other_im = site_im[:, ::-1]
    pair_re = site_re * other_re - site_im * other_im
    pair_im = site_re * other_im + site_im * other_re
    back_re = jnp.take(other_re, mirror, axis=0)
    back_im = jnp.take(other_im, mirror, axis=0)
    sig_re = (-strength * (pair_re * back_re + pair_im * back_im)).reshape(K, -1)
    sig_im = (-strength * (pair_im * back_re - pair_re * back_im)).reshape(K, -1)
    out_re = product(cos_table.T, sig_re) + product(sin_table.T, sig_im)
    out_im = product(cos_table.T, sig_im) - product(sin_table.T, sig_re)
    return (out_re.reshape(layout), out_im.reshape(layout))

def reference(panel_start, block_guess, coupling, slab_owner, expiring, ordering):
    cos_table, sin_table, mirror = tables(ordering)
    blocks = jnp.arange(N_TM, dtype=jnp.int32)
    slab_of = lax.optimization_barrier(jnp.sum(blocks[None, :] * (slab_owner[None, :] == blocks[:, None]).astype(jnp.int32), axis=1))
    position = (slab_of - expiring[0]) % N_TM
    times = position[:, None] * PANEL + jnp.arange(PANEL, dtype=jnp.int32)[None, :]
    window = N_TM * PANEL
    weights = jnp.exp(-1.5 * (window - 1 - times).astype(jnp.float32) / window) / math.sqrt(window)
    strength = coupling[0] * coupling[0]
    step_scale = 1.0 / math.sqrt(PANEL)
    split = panel_start.reshape(K, SPIN, PANEL, N_TM, 2, PANEL)
    start_re = split[:, :, :, :, 0, :]
    start_im = split[:, :, :, :, 1, :]
    current_re, current_im = (start_re, start_im)
    conv_re = jnp.zeros((K, SPIN, PANEL, PANEL), jnp.float32)
    conv_im = jnp.zeros((K, SPIN, PANEL, PANEL), jnp.float32)
    for sweep in range(PASSES):
        sig_re, sig_im = site_sigma(current_re, current_im, cos_table, sin_table, mirror, strength)
        sig_re = sig_re * weights
        sig_im = sig_im * weights
        conv_re = -(contract('ksadu,ksbdu->ksab', sig_re, current_re) + contract('ksadu,ksbdu->ksab', sig_im, current_im))
        conv_im = -(contract('ksadu,ksbdu->ksab', sig_im, current_re) - contract('ksadu,ksbdu->ksab', sig_re, current_im))
        next_re = start_re + step_scale * (contract('ksab,ksbdu->ksadu', conv_re, current_re) - contract('ksab,ksbdu->ksadu', conv_im, current_im))
        next_im = start_im + step_scale * (contract('ksab,ksbdu->ksadu', conv_re, current_im) + contract('ksab,ksbdu->ksadu', conv_im, current_re))
        current_re, current_im = (next_re, next_im)
    guess_re = block_guess[..., :PANEL]
    guess_im = block_guess[..., PANEL:]
    block_re = guess_re + step_scale * (contract('ksab,ksbc->ksac', guess_re, conv_re) - contract('ksab,ksbc->ksac', guess_im, conv_im))
    block_im = guess_im + step_scale * (contract('ksab,ksbc->ksac', guess_re, conv_im) + contract('ksab,ksbc->ksac', guess_im, conv_re))
    history = jnp.stack([current_re, current_im], axis=4)
    block = jnp.stack([block_re, block_im], axis=3)[:, :, :, None]
    owner_expiring = jnp.sum(slab_owner * (blocks == expiring[0]).astype(jnp.int32))
    chosen = (blocks == owner_expiring)[:, None, None]
    merged = jnp.where(chosen, block, history)
    return merged.reshape(K, SPIN, PANEL, 2 * window)
```

```python
import functools
import math

import jax
import jax.numpy as jnp
from jax import lax
from jax.experimental import pallas as pl
from jax.experimental.pallas import tpu as pltpu
from jax.sharding import PartitionSpec as P

LSIDE = 16
K = LSIDE * LSIDE
PANEL = 64
PASSES = 2
SPIN = 2
LANES = 2 * PANEL
CHUNKS = 2
MESH = pl.DeviceIdType.MESH


def tables(ordering):
    bits = LSIDE.bit_length() - 1
    site = lax.broadcasted_iota(jnp.int32, (K, K), 0)
    phases = ((site >> bits) * (ordering >> bits) + (site & (LSIDE - 1)) * (ordering & (LSIDE - 1))) & (LSIDE - 1)
    angles = phases.astype(jnp.float32) * (2.0 * math.pi / LSIDE)
    return jnp.cos(angles) / LSIDE, jnp.sin(angles) / LSIDE


def split(x):
    high = x.astype(jnp.bfloat16)
    return high, (x - high.astype(jnp.float32)).astype(jnp.bfloat16)


def dot3(left, right, transposed=False):
    dims = (((1,), (1 if transposed else 0,)), ((), ()))

    def one(a, b):
        return lax.dot_general(a, b, dims, preferred_element_type=jnp.float32)

    return one(left[0], right[0]) + (one(left[0], right[1]) + one(left[1], right[0]))


def step_kernel(
    n_mom, n_tm, start, guess, ordering, wvec, chosen,
    out, cur, recv, sig, ret, fwd_split, back_split, stk, part, conv, pair_buf, ring_buf, guess_all,
    local_sem, guess_own, fs, fr, rs, rr, ps, pr, ss, sr, gs, gr, qs, qr, ds, dr,
):
    mom, tm = lax.axis_index("mom"), lax.axis_index("tm")
    rows, local_k = cur.shape[3], cur.shape[4]
    group = n_mom * rows
    n_x = n_tm // 2
    half = local_k // 2
    share = half // n_x
    tm_x, core = tm // 2, tm % 2
    step_scale = 1.0 / math.sqrt(PANEL)
    lane = lax.broadcasted_iota(jnp.int32, (1, LANES), 1)
    low = lane < PANEL
    sign = jnp.where(low, -1.0, 1.0).astype(jnp.float32)
    flat_cur = cur.reshape(CHUNKS * SPIN * group * local_k, LANES)
    flat_ret = ret.reshape(CHUNKS * SPIN * group * local_k, LANES)

    def swap(x):
        return pltpu.roll(x, PANEL, 1)

    def rot(x):
        return swap(x) * sign

    barrier = pltpu.get_barrier_semaphore()
    for o in range(1, n_mom):
        pl.semaphore_signal(barrier, inc=1, device_id={"mom": lax.rem(mom + o, n_mom)}, device_id_type=MESH)
    for o in range(1, n_tm):
        pl.semaphore_signal(barrier, inc=1, device_id={"tm": lax.rem(tm + o, n_tm)}, device_id_type=MESH)

    mine = pl.ds(mom * local_k, local_k)
    other_half = pl.ds((1 - core) * half, half)
    share_at = core * half + tm_x * share
    own_share = pl.ds(share_at, share)
    partner = {"tm": tm_x * 2 + (1 - core)}

    def remote(source, target, send, recv_sem, device):
        return pltpu.make_async_remote_copy(
            src_ref=source, dst_ref=target, send_sem=send, recv_sem=recv_sem,
            device_id=device, device_id_type=MESH)

    def forward(n, c, o):
        peer = lax.rem(mom + o, n_mom)
        return remote(cur.at[c, :, peer], recv.at[c, :, :, mine, :], fs.at[n, c, o], fr.at[n, c, o], {"mom": peer})

    def forward_own(n, c):
        return pltpu.make_async_copy(cur.at[c, :, mom], recv.at[c, :, :, mine, :], local_sem.at[n, c, 0])

    def back(n, c, o):
        peer = lax.rem(mom + o, n_mom)
        return remote(
            sig.at[c, :, :, pl.ds(peer * local_k, local_k), :], ret.at[c, :, mom],
            rs.at[n, c, o], rr.at[n, c, o], {"mom": peer})

    def back_own(n, c):
        return pltpu.make_async_copy(sig.at[c, :, :, mine, :], ret.at[c, :, mom], local_sem.at[n, c, 1])

    def pair_up(n, c):
        return remote(part.at[c, other_half], pair_buf.at[c], ps.at[n, c], pr.at[n, c], partner)

    def scatter(n, c, o):
        peer = lax.rem(tm_x + o, n_x)
        return remote(
            part.at[c, pl.ds(core * half + peer * share, share)], ring_buf.at[c, o - 1],
            ss.at[n, c, o], sr.at[n, c, o], {"tm": peer * 2 + core})

    def gather(n, c, o):
        peer = lax.rem(tm_x + o, n_x)
        return remote(
            conv.at[c, own_share], conv.at[c, own_share],
            gs.at[n, c, o], gr.at[n, c, o], {"tm": peer * 2 + core})

    def pair_down(n, c, o):
        held = pl.ds(core * half + lax.rem(tm_x + n_x - o, n_x) * share, share)
        return remote(conv.at[c, held], conv.at[c, held], qs.at[n, c, o], qr.at[n, c, o], partner)

    def pair_down_recv(n, c):
        for o in range(n_x):
            pair_down(n, c, o).wait_recv()

    def guess_copy(o):
        return remote(guess, guess_all.at[tm], ds.at[o], dr.at[o], {"tm": lax.rem(tm + o, n_tm)})

    def guess_local():
        return pltpu.make_async_copy(guess, guess_all.at[tm], guess_own)

    def send_forward(n, c):
        for o in range(1, n_mom):
            forward(n, c, o).start()
        forward_own(n, c).start()

    def keep_stack(n, k, s, c, value):
        turned = rot(value)
        for at, piece in ((c * group, value), (PANEL + c * group, turned)):
            high, rest = split(piece)
            stk[n, 0, k, s, at:at + group, :] = high
            stk[n, 1, k, s, at:at + group, :] = rest

    def first_layout(c):
        @pl.loop(0, local_k)
        def _(k):
            for s in range(SPIN):
                at = ((c * SPIN + s) * group) * local_k + k
                flat_cur[pl.ds(at, group, stride=local_k), :] = start[k, s, c]

    def sigma(n, c):
        for o in range(1, n_mom):
            forward(n, c, o).wait_recv()
        forward_own(n, c).wait()
        if n > 0:
            for o in range(1, n_mom):
                back(n - 1, c, o).wait_send()

        @pl.loop(0, rows)
        def _(i):
            both = jnp.concatenate([recv[c, 0, i], recv[c, 1, i]], axis=1)
            sums = dot3((fwd_split[0], fwd_split[1]), split(both))
            site, mirrored = [], []
            for s in range(SPIN):
                with_cos = sums[:K, s * LANES:(s + 1) * LANES]
                turned = rot(sums[K:, s * LANES:(s + 1) * LANES])
                site.append(with_cos + turned)
                mirrored.append(with_cos - turned)
            first, second = site
            flipped = swap(second)
            pair = (first * jnp.where(low, second, flipped)
                    + rot(first) * jnp.where(low, flipped, second)) * wvec[...]
            pair_rot = rot(pair)
            tops, bottoms = [], []
            for s in range(SPIN):
                other = mirrored[1 - s]
                flipped = swap(other)
                value = pair * jnp.where(low, other, flipped) - pair_rot * jnp.where(low, flipped, other)
                tops.append(value)
                bottoms.append(-rot(value))
            stacked = jnp.concatenate(
                [jnp.concatenate(tops, axis=1), jnp.concatenate(bottoms, axis=1)], axis=0)
            result = dot3((back_split[0], back_split[1]), split(stacked))
            for s in range(SPIN):
                sig[c, s, i] = result[:, s * LANES:(s + 1) * LANES]

        for o in range(1, n_mom):
            back(n, c, o).start()
        back_own(n, c).start()

    def convolve(n, c):
        for o in range(1, n_mom):
            back(n, c, o).wait_recv()
        back_own(n, c).wait()
        if n > 0:
            pair_up(n - 1, c).wait_send()
            for o in range(n_x):
                pair_down(n - 1, c, o).wait_send()
            for o in range(1, n_x):
                scatter(n - 1, c, o).wait_send()
                gather(n - 1, c, o).wait_send()

        def some(base):
            @pl.loop(0, half, unroll=8)
            def _(i):
                k = base + i
                for s in range(SPIN):
                    at = ((c * SPIN + s) * group) * local_k + k
                    value = split(flat_ret[pl.ds(at, group, stride=local_k), :])
                    part[c, k, s] = dot3(value, (stk[n, 0, k, s], stk[n, 1, k, s]), True)

        some((1 - core) * half)
        pair_up(n, c).start()
        some(core * half)

    def reduce(n, c):
        pair_up(n, c).wait_recv()

        @pl.loop(0, half)
        def _(i):
            part[c, core * half + i] = part[c, core * half + i] + pair_buf[c, i]

        for o in range(1, n_x):
            scatter(n, c, o).start()
        for o in range(1, n_x):
            scatter(n, c, o).wait_recv()

        @pl.loop(0, share)
        def _(i):
            total = part[c, share_at + i]
            for o in range(1, n_x):
                total = total + ring_buf[c, o - 1, i]
            conv[c, share_at + i] = total

        for o in range(1, n_x):
            gather(n, c, o).start()
        pair_down(n, c, 0).start()
        for o in range(1, n_x):
            gather(n, c, o).wait_recv()
            pair_down(n, c, o).start()

    def update(n, c):
        for o in range(1, n_mom):
            forward(n, c, o).wait_send()

        def some(base):
            @pl.loop(0, half, unroll=8)
            def _(i):
                k = base + i
                for s in range(SPIN):
                    new = start[k, s, c] + step_scale * dot3(
                        split(conv[c, k, s]), (stk[n, 0, k, s], stk[n, 1, k, s]))
                    at = ((c * SPIN + s) * group) * local_k + k
                    flat_cur[pl.ds(at, group, stride=local_k), :] = new
                    keep_stack(n + 1, k, s, c, new)

        some(core * half)
        pair_down_recv(n, c)
        some((1 - core) * half)

    def finish(n):
        is_block = chosen[...] > 0.5

        def some(base):
            @pl.loop(0, half, unroll=4)
            def _(i):
                k = base + i
                for s in range(SPIN):
                    whole = jnp.concatenate([conv[c, k, s] for c in range(CHUNKS)], axis=0)
                    d = jnp.concatenate([guess_all[t, k, s] for t in range(n_tm)], axis=0)
                    first = jnp.concatenate([start[k, s, c] for c in range(CHUNKS)], axis=0)
                    panel = stk[n, 0, k, s].astype(jnp.float32) + stk[n, 1, k, s].astype(jnp.float32)
                    right = jnp.where(is_block, jnp.concatenate([whole, rot(whole)], axis=0), panel)
                    left = jnp.where(is_block, d, whole)
                    new = jnp.where(is_block, d, first) + step_scale * dot3(split(left), split(right))
                    for c in range(CHUNKS):
                        out[k, s, c] = new[c * group:(c + 1) * group, :]

        for c in range(CHUNKS - 1):
            pair_down_recv(n, c)
        some(core * half)
        pair_down_recv(n, CHUNKS - 1)
        some((1 - core) * half)

    first_layout(0)
    pl.semaphore_wait(barrier, n_mom + n_tm - 2)
    send_forward(0, 0)
    for c in range(1, CHUNKS):
        first_layout(c)
        send_forward(0, c)
    for o in range(1, n_tm):
        guess_copy(o).start()
    guess_local().start()

    for at, table in enumerate(tables(ordering[...])):
        fwd_split[0, at * K:(at + 1) * K, :], fwd_split[1, at * K:(at + 1) * K, :] = split(table)
        turned = split(table.T)
        back_split[0, :, at * K:(at + 1) * K], back_split[1, :, at * K:(at + 1) * K] = turned

    @pl.loop(0, local_k, unroll=4)
    def _(k):
        for s in range(SPIN):
            for c in range(CHUNKS):
                keep_stack(0, k, s, c, start[k, s, c])

    for n in range(PASSES):
        for c in range(CHUNKS):
            sigma(n, c)
        for c in range(CHUNKS):
            convolve(n, c)
            reduce(n, c)
            if n < PASSES - 1:
                update(n, c)
                send_forward(n + 1, c)

    for o in range(1, n_tm):
        guess_copy(o).wait_recv()
    guess_local().wait()
    finish(PASSES - 1)

    n = PASSES - 1
    for c in range(CHUNKS):
        pair_up(n, c).wait_send()
        for o in range(n_x):
            pair_down(n, c, o).wait_send()
        for o in range(1, n_x):
            scatter(n, c, o).wait_send()
            gather(n, c, o).wait_send()
        for o in range(1, n_mom):
            forward(n, c, o).wait_send()
            back(n, c, o).wait_send()
    for o in range(1, n_tm):
        guess_copy(o).wait_send()


def panel_step(n_mom, n_tm, start, guess, ordering, wvec, chosen):
    local_k = start.shape[0]
    group = start.shape[3]
    rows = group // n_mom
    share = local_k // n_tm
    panel = (CHUNKS, SPIN, n_mom, rows, local_k, LANES)
    sites = (CHUNKS, SPIN, rows, K, LANES)
    f32, bf16 = jnp.float32, jnp.bfloat16
    dma = pltpu.SemaphoreType.DMA
    vmem = pl.BlockSpec(memory_space=pltpu.VMEM)
    one, many_mom, many_x = (PASSES, CHUNKS), (PASSES, CHUNKS, n_mom), (PASSES, CHUNKS, n_tm // 2)
    return pl.pallas_call(
        functools.partial(step_kernel, n_mom, n_tm),
        out_shape=jax.ShapeDtypeStruct(start.shape, f32),
        in_specs=[vmem] * 5,
        out_specs=vmem,
        scratch_shapes=[
            pltpu.VMEM(panel, f32),
            pltpu.VMEM(sites, f32),
            pltpu.VMEM(sites, f32),
            pltpu.VMEM(panel, f32),
            pltpu.VMEM((2, 2 * K, K), bf16),
            pltpu.VMEM((2, K, 2 * K), bf16),
            pltpu.VMEM((PASSES, 2, local_k, SPIN, LANES, LANES), bf16),
            pltpu.VMEM((CHUNKS, local_k, SPIN, group, LANES), f32),
            pltpu.VMEM((CHUNKS, local_k, SPIN, group, LANES), f32),
            pltpu.VMEM((CHUNKS, local_k // 2, SPIN, group, LANES), f32),
            pltpu.VMEM((CHUNKS, max(n_tm // 2 - 1, 1), share, SPIN, group, LANES), f32),
            pltpu.VMEM((n_tm,) + guess.shape, f32),
            dma(one + (2,)), dma,
            dma(many_mom), dma(many_mom), dma(many_mom), dma(many_mom),
            dma(one), dma(one),
            dma(many_x), dma(many_x), dma(many_x), dma(many_x),
            dma(many_x), dma(many_x),
            dma((n_tm,)), dma((n_tm,)),
        ],
        compiler_params=pltpu.CompilerParams(
            collective_id=0, has_side_effects=True, vmem_limit_bytes=63 * 1024 * 1024),
        name="panel_step",
    )(start, guess, ordering, wvec, chosen)


SUBLANES = 8
CHUNK = 2
LAG = 2
LEAD = 2


def block_transpose(blocks, lane, width):
    blocks = list(blocks)
    bit = 1
    while bit < len(blocks):
        keep = (lane // width) % (2 * bit) < bit
        for p in range(len(blocks)):
            if p & bit == 0:
                a, b = blocks[p], blocks[p + bit]
                blocks[p] = jnp.where(keep, a, pltpu.roll(b, bit * width, 1))
                blocks[p + bit] = jnp.where(keep, pltpu.roll(a, LANES - bit * width, 1), b)
        bit *= 2
    return blocks


def share_kernel(
    n, start, guess, ordering, wvec, chosen,
    out, snd, recv, sig, rx_g, rx_s, stk, rbuf, lbuf, tot, guess_all, fwd_split, back_split,
    fl, fs, fr, gl, gs, gr, sl, ss, sr, tl, ts, tr, rs, rr, ls, lr, credit, room, cl, cs, cr,
    al, aps, apr, axs, axr, aqs, aqr,
):
    mom, tm = lax.axis_index("mom"), lax.axis_index("tm")
    local_k = start.shape[0]
    quarter = local_k // n
    rows = PANEL // n
    width = PANEL // n
    halves = rows // SUBLANES
    half_rows = n * SUBLANES
    subs = quarter // SUBLANES
    per_half = n * subs
    pieces = halves * per_half
    chunks = rows // CHUNK
    half_chunks = SUBLANES // CHUNK
    n_x = n // 2
    tm_x, core = tm // 2, tm % 2
    partner = {"tm": tm_x * 2 + (1 - core)}
    step_scale = 1.0 / math.sqrt(PANEL)
    lane = lax.broadcasted_iota(jnp.int32, (1, LANES), 1)
    low = lane < PANEL
    sign = jnp.where(low, -1.0, 1.0).astype(jnp.float32)
    flat = n * rows * SPIN * local_k
    flat_snd = snd.reshape(flat, LANES)
    flat_recv = recv.reshape(flat, LANES)
    flat_sig = sig.reshape(flat, LANES)
    flat_rx_g = rx_g.reshape(flat, LANES)
    flat_rx_s = rx_s.reshape(flat, LANES)
    own_first = rx_g.reshape(local_k, SPIN, PANEL, LANES)
    own_last = recv.reshape(halves, local_k, SPIN, half_rows, LANES)
    near_left = mom < n // 2

    def swap(x):
        return pltpu.roll(x, PANEL, 1)

    def rot(x):
        return swap(x) * sign

    barrier = pltpu.get_barrier_semaphore()
    for o in range(1, n):
        pl.semaphore_signal(barrier, inc=1, device_id={"mom": lax.rem(mom + o, n)}, device_id_type=MESH)
    for o in range(1, n):
        pl.semaphore_signal(barrier, inc=1, device_id={"tm": lax.rem(tm + o, n)}, device_id_type=MESH)

    def remote(source, target, send, recv_sem, device):
        return pltpu.make_async_remote_copy(
            src_ref=source, dst_ref=target, send_sem=send, recv_sem=recv_sem,
            device_id=device, device_id_type=MESH)

    def local(source, target, sem):
        return pltpu.make_async_copy(source, target, sem)

    def span(q):
        return pl.ds(q * CHUNK, CHUNK)

    def forward(q, o):
        peer = lax.rem(mom + o, n)
        return remote(snd.at[peer, span(q)], recv.at[span(q), :, mom], fs.at[q, o], fr.at[q, o], {"mom": peer})

    def forward_own(q):
        return local(snd.at[mom, span(q)], recv.at[span(q), :, mom], fl.at[q])

    def panel_out(q, o):
        peer = lax.rem(tm + o, n)
        return remote(recv.at[span(q), :, :, peer], rx_g.at[tm, span(q)], gs.at[q, o], gr.at[q, o], {"tm": peer})

    def panel_own(q):
        return local(recv.at[span(q), :, :, tm], rx_g.at[tm, span(q)], gl.at[q])

    def sigma_out(n_pass, q, o):
        peer = lax.rem(tm + o, n)
        return remote(
            sig.at[span(q), :, :, peer], rx_s.at[tm, span(q)], ss.at[n_pass, q, o], sr.at[n_pass, q, o], {"tm": peer})

    def sigma_own(n_pass, q):
        return local(sig.at[span(q), :, :, tm], rx_s.at[tm, span(q)], sl.at[n_pass, q])

    def place(p):
        half, rest = p // per_half, p % per_half
        sub, turn = rest // n, rest % n
        odd = turn % 2
        block = (1 - odd) * (n - 1 - turn // 2) + odd * (turn // 2)
        return half, sub, block

    def next_out(p, o):
        half, sub, block = place(p)
        peer = lax.rem(tm + o, n)
        at, ks = pl.ds(half * SUBLANES, SUBLANES), pl.ds(sub * SUBLANES, SUBLANES)
        return remote(
            snd.at[peer, at, :, block, ks], recv.at[at, :, block, tm, ks], ts.at[p, o], tr.at[p, o], {"tm": peer})

    def next_own(p):
        half, sub, block = place(p)
        at, ks = pl.ds(half * SUBLANES, SUBLANES), pl.ds(sub * SUBLANES, SUBLANES)
        return local(snd.at[tm, at, :, block, ks], recv.at[at, :, block, tm, ks], tl.at[p])

    def window(p):
        half, sub, block = place(p)
        return pl.ds(block * quarter + sub * SUBLANES, SUBLANES), pl.ds(half * half_rows, half_rows)

    def right_out(n_pass, p):
        ks, at = window(p)
        return remote(
            rbuf.at[ks, :, at], rbuf.at[ks, :, at], rs.at[n_pass, p], rr.at[n_pass, p],
            {"mom": jnp.minimum(mom + 1, n - 1)})

    def left_out(n_pass, p):
        ks, at = window(p)
        return remote(
            lbuf.at[ks, :, at], lbuf.at[ks, :, at], ls.at[n_pass, p], lr.at[n_pass, p],
            {"mom": jnp.maximum(mom - 1, 0)})

    def last_out(half, sub, o):
        at = half * subs + sub
        return remote(
            tot.at[1, pl.ds(sub * SUBLANES, SUBLANES), :, pl.ds(half * half_rows, half_rows)],
            own_last.at[half, pl.ds(tm * quarter + sub * SUBLANES, SUBLANES)],
            cs.at[at, o], cr.at[at, o], {"tm": lax.rem(tm + o, n)})

    def last_own(half, sub):
        return local(
            tot.at[1, pl.ds(sub * SUBLANES, SUBLANES), :, pl.ds(half * half_rows, half_rows)],
            own_last.at[half, pl.ds(tm * quarter + sub * SUBLANES, SUBLANES)], cl.at[half * subs + sub])

    class Spread:
        def __init__(self, at, source, target):
            self.at, self.source, self.target = at, source, target

        def own(self):
            return local(self.source, self.target(tm), al.at[self.at])

        def pair(self):
            return remote(self.source, self.target(tm), aps.at[self.at], apr.at[self.at], partner)

        def across(self, o):
            peer = lax.rem(tm_x + o, n_x)
            return remote(
                self.source, self.target(tm), axs.at[self.at, o], axr.at[self.at, o], {"tm": peer * 2 + core})

        def relay(self, o):
            held = self.target(lax.rem(tm_x + n_x - o, n_x) * 2 + core)
            return remote(held, held, aqs.at[self.at, o], aqr.at[self.at, o], partner)

        def begin(self):
            for o in range(1, n_x):
                self.across(o).start()
            self.pair().start()
            self.own().start()

        def pass_on(self):
            for o in range(1, n_x):
                self.across(o).wait_recv()
                self.relay(o).start()

        def arrive(self):
            self.own().wait()
            self.pair().wait_recv()
            for o in range(1, n_x):
                self.relay(o).wait_recv()
                self.relay(o).wait_send()

        def end(self):
            self.pair().wait_send()
            for o in range(1, n_x):
                self.across(o).wait_send()

    guesses = Spread(0, guess, lambda t: guess_all.at[t])
    firsts = Spread(1, tot.at[0], lambda t: own_first.at[pl.ds(t * quarter, quarter)])

    def spread_rows(target, half, s, k, parts):
        for j, value in enumerate(block_transpose(parts, lane, width)):
            at = ((j * rows + half * SUBLANES) * SPIN + s) * local_k + k
            target[pl.ds(at, SUBLANES, stride=SPIN * local_k), :] = value

    def gather_rows(source, half, s, k):
        parts = []
        for t in range(n):
            at = ((t * rows + half * SUBLANES) * SPIN + s) * local_k + k
            parts.append(source[pl.ds(at, SUBLANES, stride=SPIN * local_k), :])
        return jnp.concatenate(block_transpose(parts, lane, width), axis=0)

    def first_layout(half):
        @pl.loop(0, local_k, unroll=4)
        def _(k):
            for s in range(SPIN):
                parts = [start[k, s, half * half_rows + g * SUBLANES:half * half_rows + (g + 1) * SUBLANES, :]
                         for g in range(n)]
                spread_rows(flat_snd, half, s, k, parts)

    def keep_stack(n_pass, k, s, half, value):
        for base, piece in ((0, value), (PANEL, rot(value))):
            high, rest = split(piece)
            at = pl.ds(pl.multiple_of(base + half * half_rows, half_rows), half_rows)
            stk[n_pass, k, s, 0, at, :] = high
            stk[n_pass, k, s, 1, at, :] = rest

    def first_stack(half):
        @pl.loop(0, half_chunks)
        def _(d):
            q = half * half_chunks + d
            for o in range(1, n):
                panel_out(q, o).wait_recv()
            panel_own(q).wait()

        @pl.loop(0, local_k, unroll=4)
        def _(k):
            for s in range(SPIN):
                keep_stack(0, k, s, half, gather_rows(flat_rx_g, half, s, k))

    def sigma(q):
        @pl.loop(0, CHUNK)
        def _(d):
            i = q * CHUNK + d
            both = jnp.concatenate(
                [flat_recv[pl.ds(pl.multiple_of((i * SPIN + s) * K, K), K), :] for s in range(SPIN)], axis=1)
            sums = dot3((fwd_split[0], fwd_split[1]), split(both))
            site, mirrored = [], []
            for s in range(SPIN):
                with_cos = sums[:K, s * LANES:(s + 1) * LANES]
                turned = rot(sums[K:, s * LANES:(s + 1) * LANES])
                site.append(with_cos + turned)
                mirrored.append(with_cos - turned)
            first, second = site
            flipped = swap(second)
            pair = (first * jnp.where(low, second, flipped)
                    + rot(first) * jnp.where(low, flipped, second)) * wvec[...]
            pair_rot = rot(pair)
            tops, bottoms = [], []
            for s in range(SPIN):
                other = mirrored[1 - s]
                flipped = swap(other)
                value = pair * jnp.where(low, other, flipped) - pair_rot * jnp.where(low, flipped, other)
                tops.append(value)
                bottoms.append(-rot(value))
            stacked = jnp.concatenate(
                [jnp.concatenate(tops, axis=1), jnp.concatenate(bottoms, axis=1)], axis=0)
            result = dot3((back_split[0], back_split[1]), split(stacked))
            for s in range(SPIN):
                flat_sig[pl.ds(pl.multiple_of((i * SPIN + s) * K, K), K), :] = result[:, s * LANES:(s + 1) * LANES]

    def send_sigma(n_pass, q):
        for o in range(1, n):
            sigma_out(n_pass, q, o).start()
        sigma_own(n_pass, q).start()

    def wait_sigma(n_pass, half):
        @pl.loop(0, half_chunks)
        def _(d):
            q = half * half_chunks + d
            for o in range(1, n):
                sigma_out(n_pass, q, o).wait_recv()
            sigma_own(n_pass, q).wait()

    def second_sigma(q):
        half = q // half_chunks

        @pl.when(q % half_chunks == 0)
        def _():
            @pl.loop(0, per_half)
            def _(d):
                p = half * per_half + d
                for o in range(1, n):
                    next_out(p, o).wait_recv()
                next_own(p).wait()

        for o in range(1, n):
            sigma_out(0, q, o).wait_send()
        sigma(q)
        send_sigma(1, q)

    def convolve(n_pass, p):
        half, sub, block = place(p)

        @pl.when(p % per_half == 0)
        def _():
            wait_sigma(n_pass, half)

        at = pl.ds(pl.multiple_of(half * half_rows, half_rows), half_rows)

        @pl.loop(0, SUBLANES, unroll=SUBLANES)
        def _(m):
            k = block * quarter + sub * SUBLANES + m
            for s in range(SPIN):
                value = split(gather_rows(flat_rx_s, half, s, k))
                out[k, s, at, :] = dot3(value, (stk[n_pass, k, s, 0], stk[n_pass, k, s, 1]), True)

    def each(p, body):
        half, sub, block = place(p)
        at = pl.ds(pl.multiple_of(half * half_rows, half_rows), half_rows)

        @pl.loop(0, SUBLANES)
        def _(m):
            k = block * quarter + sub * SUBLANES + m
            for s in range(SPIN):
                body(k, s, at, sub * SUBLANES + m)

    def flows(n_pass, p):
        block = place(p)[2]
        if n_pass == 0:
            yes = block >= 0
            return yes, yes, yes, yes, yes
        return block >= mom, block > mom, block <= mom, block < mom, block == mom

    def origin(n_pass, p):
        _, send_right, _, send_left, _ = flows(n_pass, p)

        @pl.when(mom == 0)
        def _():
            def body(k, s, at, m):
                rbuf[k, s, at, :] = out[k, s, at, :]
            each(p, body)

            @pl.when(send_right)
            def _():
                right_out(n_pass, p).start()

        @pl.when(mom == n - 1)
        def _():
            def body(k, s, at, m):
                lbuf[k, s, at, :] = out[k, s, at, :]
            each(p, body)

            @pl.when(send_left)
            def _():
                left_out(n_pass, p).start()

    def near_step(n_pass, p):
        from_left, send_right, from_right, send_left, _ = flows(n_pass, p)

        @pl.when(near_left & (mom > 0) & from_left)
        def _():
            right_out(n_pass, p).wait_recv()

            def body(k, s, at, m):
                rbuf[k, s, at, :] = rbuf[k, s, at, :] + out[k, s, at, :]
            each(p, body)

            @pl.when(send_right)
            def _():
                right_out(n_pass, p).start()

        @pl.when((mom >= n // 2) & (mom < n - 1) & from_right)
        def _():
            left_out(n_pass, p).wait_recv()

            def body(k, s, at, m):
                lbuf[k, s, at, :] = lbuf[k, s, at, :] + out[k, s, at, :]
            each(p, body)

            @pl.when(send_left)
            def _():
                left_out(n_pass, p).start()

    def far_step(n_pass, p):
        from_left, send_right, from_right, send_left, keep = flows(n_pass, p)

        def one(mine, other, outer, send, copy):
            copy.wait_recv()
            if n_pass == 0:
                def body(k, s, at, m):
                    arrived, held = other[k, s, at, :], out[k, s, at, :]
                    other[k, s, at, :] = arrived + held
                    out[k, s, at, :] = mine[k, s, at, :] + arrived
                each(p, body)
            else:
                @pl.when(send)
                def _():
                    def body(k, s, at, m):
                        other[k, s, at, :] = other[k, s, at, :] + out[k, s, at, :]
                    each(p, body)

                @pl.when(keep)
                def _():
                    def body(k, s, at, m):
                        tot[1, m, s, at, :] = mine[k, s, at, :] + other[k, s, at, :]
                    each(p, body)

            @pl.when(outer & send)
            def _():
                copy.start()

        @pl.when(near_left & from_right)
        def _():
            one(rbuf, lbuf, mom > 0, send_left, left_out(n_pass, p))

        @pl.when((mom >= n // 2) & from_left)
        def _():
            one(lbuf, rbuf, mom < n - 1, send_right, right_out(n_pass, p))

    def update(p):
        half, sub, block = place(p)
        at = pl.ds(pl.multiple_of(half * half_rows, half_rows), half_rows)

        @pl.when(block == mom)
        def _():
            def body(k, s, at, m):
                tot[0, m, s, at, :] = out[k, s, at, :]
            each(p, body)

        @pl.loop(0, SUBLANES, unroll=SUBLANES)
        def _(m):
            k = block * quarter + sub * SUBLANES + m
            for s in range(SPIN):
                old = stk[0, k, s, 0, at, :].astype(jnp.float32) + stk[0, k, s, 1, at, :].astype(jnp.float32)
                new = old + step_scale * dot3(split(out[k, s, at, :]), (stk[0, k, s, 0], stk[0, k, s, 1]))
                keep_stack(1, k, s, half, new)
                spread_rows(
                    flat_snd, half, s, k, [new[g * SUBLANES:(g + 1) * SUBLANES, :] for g in range(n)])

        for o in range(1, n):
            next_out(p, o).start()
        next_own(p).start()

    def own_panel(group):
        @pl.loop(0, SUBLANES, unroll=4)
        def _(m):
            k = group * SUBLANES + m
            for s in range(SPIN):
                first = start[k, s]
                right = jnp.concatenate([first, rot(first)], axis=0)
                own_first[k, s] = first + step_scale * dot3(split(own_first[k, s]), split(right))

    def finish(sub):
        is_block = chosen[...] > 0.5
        for half in range(halves):
            for o in range(1, n):
                last_out(half, sub, o).wait_recv()
            last_own(half, sub).wait()

        @pl.loop(0, n * SUBLANES, unroll=4)
        def _(d):
            k = (d // SUBLANES) * quarter + sub * SUBLANES + d % SUBLANES
            for s in range(SPIN):
                whole = jnp.concatenate([own_last[half, k, s] for half in range(halves)], axis=0)
                d_rows = jnp.concatenate([guess_all[t, k, s] for t in range(n)], axis=0)
                right = jnp.where(is_block, whole, own_first[k, s])
                left = jnp.where(is_block, d_rows, whole)
                right = jnp.concatenate([right, rot(right)], axis=0)
                out[k, s] = jnp.where(is_block, d_rows, start[k, s]) + step_scale * dot3(split(left), split(right))

    first_layout(0)
    pl.semaphore_wait(barrier, 2 * n - 2)
    for half in range(halves):
        if half > 0:
            first_layout(half)
        for q in range(half * half_chunks, (half + 1) * half_chunks):
            for o in range(1, n):
                forward(q, o).start()
            forward_own(q).start()
        if half == 0:
            guesses.begin()

    for at, table in enumerate(tables(ordering[...])):
        fwd_split[0, at * K:(at + 1) * K, :], fwd_split[1, at * K:(at + 1) * K, :] = split(table)
        turned = split(table.T)
        back_split[0, :, at * K:(at + 1) * K], back_split[1, :, at * K:(at + 1) * K] = turned

    @pl.loop(0, chunks + 1)
    def _(q):
        @pl.when(q < chunks)
        def _():
            for o in range(1, n):
                forward(q, o).wait_recv()
            forward_own(q).wait()
            for o in range(1, n):
                panel_out(q, o).start()
            panel_own(q).start()
            sigma(q)
            send_sigma(0, q)

        for half in range(halves - 1):
            @pl.when(q == (half + 1) * half_chunks + 1)
            def _():
                first_stack(half)

        @pl.when(q == chunks)
        def _():
            first_stack(halves - 1)

    guesses.pass_on()

    @pl.loop(0, chunks)
    def _(q):
        for o in range(1, n):
            forward(q, o).wait_send()
            panel_out(q, o).wait_send()

    for o in range(1, n):
        pl.semaphore_signal(room, inc=1, device_id={"tm": lax.rem(tm + o, n)}, device_id_type=MESH)

    sigma_at = per_half + LAG + per_half + 1

    @pl.loop(0, pieces + per_half + LAG)
    def _(t):
        @pl.when(t < pieces)
        def _():
            convolve(0, t)
            origin(0, t)

        @pl.when((t >= per_half) & (t - per_half < pieces))
        def _():
            near_step(0, t - per_half)

        @pl.when(t >= per_half + LAG)
        def _():
            p = t - per_half - LAG
            far_step(0, p)

            @pl.when(p == 0)
            def _():
                pl.semaphore_wait(room, n - 1)

            update(p)

        @pl.when((t >= sigma_at) & (t < sigma_at + (halves - 1) * half_chunks))
        def _():
            second_sigma(t - sigma_at)

    @pl.loop(0, pieces)
    def _(p):
        @pl.when(mom < n - 1)
        def _():
            right_out(0, p).wait_send()

        @pl.when(mom > 0)
        def _():
            left_out(0, p).wait_send()

    @pl.when(mom > 0)
    def _():
        pl.semaphore_signal(credit.at[1], inc=1, device_id={"mom": jnp.maximum(mom - 1, 0)}, device_id_type=MESH)

    @pl.when(mom < n - 1)
    def _():
        pl.semaphore_signal(credit.at[0], inc=1, device_id={"mom": jnp.minimum(mom + 1, n - 1)}, device_id_type=MESH)

    firsts.begin()

    @pl.when(mom > 0)
    def _():
        pl.semaphore_wait(credit.at[0], 1)

    @pl.when(mom < n - 1)
    def _():
        pl.semaphore_wait(credit.at[1], 1)

    @pl.loop(0, pieces + LEAD + LAG)
    def _(t):
        @pl.when(t < pieces)
        def _():
            convolve(1, t)
            origin(1, t)

        @pl.when(t < half_chunks)
        def _():
            second_sigma((halves - 1) * half_chunks + t)

        @pl.when((t >= LEAD) & (t - LEAD < pieces))
        def _():
            near_step(1, t - LEAD)

        @pl.when(t >= LEAD + LAG)
        def _():
            p = t - LEAD - LAG
            far_step(1, p)
            half, sub, block = place(p)

            @pl.when(block == mom)
            def _():
                for o in range(1, n):
                    last_out(half, sub, o).start()
                last_own(half, sub).start()

        @pl.when(t == per_half)
        def _():
            firsts.pass_on()
            firsts.arrive()

        @pl.when((t >= per_half) & (t < per_half + local_k // SUBLANES))
        def _():
            own_panel(t - per_half)

    guesses.arrive()
    for sub in range(subs):
        finish(sub)

    @pl.loop(0, pieces)
    def _(p):
        _, send_right, _, send_left, _ = flows(1, p)

        @pl.when((mom < n - 1) & send_right)
        def _():
            right_out(1, p).wait_send()

        @pl.when((mom > 0) & send_left)
        def _():
            left_out(1, p).wait_send()

        for o in range(1, n):
            next_out(p, o).wait_send()

    @pl.loop(0, chunks)
    def _(q):
        for o in range(1, n):
            sigma_out(1, q, o).wait_send()

    for half in range(halves):
        for sub in range(subs):
            for o in range(1, n):
                last_out(half, sub, o).wait_send()
    guesses.end()
    firsts.end()


def share_step(n, start, guess, ordering, wvec, chosen):
    local_k = start.shape[0]
    quarter, rows = local_k // n, PANEL // n
    pieces = (rows // SUBLANES) * n * (quarter // SUBLANES)
    chunks, ends = rows // CHUNK, (rows // SUBLANES) * (quarter // SUBLANES)
    f32, bf16 = jnp.float32, jnp.bfloat16
    dma = pltpu.SemaphoreType.DMA
    vmem = pl.BlockSpec(memory_space=pltpu.VMEM)
    moved = pltpu.VMEM((n, rows, SPIN, n, quarter, LANES), f32)
    grid = pltpu.VMEM((rows, SPIN, n, n, quarter, LANES), f32)
    square = (local_k, SPIN, PANEL, LANES)
    return pl.pallas_call(
        functools.partial(share_kernel, n),
        out_shape=jax.ShapeDtypeStruct(start.shape, f32),
        in_specs=[vmem] * 5,
        out_specs=vmem,
        scratch_shapes=[
            moved, grid, grid, moved, moved,
            pltpu.VMEM((PASSES, local_k, SPIN, 2, 2 * PANEL, LANES), bf16),
            pltpu.VMEM(square, f32), pltpu.VMEM(square, f32),
            pltpu.VMEM((PASSES, quarter, SPIN, PANEL, LANES), f32),
            pltpu.VMEM((n,) + guess.shape, f32),
            pltpu.VMEM((2, 2 * K, K), bf16),
            pltpu.VMEM((2, K, 2 * K), bf16),
            dma((chunks,)), dma((chunks, n)), dma((chunks, n)),
            dma((chunks,)), dma((chunks, n)), dma((chunks, n)),
            dma((PASSES, chunks)), dma((PASSES, chunks, n)), dma((PASSES, chunks, n)),
            dma((pieces,)), dma((pieces, n)), dma((pieces, n)),
            dma((PASSES, pieces)), dma((PASSES, pieces)), dma((PASSES, pieces)), dma((PASSES, pieces)),
            pltpu.SemaphoreType.REGULAR((2,)), pltpu.SemaphoreType.REGULAR,
            dma((ends,)), dma((ends, n)), dma((ends, n)),
            dma((2,)), dma((2,)), dma((2,)), dma((2, n)), dma((2, n)), dma((2, n)), dma((2, n)),
        ],
        compiler_params=pltpu.CompilerParams(
            collective_id=0, has_side_effects=True, vmem_limit_bytes=63 * 1024 * 1024),
        name="share_step",
    )(start, guess, ordering, wvec, chosen)


def body(panel_start, block_guess, coupling, slab_owner, expiring, ordering):
    slab_count = lax.axis_size("tm")
    n_mom = lax.axis_size("mom")
    own_index = lax.axis_index("tm")
    blocks = jnp.arange(slab_count, dtype=jnp.int32)
    slab_mine = jnp.sum(blocks * (slab_owner == own_index).astype(jnp.int32))
    position = (slab_mine - expiring[0]) % slab_count
    window = slab_count * PANEL
    local_k = panel_start.shape[0]
    shared = n_mom == slab_count and local_k % (SUBLANES * slab_count) == 0 and PANEL % (SUBLANES * slab_count) == 0
    within = jnp.arange(PANEL, dtype=jnp.int32)
    if shared:
        share = PANEL // n_mom
        within = lax.axis_index("mom") * share + within % share
    times = position * PANEL + within
    weights = jnp.exp(-1.5 * (window - 1 - times).astype(jnp.float32) / window) / math.sqrt(window)
    strength = coupling[0] * coupling[0]
    wvec = (strength * jnp.concatenate([weights, weights]))[None, :]
    owner_expiring = jnp.sum(slab_owner * (blocks == expiring[0]).astype(jnp.int32))
    chosen = jnp.broadcast_to((own_index == owner_expiring).astype(jnp.float32), (1, LANES))
    if shared:
        return share_step(n_mom, panel_start, block_guess, ordering[None, :], wvec, chosen)
    start = panel_start.reshape(local_k, SPIN, CHUNKS, PANEL // CHUNKS, LANES)
    result = panel_step(n_mom, slab_count, start, block_guess, ordering[None, :], wvec, chosen)
    return result.reshape(panel_start.shape)


def solution(mesh):
    return jax.shard_map(
        body,
        mesh=mesh,
        in_specs=(
            P("mom", "groups", None, "tm"),
            P("mom", "groups", "tm", None),
            P("groups"),
            P("groups"),
            P("groups"),
            P(),
        ),
        out_specs=P("mom", "groups", None, "tm"),
        check_vma=False,
    )
```

```python
import functools
import math

import jax
import jax.numpy as jnp
from jax import lax
from jax.experimental import pallas as pl
from jax.experimental.pallas import tpu as pltpu
from jax.sharding import PartitionSpec as P

LSIDE = 16
K = LSIDE * LSIDE
PANEL = 64
PASSES = 2
SPIN = 2
LANES = 2 * PANEL
CHUNKS = 2
MESH = pl.DeviceIdType.MESH


def tables(ordering):
    bits = LSIDE.bit_length() - 1
    site = lax.broadcasted_iota(jnp.int32, (K, K), 0)
    phases = ((site >> bits) * (ordering >> bits) + (site & (LSIDE - 1)) * (ordering & (LSIDE - 1))) & (LSIDE - 1)
    angles = phases.astype(jnp.float32) * (2.0 * math.pi / LSIDE)
    return jnp.cos(angles) / LSIDE, jnp.sin(angles) / LSIDE


def split(x):
    high = x.astype(jnp.bfloat16)
    return high, (x - high.astype(jnp.float32)).astype(jnp.bfloat16)


def dot3(left, right, transposed=False):
    dims = (((1,), (1 if transposed else 0,)), ((), ()))

    def one(a, b):
        return lax.dot_general(a, b, dims, preferred_element_type=jnp.float32)

    return one(left[0], right[0]) + (one(left[0], right[1]) + one(left[1], right[0]))


def step_kernel(
    n_mom, n_tm, start, guess, ordering, wvec, chosen,
    out, cur, recv, sig, ret, fwd_split, back_split, stk, part, conv, pair_buf, ring_buf, guess_all,
    local_sem, guess_own, fs, fr, rs, rr, ps, pr, ss, sr, gs, gr, qs, qr, ds, dr,
):
    mom, tm = lax.axis_index("mom"), lax.axis_index("tm")
    rows, local_k = cur.shape[3], cur.shape[4]
    group = n_mom * rows
    n_x = n_tm // 2
    half = local_k // 2
    share = half // n_x
    tm_x, core = tm // 2, tm % 2
    step_scale = 1.0 / math.sqrt(PANEL)
    lane = lax.broadcasted_iota(jnp.int32, (1, LANES), 1)
    low = lane < PANEL
    sign = jnp.where(low, -1.0, 1.0).astype(jnp.float32)
    flat_cur = cur.reshape(CHUNKS * SPIN * group * local_k, LANES)
    flat_ret = ret.reshape(CHUNKS * SPIN * group * local_k, LANES)

    def swap(x):
        return pltpu.roll(x, PANEL, 1)

    def rot(x):
        return swap(x) * sign

    barrier = pltpu.get_barrier_semaphore()
    for o in range(1, n_mom):
        pl.semaphore_signal(barrier, inc=1, device_id={"mom": lax.rem(mom + o, n_mom)}, device_id_type=MESH)
    for o in range(1, n_tm):
        pl.semaphore_signal(barrier, inc=1, device_id={"tm": lax.rem(tm + o, n_tm)}, device_id_type=MESH)

    mine = pl.ds(mom * local_k, local_k)
    other_half = pl.ds((1 - core) * half, half)
    share_at = core * half + tm_x * share
    own_share = pl.ds(share_at, share)
    partner = {"tm": tm_x * 2 + (1 - core)}

    def remote(source, target, send, recv_sem, device):
        return pltpu.make_async_remote_copy(
            src_ref=source, dst_ref=target, send_sem=send, recv_sem=recv_sem,
            device_id=device, device_id_type=MESH)

    def forward(n, c, o):
        peer = lax.rem(mom + o, n_mom)
        return remote(cur.at[c, :, peer], recv.at[c, :, :, mine, :], fs.at[n, c, o], fr.at[n, c, o], {"mom": peer})

    def forward_own(n, c):
        return pltpu.make_async_copy(cur.at[c, :, mom], recv.at[c, :, :, mine, :], local_sem.at[n, c, 0])

    def back(n, c, o):
        peer = lax.rem(mom + o, n_mom)
        return remote(
            sig.at[c, :, :, pl.ds(peer * local_k, local_k), :], ret.at[c, :, mom],
            rs.at[n, c, o], rr.at[n, c, o], {"mom": peer})

    def back_own(n, c):
        return pltpu.make_async_copy(sig.at[c, :, :, mine, :], ret.at[c, :, mom], local_sem.at[n, c, 1])

    def pair_up(n, c):
        return remote(part.at[c, other_half], pair_buf.at[c], ps.at[n, c], pr.at[n, c], partner)

    def scatter(n, c, o):
        peer = lax.rem(tm_x + o, n_x)
        return remote(
            part.at[c, pl.ds(core * half + peer * share, share)], ring_buf.at[c, o - 1],
            ss.at[n, c, o], sr.at[n, c, o], {"tm": peer * 2 + core})

    def gather(n, c, o):
        peer = lax.rem(tm_x + o, n_x)
        return remote(
            conv.at[c, own_share], conv.at[c, own_share],
            gs.at[n, c, o], gr.at[n, c, o], {"tm": peer * 2 + core})

    def pair_down(n, c, o):
        held = pl.ds(core * half + lax.rem(tm_x + n_x - o, n_x) * share, share)
        return remote(conv.at[c, held], conv.at[c, held], qs.at[n, c, o], qr.at[n, c, o], partner)

    def pair_down_recv(n, c):
        for o in range(n_x):
            pair_down(n, c, o).wait_recv()

    def guess_copy(o):
        return remote(guess, guess_all.at[tm], ds.at[o], dr.at[o], {"tm": lax.rem(tm + o, n_tm)})

    def guess_local():
        return pltpu.make_async_copy(guess, guess_all.at[tm], guess_own)

    def send_forward(n, c):
        for o in range(1, n_mom):
            forward(n, c, o).start()
        forward_own(n, c).start()

    def keep_stack(n, k, s, c, value):
        turned = rot(value)
        for at, piece in ((c * group, value), (PANEL + c * group, turned)):
            high, rest = split(piece)
            stk[n, 0, k, s, at:at + group, :] = high
            stk[n, 1, k, s, at:at + group, :] = rest

    def first_layout(c):
        @pl.loop(0, local_k)
        def _(k):
            for s in range(SPIN):
                at = ((c * SPIN + s) * group) * local_k + k
                flat_cur[pl.ds(at, group, stride=local_k), :] = start[k, s, c]

    def sigma(n, c):
        for o in range(1, n_mom):
            forward(n, c, o).wait_recv()
        forward_own(n, c).wait()
        if n > 0:
            for o in range(1, n_mom):
                back(n - 1, c, o).wait_send()

        @pl.loop(0, rows)
        def _(i):
            both = jnp.concatenate([recv[c, 0, i], recv[c, 1, i]], axis=1)
            sums = dot3((fwd_split[0], fwd_split[1]), split(both))
            site, mirrored = [], []
            for s in range(SPIN):
                with_cos = sums[:K, s * LANES:(s + 1) * LANES]
                turned = rot(sums[K:, s * LANES:(s + 1) * LANES])
                site.append(with_cos + turned)
                mirrored.append(with_cos - turned)
            first, second = site
            flipped = swap(second)
            pair = (first * jnp.where(low, second, flipped)
                    + rot(first) * jnp.where(low, flipped, second)) * wvec[...]
            pair_rot = rot(pair)
            tops, bottoms = [], []
            for s in range(SPIN):
                other = mirrored[1 - s]
                flipped = swap(other)
                value = pair * jnp.where(low, other, flipped) - pair_rot * jnp.where(low, flipped, other)
                tops.append(value)
                bottoms.append(-rot(value))
            stacked = jnp.concatenate(
                [jnp.concatenate(tops, axis=1), jnp.concatenate(bottoms, axis=1)], axis=0)
            result = dot3((back_split[0], back_split[1]), split(stacked))
            for s in range(SPIN):
                sig[c, s, i] = result[:, s * LANES:(s + 1) * LANES]

        for o in range(1, n_mom):
            back(n, c, o).start()
        back_own(n, c).start()

    def convolve(n, c):
        for o in range(1, n_mom):
            back(n, c, o).wait_recv()
        back_own(n, c).wait()
        if n > 0:
            pair_up(n - 1, c).wait_send()
            for o in range(n_x):
                pair_down(n - 1, c, o).wait_send()
            for o in range(1, n_x):
                scatter(n - 1, c, o).wait_send()
                gather(n - 1, c, o).wait_send()

        def some(base):
            @pl.loop(0, half, unroll=8)
            def _(i):
                k = base + i
                for s in range(SPIN):
                    at = ((c * SPIN + s) * group) * local_k + k
                    value = split(flat_ret[pl.ds(at, group, stride=local_k), :])
                    part[c, k, s] = dot3(value, (stk[n, 0, k, s], stk[n, 1, k, s]), True)

        some((1 - core) * half)
        pair_up(n, c).start()
        some(core * half)

    def reduce(n, c):
        pair_up(n, c).wait_recv()

        @pl.loop(0, half)
        def _(i):
            part[c, core * half + i] = part[c, core * half + i] + pair_buf[c, i]

        for o in range(1, n_x):
            scatter(n, c, o).start()
        for o in range(1, n_x):
            scatter(n, c, o).wait_recv()

        @pl.loop(0, share)
        def _(i):
            total = part[c, share_at + i]
            for o in range(1, n_x):
                total = total + ring_buf[c, o - 1, i]
            conv[c, share_at + i] = total

        for o in range(1, n_x):
            gather(n, c, o).start()
        pair_down(n, c, 0).start()
        for o in range(1, n_x):
            gather(n, c, o).wait_recv()
            pair_down(n, c, o).start()

    def update(n, c):
        for o in range(1, n_mom):
            forward(n, c, o).wait_send()

        def some(base):
            @pl.loop(0, half, unroll=8)
            def _(i):
                k = base + i
                for s in range(SPIN):
                    new = start[k, s, c] + step_scale * dot3(
                        split(conv[c, k, s]), (stk[n, 0, k, s], stk[n, 1, k, s]))
                    at = ((c * SPIN + s) * group) * local_k + k
                    flat_cur[pl.ds(at, group, stride=local_k), :] = new
                    keep_stack(n + 1, k, s, c, new)

        some(core * half)
        pair_down_recv(n, c)
        some((1 - core) * half)

    def finish(n):
        is_block = chosen[...] > 0.5

        def some(base):
            @pl.loop(0, half, unroll=4)
            def _(i):
                k = base + i
                for s in range(SPIN):
                    whole = jnp.concatenate([conv[c, k, s] for c in range(CHUNKS)], axis=0)
                    d = jnp.concatenate([guess_all[t, k, s] for t in range(n_tm)], axis=0)
                    first = jnp.concatenate([start[k, s, c] for c in range(CHUNKS)], axis=0)
                    panel = stk[n, 0, k, s].astype(jnp.float32) + stk[n, 1, k, s].astype(jnp.float32)
                    right = jnp.where(is_block, jnp.concatenate([whole, rot(whole)], axis=0), panel)
                    left = jnp.where(is_block, d, whole)
                    new = jnp.where(is_block, d, first) + step_scale * dot3(split(left), split(right))
                    for c in range(CHUNKS):
                        out[k, s, c] = new[c * group:(c + 1) * group, :]

        for c in range(CHUNKS - 1):
            pair_down_recv(n, c)
        some(core * half)
        pair_down_recv(n, CHUNKS - 1)
        some((1 - core) * half)

    first_layout(0)
    pl.semaphore_wait(barrier, n_mom + n_tm - 2)
    send_forward(0, 0)
    for c in range(1, CHUNKS):
        first_layout(c)
        send_forward(0, c)
    for o in range(1, n_tm):
        guess_copy(o).start()
    guess_local().start()

    for at, table in enumerate(tables(ordering[...])):
        fwd_split[0, at * K:(at + 1) * K, :], fwd_split[1, at * K:(at + 1) * K, :] = split(table)
        turned = split(table.T)
        back_split[0, :, at * K:(at + 1) * K], back_split[1, :, at * K:(at + 1) * K] = turned

    @pl.loop(0, local_k, unroll=4)
    def _(k):
        for s in range(SPIN):
            for c in range(CHUNKS):
                keep_stack(0, k, s, c, start[k, s, c])

    for n in range(PASSES):
        for c in range(CHUNKS):
            sigma(n, c)
        for c in range(CHUNKS):
            convolve(n, c)
            reduce(n, c)
            if n < PASSES - 1:
                update(n, c)
                send_forward(n + 1, c)

    for o in range(1, n_tm):
        guess_copy(o).wait_recv()
    guess_local().wait()
    finish(PASSES - 1)

    n = PASSES - 1
    for c in range(CHUNKS):
        pair_up(n, c).wait_send()
        for o in range(n_x):
            pair_down(n, c, o).wait_send()
        for o in range(1, n_x):
            scatter(n, c, o).wait_send()
            gather(n, c, o).wait_send()
        for o in range(1, n_mom):
            forward(n, c, o).wait_send()
            back(n, c, o).wait_send()
    for o in range(1, n_tm):
        guess_copy(o).wait_send()


def panel_step(n_mom, n_tm, start, guess, ordering, wvec, chosen):
    local_k = start.shape[0]
    group = start.shape[3]
    rows = group // n_mom
    share = local_k // n_tm
    panel = (CHUNKS, SPIN, n_mom, rows, local_k, LANES)
    sites = (CHUNKS, SPIN, rows, K, LANES)
    f32, bf16 = jnp.float32, jnp.bfloat16
    dma = pltpu.SemaphoreType.DMA
    vmem = pl.BlockSpec(memory_space=pltpu.VMEM)
    one, many_mom, many_x = (PASSES, CHUNKS), (PASSES, CHUNKS, n_mom), (PASSES, CHUNKS, n_tm // 2)
    return pl.pallas_call(
        functools.partial(step_kernel, n_mom, n_tm),
        out_shape=jax.ShapeDtypeStruct(start.shape, f32),
        in_specs=[vmem] * 5,
        out_specs=vmem,
        scratch_shapes=[
            pltpu.VMEM(panel, f32),
            pltpu.VMEM(sites, f32),
            pltpu.VMEM(sites, f32),
            pltpu.VMEM(panel, f32),
            pltpu.VMEM((2, 2 * K, K), bf16),
            pltpu.VMEM((2, K, 2 * K), bf16),
            pltpu.VMEM((PASSES, 2, local_k, SPIN, LANES, LANES), bf16),
            pltpu.VMEM((CHUNKS, local_k, SPIN, group, LANES), f32),
            pltpu.VMEM((CHUNKS, local_k, SPIN, group, LANES), f32),
            pltpu.VMEM((CHUNKS, local_k // 2, SPIN, group, LANES), f32),
            pltpu.VMEM((CHUNKS, max(n_tm // 2 - 1, 1), share, SPIN, group, LANES), f32),
            pltpu.VMEM((n_tm,) + guess.shape, f32),
            dma(one + (2,)), dma,
            dma(many_mom), dma(many_mom), dma(many_mom), dma(many_mom),
            dma(one), dma(one),
            dma(many_x), dma(many_x), dma(many_x), dma(many_x),
            dma(many_x), dma(many_x),
            dma((n_tm,)), dma((n_tm,)),
        ],
        compiler_params=pltpu.CompilerParams(
            collective_id=0, has_side_effects=True, vmem_limit_bytes=63 * 1024 * 1024),
        name="panel_step",
    )(start, guess, ordering, wvec, chosen)


SUBLANES = 8
CHUNK = 2
AHEAD = 3
LAG = 3
LEAD = (8, 4)


def block_transpose(blocks, lane, width):
    blocks = list(blocks)
    bit = 1
    while bit < len(blocks):
        keep = (lane // width) % (2 * bit) < bit
        for p in range(len(blocks)):
            if p & bit == 0:
                a, b = blocks[p], blocks[p + bit]
                blocks[p] = jnp.where(keep, a, pltpu.roll(b, bit * width, 1))
                blocks[p + bit] = jnp.where(keep, pltpu.roll(a, LANES - bit * width, 1), b)
        bit *= 2
    return blocks


def share_kernel(
    n, start, guess, ordering, coupling, slab_owner, expiring,
    out, snd, recv, sig, rx_g, rx_s, stk_a, stk_b, wvec, rbuf, lbuf, tot, guess_all, fwd_split, back_split,
    fl, fs, fr, gl, gs, gr, sl, ss, sr, tl, ts, tr, rs, rr, ls, lr, credit, room,
    al, aps, apr, axs, axr, aqs, aqr,
):
    mom, tm = lax.axis_index("mom"), lax.axis_index("tm")
    local_k = start.shape[0]
    quarter = local_k // n
    rows = PANEL // n
    width = PANEL // n
    halves = rows // SUBLANES
    half_rows = n * SUBLANES
    subs = quarter // SUBLANES
    per_half = n * subs * SPIN
    pieces = halves * per_half
    chunks = rows // CHUNK
    half_chunks = SUBLANES // CHUNK
    n_x = n // 2
    tm_x, core = tm // 2, tm % 2
    partner = {"tm": tm_x * 2 + (1 - core)}
    step_scale = 1.0 / math.sqrt(PANEL)
    lane = lax.broadcasted_iota(jnp.int32, (1, LANES), 1)
    low = lane < PANEL
    sign = jnp.where(low, -1.0, 1.0).astype(jnp.float32)
    flat = n * rows * SPIN * local_k
    flat_snd = snd.reshape(flat, LANES)
    flat_rx_g = rx_g.reshape(flat, LANES)
    flat_rx_s = rx_s.reshape(flat, LANES)
    own_first = rx_g.reshape(local_k, SPIN, halves, half_rows, LANES)
    part = out.reshape(local_k, SPIN, halves, half_rows, LANES)
    stacks = (stk_a, stk_b)
    own_last = recv.reshape(halves, local_k, SPIN, half_rows, LANES)
    near_left = mom < n // 2

    def swap(x):
        return pltpu.roll(x, PANEL, 1)

    def rot(x):
        return swap(x) * sign

    barrier = pltpu.get_barrier_semaphore()
    for o in range(1, n):
        pl.semaphore_signal(barrier, inc=1, device_id={"mom": lax.rem(mom + o, n)}, device_id_type=MESH)
    for o in range(1, n):
        pl.semaphore_signal(barrier, inc=1, device_id={"tm": lax.rem(tm + o, n)}, device_id_type=MESH)

    def remote(source, target, send, recv_sem, device):
        return pltpu.make_async_remote_copy(
            src_ref=source, dst_ref=target, send_sem=send, recv_sem=recv_sem,
            device_id=device, device_id_type=MESH)

    def local(source, target, sem):
        return pltpu.make_async_copy(source, target, sem)

    def span(q):
        return pl.ds(q * CHUNK, CHUNK)

    def forward(q, o):
        peer = lax.rem(mom + o, n)
        return remote(snd.at[peer, span(q)], recv.at[span(q), :, mom], fs.at[q, o], fr.at[q, o], {"mom": peer})

    def forward_own(q):
        return local(snd.at[mom, span(q)], recv.at[span(q), :, mom], fl.at[q])

    def panel_out(q, o):
        peer = lax.rem(tm + o, n)
        return remote(recv.at[span(q), :, :, peer], rx_g.at[tm, span(q)], gs.at[q, o], gr.at[q, o], {"tm": peer})

    def panel_own(q):
        return local(recv.at[span(q), :, :, tm], rx_g.at[tm, span(q)], gl.at[q])

    def sigma_out(n_pass, q, o):
        peer = lax.rem(tm + o, n)
        return remote(
            sig.at[span(q), :, :, peer], rx_s.at[tm, span(q)], ss.at[n_pass, q, o], sr.at[n_pass, q, o], {"tm": peer})

    def sigma_own(n_pass, q):
        return local(sig.at[span(q), :, :, tm], rx_s.at[tm, span(q)], sl.at[n_pass, q])

    def place(p):
        half, rest = p // per_half, p % per_half
        group, turn = rest // n, rest % n
        odd = turn % 2
        block = (1 - odd) * (n - 1 - turn // 2) + odd * (turn // 2)
        return half, group // SPIN, group % SPIN, block

    def next_out(p, o):
        half, sub, s, block = place(p)
        peer = lax.rem(tm + o, n)
        at, ks = pl.ds(half * SUBLANES, SUBLANES), pl.ds(sub * SUBLANES, SUBLANES)
        return remote(
            snd.at[peer, at, s, block, ks], recv.at[at, s, block, tm, ks], ts.at[p, o], tr.at[p, o], {"tm": peer})

    def next_own(p):
        half, sub, s, block = place(p)
        at, ks = pl.ds(half * SUBLANES, SUBLANES), pl.ds(sub * SUBLANES, SUBLANES)
        return local(snd.at[tm, at, s, block, ks], recv.at[at, s, block, tm, ks], tl.at[p])

    def window(p):
        half, sub, s, block = place(p)
        return pl.ds(block * quarter + sub * SUBLANES, SUBLANES), s, half

    def right_out(n_pass, p):
        at = window(p)
        return remote(
            rbuf.at[at], rbuf.at[at], rs.at[n_pass, p], rr.at[n_pass, p],
            {"mom": jnp.minimum(mom + 1, n - 1)})

    def left_out(n_pass, p):
        at = window(p)
        return remote(
            lbuf.at[at], lbuf.at[at], ls.at[n_pass, p], lr.at[n_pass, p],
            {"mom": jnp.maximum(mom - 1, 0)})

    class Spread:
        def __init__(self, at, source, target):
            self.at, self.source, self.target = at, source, target

        def own(self):
            return local(self.source, self.target(tm), al.at[self.at])

        def pair(self):
            return remote(self.source, self.target(tm), aps.at[self.at], apr.at[self.at], partner)

        def across(self, o):
            peer = lax.rem(tm_x + o, n_x)
            return remote(
                self.source, self.target(tm), axs.at[self.at, o], axr.at[self.at, o], {"tm": peer * 2 + core})

        def relay(self, o):
            held = self.target(lax.rem(tm_x + n_x - o, n_x) * 2 + core)
            return remote(held, held, aqs.at[self.at, o], aqr.at[self.at, o], partner)

        def begin(self):
            for o in range(1, n_x):
                self.across(o).start()
            self.pair().start()
            self.own().start()

        def pass_on(self):
            for o in range(1, n_x):
                self.across(o).wait_recv()
                self.relay(o).start()

        def arrive(self):
            self.own().wait()
            self.pair().wait_recv()
            for o in range(1, n_x):
                self.relay(o).wait_recv()
                self.relay(o).wait_send()

        def end(self):
            self.pair().wait_send()
            for o in range(1, n_x):
                self.across(o).wait_send()

    guesses = Spread(0, guess, lambda t: guess_all.at[t])
    firsts = [
        Spread(1 + half, tot.at[0, :, :, half], lambda t, half=half: own_first.at[pl.ds(t * quarter, quarter), :, half])
        for half in range(halves)]

    def lasts(half, sub, s):
        return Spread(
            1 + halves + (half * subs + sub) * SPIN + s, tot.at[1, pl.ds(sub * SUBLANES, SUBLANES), s, half],
            lambda t: own_last.at[half, pl.ds(t * quarter + sub * SUBLANES, SUBLANES), s])

    def spread_rows(target, half, s, k, parts):
        for j, value in enumerate(block_transpose(parts, lane, width)):
            at = ((j * rows + half * SUBLANES) * SPIN + s) * local_k + k
            target[pl.ds(at, SUBLANES, stride=SPIN * local_k), :] = value

    def gather_rows(source, half, s, k):
        parts = []
        for t in range(n):
            at = ((t * rows + half * SUBLANES) * SPIN + s) * local_k + k
            parts.append(source[pl.ds(at, SUBLANES, stride=SPIN * local_k), :])
        return jnp.concatenate(block_transpose(parts, lane, width), axis=0)

    def first_layout(half):
        @pl.loop(0, local_k, unroll=4)
        def _(k):
            for s in range(SPIN):
                parts = [start[k, s, half * half_rows + g * SUBLANES:half * half_rows + (g + 1) * SUBLANES, :]
                         for g in range(n)]
                spread_rows(flat_snd, half, s, k, parts)

    def keep_stack(n_pass, k, s, half, value):
        for at, piece in enumerate((value, rot(value))):
            stacks[n_pass][k, s, 0, at, half], stacks[n_pass][k, s, 1, at, half] = split(piece)

    def stack_of(n_pass, k, s):
        return tuple(stacks[n_pass][k, s, at].reshape(2 * PANEL, LANES) for at in range(2))

    def first_stack(half):
        @pl.loop(0, half_chunks)
        def _(d):
            q = half * half_chunks + d
            for o in range(1, n):
                panel_out(q, o).wait_recv()
            panel_own(q).wait()

        @pl.loop(0, local_k, unroll=4)
        def _(k):
            for s in range(SPIN):
                keep_stack(0, k, s, half, gather_rows(flat_rx_g, half, s, k))

    def sigma(q):
        @pl.loop(0, CHUNK)
        def _(d):
            i = q * CHUNK + d
            both = jnp.concatenate(
                [recv[i, s].reshape(K, LANES) for s in range(SPIN)], axis=1)
            sums = dot3((fwd_split[0], fwd_split[1]), split(both))
            site, mirrored = [], []
            for s in range(SPIN):
                with_cos = sums[:K, s * LANES:(s + 1) * LANES]
                turned = rot(sums[K:, s * LANES:(s + 1) * LANES])
                site.append(with_cos + turned)
                mirrored.append(with_cos - turned)
            first, second = site
            flipped = swap(second)
            pair = (first * jnp.where(low, second, flipped)
                    + rot(first) * jnp.where(low, flipped, second)) * wvec[...]
            pair_rot = rot(pair)
            tops, bottoms = [], []
            for s in range(SPIN):
                other = mirrored[1 - s]
                flipped = swap(other)
                value = pair * jnp.where(low, other, flipped) - pair_rot * jnp.where(low, flipped, other)
                tops.append(value)
                bottoms.append(-rot(value))
            stacked = jnp.concatenate(
                [jnp.concatenate(tops, axis=1), jnp.concatenate(bottoms, axis=1)], axis=0)
            result = dot3((back_split[0], back_split[1]), split(stacked))
            for s in range(SPIN):
                sig[i, s] = result[:, s * LANES:(s + 1) * LANES].reshape(sig.shape[2:])

    def send_sigma(n_pass, q):
        for o in range(1, n):
            sigma_out(n_pass, q, o).start()
        sigma_own(n_pass, q).start()

    def wait_sigma(n_pass, half):
        @pl.loop(0, half_chunks)
        def _(d):
            q = half * half_chunks + d
            for o in range(1, n):
                sigma_out(n_pass, q, o).wait_recv()
            sigma_own(n_pass, q).wait()

    def second_sigma(q):
        half = q // half_chunks

        @pl.when(q % half_chunks == 0)
        def _():
            @pl.loop(0, per_half)
            def _(d):
                p = half * per_half + d
                for o in range(1, n):
                    next_out(p, o).wait_recv()
                next_own(p).wait()

        for o in range(1, n):
            sigma_out(0, q, o).wait_send()
        sigma(q)
        send_sigma(1, q)

    def convolve(n_pass, p):
        half, sub, s, block = place(p)

        @pl.when(p % per_half == 0)
        def _():
            wait_sigma(n_pass, half)

        results = []
        for m in range(SUBLANES):
            k = block * quarter + sub * SUBLANES + m
            value = split(gather_rows(flat_rx_s, half, s, k))
            results.append((k, dot3(value, stack_of(n_pass, k, s), True)))
        for k, result in results:
            part[k, s, half] = result

    def each(p, body):
        half, sub, s, block = place(p)
        done = [body((block * quarter + sub * SUBLANES + m, s, half), sub * SUBLANES + m) for m in range(SUBLANES)]
        for stores in done:
            for target, at, value in stores:
                target[at] = value

    def flows(n_pass, p):
        block = place(p)[3]
        if n_pass == 0:
            yes = block >= 0
            return yes, yes, yes, yes, yes
        return block >= mom, block > mom, block <= mom, block < mom, block == mom

    def origin(n_pass, p):
        _, send_right, _, send_left, _ = flows(n_pass, p)

        @pl.when(mom == 0)
        def _():
            each(p, lambda at, m: [(rbuf, at, part[at])])

            @pl.when(send_right)
            def _():
                right_out(n_pass, p).start()

        @pl.when(mom == n - 1)
        def _():
            each(p, lambda at, m: [(lbuf, at, part[at])])

            @pl.when(send_left)
            def _():
                left_out(n_pass, p).start()

    def near_step(n_pass, p):
        from_left, send_right, from_right, send_left, _ = flows(n_pass, p)

        @pl.when(near_left & (mom > 0) & from_left)
        def _():
            right_out(n_pass, p).wait_recv()

            each(p, lambda at, m: [(rbuf, at, rbuf[at] + part[at])])

            @pl.when(send_right)
            def _():
                right_out(n_pass, p).start()

        @pl.when((mom >= n // 2) & (mom < n - 1) & from_right)
        def _():
            left_out(n_pass, p).wait_recv()

            each(p, lambda at, m: [(lbuf, at, lbuf[at] + part[at])])

            @pl.when(send_left)
            def _():
                left_out(n_pass, p).start()

    def far_step(n_pass, p):
        from_left, send_right, from_right, send_left, keep = flows(n_pass, p)

        def one(mine, other, outer, send, copy):
            copy.wait_recv()
            if n_pass == 0:
                each(p, lambda at, m: [
                    (other, at, other[at] + part[at]), (part, at, mine[at] + other[at])])
            else:
                @pl.when(send)
                def _():
                    each(p, lambda at, m: [(other, at, other[at] + part[at])])

                @pl.when(keep)
                def _():
                    each(p, lambda at, m: [(tot, (1, m) + at[1:], mine[at] + other[at])])

            @pl.when(outer & send)
            def _():
                copy.start()

        @pl.when(near_left & from_right)
        def _():
            one(rbuf, lbuf, mom > 0, send_left, left_out(n_pass, p))

        @pl.when((mom >= n // 2) & from_left)
        def _():
            one(lbuf, rbuf, mom < n - 1, send_right, right_out(n_pass, p))

    def update(p):
        half, sub, s, block = place(p)

        @pl.when(block == mom)
        def _():
            each(p, lambda at, m: [(tot, (0, m) + at[1:], part[at])])

        results = []
        for m in range(SUBLANES):
            k = block * quarter + sub * SUBLANES + m
            old = stk_a[k, s, 0, 0, half].astype(jnp.float32) + stk_a[k, s, 1, 0, half].astype(jnp.float32)
            results.append((k, old + step_scale * dot3(split(part[k, s, half]), stack_of(0, k, s))))
        for k, new in results:
            keep_stack(1, k, s, half, new)
            spread_rows(flat_snd, half, s, k, [new[g * SUBLANES:(g + 1) * SUBLANES, :] for g in range(n)])

        for o in range(1, n):
            next_out(p, o).start()
        next_own(p).start()

    def own_panel(group):
        results = []
        for m in range(SUBLANES // 2):
            k = group * (SUBLANES // 2) + m
            for s in range(SPIN):
                first = start[k, s]
                right = split(jnp.concatenate([first, rot(first)], axis=0))
                new = first + step_scale * dot3(split(own_first[k, s].reshape(PANEL, LANES)), right)
                results.append((k, s, new))
        for k, s, new in results:
            own_first[k, s] = new.reshape(halves, half_rows, LANES)

    def finish(sub, s):
        is_block = chosen > 0.5
        for half in range(halves):
            lasts(half, sub, s).arrive()

        @pl.loop(0, n)
        def _(t):
            results = []
            for m in range(SUBLANES):
                k = t * quarter + sub * SUBLANES + m
                whole = jnp.concatenate([own_last[half, k, s] for half in range(halves)], axis=0)
                d_rows = jnp.concatenate([guess_all[at, k, s] for at in range(n)], axis=0)
                right = jnp.where(is_block, whole, own_first[k, s].reshape(PANEL, LANES))
                left = jnp.where(is_block, d_rows, whole)
                right = split(jnp.concatenate([right, rot(right)], axis=0))
                new = jnp.where(is_block, d_rows, start[k, s]) + step_scale * dot3(split(left), right)
                results.append((k, new))
            for k, new in results:
                out[k, s] = new

    def begin_forward(q):
        for o in range(1, n):
            forward(q, o).start()
        forward_own(q).start()

    first_layout(0)
    pl.semaphore_wait(barrier, 2 * n - 2)
    for q in range(min(AHEAD, half_chunks)):
        begin_forward(q)
    for half in range(1, halves):
        first_layout(half)

    for at, table in enumerate(tables(ordering[...])):
        fwd_split[0, at * K:(at + 1) * K, :], fwd_split[1, at * K:(at + 1) * K, :] = split(table)
        turned = split(table.T)
        back_split[0, :, at * K:(at + 1) * K], back_split[1, :, at * K:(at + 1) * K] = turned

    owners = slab_owner[...].astype(jnp.float32)
    slabs = lax.broadcasted_iota(jnp.int32, owners.shape, 1).astype(jnp.float32)
    oldest = expiring[...].astype(jnp.float32)
    mine = tm.astype(jnp.float32)
    slab_mine = jnp.sum(jnp.where(owners == mine, slabs, 0.0), axis=1, keepdims=True)
    owner_expiring = jnp.sum(jnp.where(slabs == oldest, owners, 0.0), axis=1, keepdims=True)
    position = slab_mine - oldest
    position = jnp.where(position < 0.0, position + n, position)
    within = (mom * rows + lane % rows).astype(jnp.float32)
    ahead = (n * PANEL - 1) - (position * PANEL + within)
    strength = coupling[...] * coupling[...]
    wvec[...] = strength * (jnp.exp(-1.5 * ahead / (n * PANEL)) / math.sqrt(n * PANEL))
    chosen = jnp.where(owner_expiring == mine, jnp.ones((1, LANES), jnp.float32), 0.0)

    @pl.loop(0, chunks + 1)
    def _(q):
        @pl.when(q < chunks)
        def _():
            for o in range(1, n):
                forward(q, o).wait_recv()
            forward_own(q).wait()

            @pl.when(q + AHEAD < chunks)
            def _():
                begin_forward(q + AHEAD)

            for o in range(1, n):
                panel_out(q, o).start()
            panel_own(q).start()
            sigma(q)
            send_sigma(0, q)

        for half in range(halves - 1):
            @pl.when(q == (half + 1) * half_chunks + 1)
            def _():
                first_stack(half)

        @pl.when(q == chunks)
        def _():
            first_stack(halves - 1)

    @pl.loop(0, chunks)
    def _(q):
        for o in range(1, n):
            forward(q, o).wait_send()
            panel_out(q, o).wait_send()

    for o in range(1, n):
        pl.semaphore_signal(room, inc=1, device_id={"tm": lax.rem(tm + o, n)}, device_id_type=MESH)
    guesses.begin()

    lead = LEAD[0]
    told = per_half + lead + LAG
    sigma_at = told + 3

    @pl.loop(0, pieces + lead + LAG)
    def _(t):
        @pl.when(t < pieces)
        def _():
            convolve(0, t)
            origin(0, t)

        @pl.when((t >= lead) & (t - lead < pieces))
        def _():
            near_step(0, t - lead)

        @pl.when(t >= lead + LAG)
        def _():
            p = t - lead - LAG
            far_step(0, p)

            @pl.when(p == 0)
            def _():
                pl.semaphore_wait(room, n - 1)

            update(p)

        for half in range(halves - 1):
            @pl.when(t == told + half * per_half)
            def _():
                firsts[half].begin()

        @pl.when(t == told)
        def _():
            guesses.pass_on()

        d = t - sigma_at

        @pl.when((d >= 0) & (d < 2 * (halves - 1) * half_chunks) & (d % 2 == 0))
        def _():
            second_sigma(d // 2)

    @pl.loop(0, pieces)
    def _(p):
        @pl.when(mom < n - 1)
        def _():
            right_out(0, p).wait_send()

        @pl.when(mom > 0)
        def _():
            left_out(0, p).wait_send()

    @pl.when(mom > 0)
    def _():
        pl.semaphore_signal(credit.at[1], inc=1, device_id={"mom": jnp.maximum(mom - 1, 0)}, device_id_type=MESH)

    @pl.when(mom < n - 1)
    def _():
        pl.semaphore_signal(credit.at[0], inc=1, device_id={"mom": jnp.minimum(mom + 1, n - 1)}, device_id_type=MESH)

    @pl.when(mom > 0)
    def _():
        pl.semaphore_wait(credit.at[0], 1)

    @pl.when(mom < n - 1)
    def _():
        pl.semaphore_wait(credit.at[1], 1)

    lead = LEAD[1]
    panel_at = 2 * per_half - 2 * local_k // SUBLANES + 6

    @pl.loop(0, pieces + lead + LAG)
    def _(t):
        @pl.when(t < pieces)
        def _():
            convolve(1, t)
            origin(1, t)

        @pl.when((t >= 4) & (t < 4 + 2 * half_chunks) & (t % 2 == 0))
        def _():
            second_sigma((halves - 1) * half_chunks + (t - 4) // 2)

        @pl.when((t >= lead) & (t - lead < pieces))
        def _():
            near_step(1, t - lead)

        @pl.when(t >= lead + LAG)
        def _():
            p = t - lead - LAG
            far_step(1, p)
            half, sub, s, block = place(p)

            @pl.when(block == mom)
            def _():
                lasts(half, sub, s).begin()

        @pl.when(t == 4 + 2 * half_chunks)
        def _():
            firsts[halves - 1].begin()

        @pl.when(t == panel_at)
        def _():
            for first in firsts:
                first.pass_on()
            for first in firsts:
                first.arrive()

        @pl.when((t >= panel_at) & (t < panel_at + 2 * local_k // SUBLANES))
        def _():
            own_panel(t - panel_at)

    guesses.arrive()

    @pl.loop(0, subs * SPIN)
    def _(d):
        for half in range(halves):
            lasts(half, d // SPIN, d % SPIN).pass_on()
        finish(d // SPIN, d % SPIN)

    @pl.loop(0, pieces)
    def _(p):
        _, send_right, _, send_left, _ = flows(1, p)

        @pl.when((mom < n - 1) & send_right)
        def _():
            right_out(1, p).wait_send()

        @pl.when((mom > 0) & send_left)
        def _():
            left_out(1, p).wait_send()

        for o in range(1, n):
            next_out(p, o).wait_send()

    @pl.loop(0, chunks)
    def _(q):
        for o in range(1, n):
            sigma_out(1, q, o).wait_send()

    for half in range(halves):
        @pl.loop(0, subs * SPIN)
        def _(d):
            lasts(half, d // SPIN, d % SPIN).end()
    guesses.end()
    for first in firsts:
        first.end()


def share_step(n, start, guess, ordering, coupling, slab_owner, expiring):
    local_k = start.shape[0]
    quarter, rows = local_k // n, PANEL // n
    halves, subs = rows // SUBLANES, quarter // SUBLANES
    pieces, chunks = halves * n * subs * SPIN, rows // CHUNK
    spreads = 1 + halves + halves * subs * SPIN
    half_rows = n * SUBLANES
    f32, bf16 = jnp.float32, jnp.bfloat16
    dma = pltpu.SemaphoreType.DMA
    vmem = pl.BlockSpec(memory_space=pltpu.VMEM)
    moved = pltpu.VMEM((n, rows, SPIN, n, quarter, LANES), f32)
    grid = pltpu.VMEM((rows, SPIN, n, n, quarter, LANES), f32)
    square = (local_k, SPIN, halves, half_rows, LANES)
    stack = pltpu.VMEM((local_k, SPIN, 2, 2, halves, half_rows, LANES), bf16)
    return pl.pallas_call(
        functools.partial(share_kernel, n),
        out_shape=jax.ShapeDtypeStruct(start.shape, f32),
        in_specs=[vmem] * 6,
        out_specs=vmem,
        scratch_shapes=[
            moved, grid, grid, moved, moved,
            stack, stack, pltpu.VMEM((1, LANES), f32),
            pltpu.VMEM(square, f32), pltpu.VMEM(square, f32),
            pltpu.VMEM((PASSES, quarter) + square[1:], f32),
            pltpu.VMEM((n,) + guess.shape, f32),
            pltpu.VMEM((2, 2 * K, K), bf16),
            pltpu.VMEM((2, K, 2 * K), bf16),
            dma((chunks,)), dma((chunks, n)), dma((chunks, n)),
            dma((chunks,)), dma((chunks, n)), dma((chunks, n)),
            dma((PASSES, chunks)), dma((PASSES, chunks, n)), dma((PASSES, chunks, n)),
            dma((pieces,)), dma((pieces, n)), dma((pieces, n)),
            dma((PASSES, pieces)), dma((PASSES, pieces)), dma((PASSES, pieces)), dma((PASSES, pieces)),
            pltpu.SemaphoreType.REGULAR((2,)), pltpu.SemaphoreType.REGULAR,
            dma((spreads,)), dma((spreads,)), dma((spreads,)),
            dma((spreads, n)), dma((spreads, n)), dma((spreads, n)), dma((spreads, n)),
        ],
        compiler_params=pltpu.CompilerParams(
            collective_id=0, has_side_effects=True, vmem_limit_bytes=63 * 1024 * 1024),
        name="share_step",
    )(start, guess, ordering, coupling, slab_owner, expiring)


def body(panel_start, block_guess, coupling, slab_owner, expiring, ordering):
    slab_count = lax.axis_size("tm")
    n_mom = lax.axis_size("mom")
    local_k = panel_start.shape[0]
    unit = SUBLANES * slab_count
    if n_mom == slab_count and local_k % unit == 0 and PANEL % unit == 0:
        return share_step(
            n_mom, panel_start, block_guess, ordering[None, :], coupling[None, :], slab_owner[None, :], expiring[None, :])
    own_index = lax.axis_index("tm")
    blocks = jnp.arange(slab_count, dtype=jnp.int32)
    slab_mine = jnp.sum(blocks * (slab_owner == own_index).astype(jnp.int32))
    position = (slab_mine - expiring[0]) % slab_count
    window = slab_count * PANEL
    times = position * PANEL + jnp.arange(PANEL, dtype=jnp.int32)
    weights = jnp.exp(-1.5 * (window - 1 - times).astype(jnp.float32) / window) / math.sqrt(window)
    strength = coupling[0] * coupling[0]
    wvec = (strength * jnp.concatenate([weights, weights]))[None, :]
    owner_expiring = jnp.sum(slab_owner * (blocks == expiring[0]).astype(jnp.int32))
    chosen = jnp.broadcast_to((own_index == owner_expiring).astype(jnp.float32), (1, LANES))
    start = panel_start.reshape(local_k, SPIN, CHUNKS, PANEL // CHUNKS, LANES)
    result = panel_step(n_mom, slab_count, start, block_guess, ordering[None, :], wvec, chosen)
    return result.reshape(panel_start.shape)


def solution(mesh):
    return jax.shard_map(
        body,
        mesh=mesh,
        in_specs=(
            P("mom", "groups", None, "tm"),
            P("mom", "groups", "tm", None),
            P("groups"),
            P("groups"),
            P("groups"),
            P(),
        ),
        out_specs=P("mom", "groups", None, "tm"),
        check_vma=False,
    )
```

```python
import functools
import math

import jax
import jax.numpy as jnp
from jax import lax
from jax.experimental import pallas as pl
from jax.experimental.pallas import tpu as pltpu
from jax.sharding import PartitionSpec as P

LSIDE = 16
K = LSIDE * LSIDE
PANEL = 64
PASSES = 2
SPIN = 2
LANES = 2 * PANEL
CHUNKS = 2
MESH = pl.DeviceIdType.MESH


def tables(ordering):
    bits = LSIDE.bit_length() - 1
    site = lax.broadcasted_iota(jnp.int32, (K, K), 0)
    phases = ((site >> bits) * (ordering >> bits) + (site & (LSIDE - 1)) * (ordering & (LSIDE - 1))) & (LSIDE - 1)
    angles = phases.astype(jnp.float32) * (2.0 * math.pi / LSIDE)
    return jnp.cos(angles) / LSIDE, jnp.sin(angles) / LSIDE


def split(x):
    high = x.astype(jnp.bfloat16)
    return high, (x - high.astype(jnp.float32)).astype(jnp.bfloat16)


def dot3(left, right, transposed=False):
    dims = (((1,), (1 if transposed else 0,)), ((), ()))

    def one(a, b):
        return lax.dot_general(a, b, dims, preferred_element_type=jnp.float32)

    return one(left[0], right[0]) + (one(left[0], right[1]) + one(left[1], right[0]))


def step_kernel(
    n_mom, n_tm, start, guess, ordering, wvec, chosen,
    out, cur, recv, sig, ret, fwd_split, back_split, stk, part, conv, pair_buf, ring_buf, guess_all,
    local_sem, guess_own, fs, fr, rs, rr, ps, pr, ss, sr, gs, gr, qs, qr, ds, dr,
):
    mom, tm = lax.axis_index("mom"), lax.axis_index("tm")
    rows, local_k = cur.shape[3], cur.shape[4]
    group = n_mom * rows
    n_x = n_tm // 2
    half = local_k // 2
    share = half // n_x
    tm_x, core = tm // 2, tm % 2
    step_scale = 1.0 / math.sqrt(PANEL)
    lane = lax.broadcasted_iota(jnp.int32, (1, LANES), 1)
    low = lane < PANEL
    sign = jnp.where(low, -1.0, 1.0).astype(jnp.float32)
    flat_cur = cur.reshape(CHUNKS * SPIN * group * local_k, LANES)
    flat_ret = ret.reshape(CHUNKS * SPIN * group * local_k, LANES)

    def swap(x):
        return pltpu.roll(x, PANEL, 1)

    def rot(x):
        return swap(x) * sign

    barrier = pltpu.get_barrier_semaphore()
    for o in range(1, n_mom):
        pl.semaphore_signal(barrier, inc=1, device_id={"mom": lax.rem(mom + o, n_mom)}, device_id_type=MESH)
    for o in range(1, n_tm):
        pl.semaphore_signal(barrier, inc=1, device_id={"tm": lax.rem(tm + o, n_tm)}, device_id_type=MESH)

    mine = pl.ds(mom * local_k, local_k)
    other_half = pl.ds((1 - core) * half, half)
    share_at = core * half + tm_x * share
    own_share = pl.ds(share_at, share)
    partner = {"tm": tm_x * 2 + (1 - core)}

    def remote(source, target, send, recv_sem, device):
        return pltpu.make_async_remote_copy(
            src_ref=source, dst_ref=target, send_sem=send, recv_sem=recv_sem,
            device_id=device, device_id_type=MESH)

    def forward(n, c, o):
        peer = lax.rem(mom + o, n_mom)
        return remote(cur.at[c, :, peer], recv.at[c, :, :, mine, :], fs.at[n, c, o], fr.at[n, c, o], {"mom": peer})

    def forward_own(n, c):
        return pltpu.make_async_copy(cur.at[c, :, mom], recv.at[c, :, :, mine, :], local_sem.at[n, c, 0])

    def back(n, c, o):
        peer = lax.rem(mom + o, n_mom)
        return remote(
            sig.at[c, :, :, pl.ds(peer * local_k, local_k), :], ret.at[c, :, mom],
            rs.at[n, c, o], rr.at[n, c, o], {"mom": peer})

    def back_own(n, c):
        return pltpu.make_async_copy(sig.at[c, :, :, mine, :], ret.at[c, :, mom], local_sem.at[n, c, 1])

    def pair_up(n, c):
        return remote(part.at[c, other_half], pair_buf.at[c], ps.at[n, c], pr.at[n, c], partner)

    def scatter(n, c, o):
        peer = lax.rem(tm_x + o, n_x)
        return remote(
            part.at[c, pl.ds(core * half + peer * share, share)], ring_buf.at[c, o - 1],
            ss.at[n, c, o], sr.at[n, c, o], {"tm": peer * 2 + core})

    def gather(n, c, o):
        peer = lax.rem(tm_x + o, n_x)
        return remote(
            conv.at[c, own_share], conv.at[c, own_share],
            gs.at[n, c, o], gr.at[n, c, o], {"tm": peer * 2 + core})

    def pair_down(n, c, o):
        held = pl.ds(core * half + lax.rem(tm_x + n_x - o, n_x) * share, share)
        return remote(conv.at[c, held], conv.at[c, held], qs.at[n, c, o], qr.at[n, c, o], partner)

    def pair_down_recv(n, c):
        for o in range(n_x):
            pair_down(n, c, o).wait_recv()

    def guess_copy(o):
        return remote(guess, guess_all.at[tm], ds.at[o], dr.at[o], {"tm": lax.rem(tm + o, n_tm)})

    def guess_local():
        return pltpu.make_async_copy(guess, guess_all.at[tm], guess_own)

    def send_forward(n, c):
        for o in range(1, n_mom):
            forward(n, c, o).start()
        forward_own(n, c).start()

    def keep_stack(n, k, s, c, value):
        turned = rot(value)
        for at, piece in ((c * group, value), (PANEL + c * group, turned)):
            high, rest = split(piece)
            stk[n, 0, k, s, at:at + group, :] = high
            stk[n, 1, k, s, at:at + group, :] = rest

    def first_layout(c):
        @pl.loop(0, local_k)
        def _(k):
            for s in range(SPIN):
                at = ((c * SPIN + s) * group) * local_k + k
                flat_cur[pl.ds(at, group, stride=local_k), :] = start[k, s, c]

    def sigma(n, c):
        for o in range(1, n_mom):
            forward(n, c, o).wait_recv()
        forward_own(n, c).wait()
        if n > 0:
            for o in range(1, n_mom):
                back(n - 1, c, o).wait_send()

        @pl.loop(0, rows)
        def _(i):
            both = jnp.concatenate([recv[c, 0, i], recv[c, 1, i]], axis=1)
            sums = dot3((fwd_split[0], fwd_split[1]), split(both))
            site, mirrored = [], []
            for s in range(SPIN):
                with_cos = sums[:K, s * LANES:(s + 1) * LANES]
                turned = rot(sums[K:, s * LANES:(s + 1) * LANES])
                site.append(with_cos + turned)
                mirrored.append(with_cos - turned)
            first, second = site
            flipped = swap(second)
            pair = (first * jnp.where(low, second, flipped)
                    + rot(first) * jnp.where(low, flipped, second)) * wvec[...]
            pair_rot = rot(pair)
            tops, bottoms = [], []
            for s in range(SPIN):
                other = mirrored[1 - s]
                flipped = swap(other)
                value = pair * jnp.where(low, other, flipped) - pair_rot * jnp.where(low, flipped, other)
                tops.append(value)
                bottoms.append(-rot(value))
            stacked = jnp.concatenate(
                [jnp.concatenate(tops, axis=1), jnp.concatenate(bottoms, axis=1)], axis=0)
            result = dot3((back_split[0], back_split[1]), split(stacked))
            for s in range(SPIN):
                sig[c, s, i] = result[:, s * LANES:(s + 1) * LANES]

        for o in range(1, n_mom):
            back(n, c, o).start()
        back_own(n, c).start()

    def convolve(n, c):
        for o in range(1, n_mom):
            back(n, c, o).wait_recv()
        back_own(n, c).wait()
        if n > 0:
            pair_up(n - 1, c).wait_send()
            for o in range(n_x):
                pair_down(n - 1, c, o).wait_send()
            for o in range(1, n_x):
                scatter(n - 1, c, o).wait_send()
                gather(n - 1, c, o).wait_send()

        def some(base):
            @pl.loop(0, half, unroll=8)
            def _(i):
                k = base + i
                for s in range(SPIN):
                    at = ((c * SPIN + s) * group) * local_k + k
                    value = split(flat_ret[pl.ds(at, group, stride=local_k), :])
                    part[c, k, s] = dot3(value, (stk[n, 0, k, s], stk[n, 1, k, s]), True)

        some((1 - core) * half)
        pair_up(n, c).start()
        some(core * half)

    def reduce(n, c):
        pair_up(n, c).wait_recv()

        @pl.loop(0, half)
        def _(i):
            part[c, core * half + i] = part[c, core * half + i] + pair_buf[c, i]

        for o in range(1, n_x):
            scatter(n, c, o).start()
        for o in range(1, n_x):
            scatter(n, c, o).wait_recv()

        @pl.loop(0, share)
        def _(i):
            total = part[c, share_at + i]
            for o in range(1, n_x):
                total = total + ring_buf[c, o - 1, i]
            conv[c, share_at + i] = total

        for o in range(1, n_x):
            gather(n, c, o).start()
        pair_down(n, c, 0).start()
        for o in range(1, n_x):
            gather(n, c, o).wait_recv()
            pair_down(n, c, o).start()

    def update(n, c):
        for o in range(1, n_mom):
            forward(n, c, o).wait_send()

        def some(base):
            @pl.loop(0, half, unroll=8)
            def _(i):
                k = base + i
                for s in range(SPIN):
                    new = start[k, s, c] + step_scale * dot3(
                        split(conv[c, k, s]), (stk[n, 0, k, s], stk[n, 1, k, s]))
                    at = ((c * SPIN + s) * group) * local_k + k
                    flat_cur[pl.ds(at, group, stride=local_k), :] = new
                    keep_stack(n + 1, k, s, c, new)

        some(core * half)
        pair_down_recv(n, c)
        some((1 - core) * half)

    def finish(n):
        is_block = chosen[...] > 0.5

        def some(base):
            @pl.loop(0, half, unroll=4)
            def _(i):
                k = base + i
                for s in range(SPIN):
                    whole = jnp.concatenate([conv[c, k, s] for c in range(CHUNKS)], axis=0)
                    d = jnp.concatenate([guess_all[t, k, s] for t in range(n_tm)], axis=0)
                    first = jnp.concatenate([start[k, s, c] for c in range(CHUNKS)], axis=0)
                    panel = stk[n, 0, k, s].astype(jnp.float32) + stk[n, 1, k, s].astype(jnp.float32)
                    right = jnp.where(is_block, jnp.concatenate([whole, rot(whole)], axis=0), panel)
                    left = jnp.where(is_block, d, whole)
                    new = jnp.where(is_block, d, first) + step_scale * dot3(split(left), split(right))
                    for c in range(CHUNKS):
                        out[k, s, c] = new[c * group:(c + 1) * group, :]

        for c in range(CHUNKS - 1):
            pair_down_recv(n, c)
        some(core * half)
        pair_down_recv(n, CHUNKS - 1)
        some((1 - core) * half)

    first_layout(0)
    pl.semaphore_wait(barrier, n_mom + n_tm - 2)
    send_forward(0, 0)
    for c in range(1, CHUNKS):
        first_layout(c)
        send_forward(0, c)
    for o in range(1, n_tm):
        guess_copy(o).start()
    guess_local().start()

    for at, table in enumerate(tables(ordering[...])):
        fwd_split[0, at * K:(at + 1) * K, :], fwd_split[1, at * K:(at + 1) * K, :] = split(table)
        turned = split(table.T)
        back_split[0, :, at * K:(at + 1) * K], back_split[1, :, at * K:(at + 1) * K] = turned

    @pl.loop(0, local_k, unroll=4)
    def _(k):
        for s in range(SPIN):
            for c in range(CHUNKS):
                keep_stack(0, k, s, c, start[k, s, c])

    for n in range(PASSES):
        for c in range(CHUNKS):
            sigma(n, c)
        for c in range(CHUNKS):
            convolve(n, c)
            reduce(n, c)
            if n < PASSES - 1:
                update(n, c)
                send_forward(n + 1, c)

    for o in range(1, n_tm):
        guess_copy(o).wait_recv()
    guess_local().wait()
    finish(PASSES - 1)

    n = PASSES - 1
    for c in range(CHUNKS):
        pair_up(n, c).wait_send()
        for o in range(n_x):
            pair_down(n, c, o).wait_send()
        for o in range(1, n_x):
            scatter(n, c, o).wait_send()
            gather(n, c, o).wait_send()
        for o in range(1, n_mom):
            forward(n, c, o).wait_send()
            back(n, c, o).wait_send()
    for o in range(1, n_tm):
        guess_copy(o).wait_send()


def panel_step(n_mom, n_tm, start, guess, ordering, wvec, chosen):
    local_k = start.shape[0]
    group = start.shape[3]
    rows = group // n_mom
    share = local_k // n_tm
    panel = (CHUNKS, SPIN, n_mom, rows, local_k, LANES)
    sites = (CHUNKS, SPIN, rows, K, LANES)
    f32, bf16 = jnp.float32, jnp.bfloat16
    dma = pltpu.SemaphoreType.DMA
    vmem = pl.BlockSpec(memory_space=pltpu.VMEM)
    one, many_mom, many_x = (PASSES, CHUNKS), (PASSES, CHUNKS, n_mom), (PASSES, CHUNKS, n_tm // 2)
    return pl.pallas_call(
        functools.partial(step_kernel, n_mom, n_tm),
        out_shape=jax.ShapeDtypeStruct(start.shape, f32),
        in_specs=[vmem] * 5,
        out_specs=vmem,
        scratch_shapes=[
            pltpu.VMEM(panel, f32),
            pltpu.VMEM(sites, f32),
            pltpu.VMEM(sites, f32),
            pltpu.VMEM(panel, f32),
            pltpu.VMEM((2, 2 * K, K), bf16),
            pltpu.VMEM((2, K, 2 * K), bf16),
            pltpu.VMEM((PASSES, 2, local_k, SPIN, LANES, LANES), bf16),
            pltpu.VMEM((CHUNKS, local_k, SPIN, group, LANES), f32),
            pltpu.VMEM((CHUNKS, local_k, SPIN, group, LANES), f32),
            pltpu.VMEM((CHUNKS, local_k // 2, SPIN, group, LANES), f32),
            pltpu.VMEM((CHUNKS, max(n_tm // 2 - 1, 1), share, SPIN, group, LANES), f32),
            pltpu.VMEM((n_tm,) + guess.shape, f32),
            dma(one + (2,)), dma,
            dma(many_mom), dma(many_mom), dma(many_mom), dma(many_mom),
            dma(one), dma(one),
            dma(many_x), dma(many_x), dma(many_x), dma(many_x),
            dma(many_x), dma(many_x),
            dma((n_tm,)), dma((n_tm,)),
        ],
        compiler_params=pltpu.CompilerParams(
            collective_id=0, has_side_effects=True, vmem_limit_bytes=63 * 1024 * 1024),
        name="panel_step",
    )(start, guess, ordering, wvec, chosen)


SUBLANES = 8
CHUNK = 1
AHEAD = 3
LAG = 2
LEAD = (4, 6)
ARRIVE = 3
LAST_AT = 11
PANEL_AT = 6


def block_transpose(blocks, lane, width):
    blocks = list(blocks)
    bit = 1
    while bit < len(blocks):
        keep = (lane // width) % (2 * bit) < bit
        for p in range(len(blocks)):
            if p & bit == 0:
                a, b = blocks[p], blocks[p + bit]
                blocks[p] = jnp.where(keep, a, pltpu.roll(b, bit * width, 1))
                blocks[p + bit] = jnp.where(keep, pltpu.roll(a, LANES - bit * width, 1), b)
        bit *= 2
    return blocks


def share_kernel(
    n, start, guess, ordering, coupling, slab_owner, expiring,
    result, out, out_sem, snd, recv, sig, rx_g, rx_s, stk_a, stk_b, wvec, rbuf, lbuf, tot, guess_all, fwd_split, back_split,
    fs, fr, gs, gr, ss, sr, ts, tr, rs, rr, ls, lr, credit, room,
    al, aps, apr, axs, axr, aqs, aqr,
):
    mom, tm = lax.axis_index("mom"), lax.axis_index("tm")
    local_k = start.shape[0]
    quarter = local_k // n
    rows = PANEL // n
    width = PANEL // n
    halves = rows // SUBLANES
    half_rows = n * SUBLANES
    subs = quarter // SUBLANES
    per_half = n * subs * SPIN
    pieces = halves * per_half
    chunks = rows // CHUNK
    half_chunks = SUBLANES // CHUNK
    n_x = n // 2
    tm_x, core = tm // 2, tm % 2
    partner = {"tm": tm_x * 2 + (1 - core)}
    step_scale = 1.0 / math.sqrt(PANEL)
    lane = lax.broadcasted_iota(jnp.int32, (1, LANES), 1)
    low = lane < PANEL
    sign = jnp.where(low, -1.0, 1.0).astype(jnp.float32)
    flat = n * rows * SPIN * local_k
    flat_snd = snd.reshape(flat, LANES)
    flat_rx_g = rx_g.reshape(flat, LANES)
    flat_rx_s = rx_s.reshape(flat, LANES)
    own_first = rx_g.reshape(local_k, SPIN, halves, half_rows, LANES)
    part = out.reshape(local_k, SPIN, halves, half_rows, LANES)
    stacks = (stk_a, stk_b)
    own_last = recv.reshape(halves, local_k, SPIN, half_rows, LANES)
    near_left = mom < n // 2

    def swap(x):
        return pltpu.roll(x, PANEL, 1)

    def rot(x):
        return swap(x) * sign

    barrier = pltpu.get_barrier_semaphore()
    for o in range(1, n):
        pl.semaphore_signal(barrier, inc=1, device_id={"mom": lax.rem(mom + o, n)}, device_id_type=MESH)
    for o in range(1, n):
        pl.semaphore_signal(barrier, inc=1, device_id={"tm": lax.rem(tm + o, n)}, device_id_type=MESH)

    def remote(source, target, send, recv_sem, device):
        return pltpu.make_async_remote_copy(
            src_ref=source, dst_ref=target, send_sem=send, recv_sem=recv_sem,
            device_id=device, device_id_type=MESH)

    def local(source, target, sem):
        return pltpu.make_async_copy(source, target, sem)

    def span(q):
        return pl.ds(q * CHUNK, CHUNK)

    def forward(q, o):
        peer = lax.rem(mom + o, n)
        return remote(snd.at[peer, span(q)], recv.at[span(q), :, mom], fs.at[o], fr.at[q], {"mom": peer})

    def forward_own(q):
        return local(snd.at[mom, span(q)], recv.at[span(q), :, mom], fr.at[q])

    def panel_out(q, o):
        peer = lax.rem(tm + o, n)
        return remote(recv.at[span(q), :, :, peer], rx_g.at[tm, span(q)], gs.at[o], gr.at[q // half_chunks], {"tm": peer})

    def panel_own(q):
        return local(recv.at[span(q), :, :, tm], rx_g.at[tm, span(q)], gr.at[q // half_chunks])

    def sigma_out(n_pass, q, o):
        peer = lax.rem(tm + o, n)
        return remote(
            sig.at[span(q), :, :, peer], rx_s.at[tm, span(q)], ss.at[n_pass, o], sr.at[n_pass, q // half_chunks],
            {"tm": peer})

    def sigma_own(n_pass, q):
        return local(sig.at[span(q), :, :, tm], rx_s.at[tm, span(q)], sr.at[n_pass, q // half_chunks])

    def place(p):
        half, rest = p // per_half, p % per_half
        group, turn = rest // n, rest % n
        odd = turn % 2
        block = (1 - odd) * (n - 1 - turn // 2) + odd * (turn // 2)
        return half, group // SPIN, group % SPIN, block

    def next_out(p, o):
        half, sub, s, block = place(p)
        peer = lax.rem(tm + o, n)
        at, ks = pl.ds(half * SUBLANES, SUBLANES), pl.ds(sub * SUBLANES, SUBLANES)
        return remote(
            snd.at[peer, at, s, block, ks], recv.at[at, s, block, tm, ks], ts.at[o], tr.at[half], {"tm": peer})

    def next_own(p):
        half, sub, s, block = place(p)
        at, ks = pl.ds(half * SUBLANES, SUBLANES), pl.ds(sub * SUBLANES, SUBLANES)
        return local(snd.at[tm, at, s, block, ks], recv.at[at, s, block, tm, ks], tr.at[half])

    def window(p):
        half, sub, s, block = place(p)
        return pl.ds(block * quarter + sub * SUBLANES, SUBLANES), s, half

    def whole(ref, sem):
        return local(ref, ref, sem)

    def sent(n_pass, p):
        half, _, _, block = place(p)
        return half if n_pass == 0 else block

    def right_out(n_pass, p):
        at = window(p)
        return remote(
            rbuf.at[at], rbuf.at[at], rs.at[n_pass, sent(n_pass, p)], rr.at[p],
            {"mom": jnp.minimum(mom + 1, n - 1)})

    def left_out(n_pass, p):
        at = window(p)
        return remote(
            lbuf.at[at], lbuf.at[at], ls.at[n_pass, sent(n_pass, p)], lr.at[p],
            {"mom": jnp.maximum(mom - 1, 0)})

    class Spread:
        def __init__(self, at, source, target):
            self.at, self.source, self.target = at, source, target

        def own(self):
            return local(self.source, self.target(tm), al.at[self.at])

        def pair(self):
            return remote(self.source, self.target(tm), aps.at[self.at], apr.at[self.at], partner)

        def across(self, o):
            peer = lax.rem(tm_x + o, n_x)
            return remote(
                self.source, self.target(tm), axs.at[self.at, o - 1], axr.at[self.at, o - 1], {"tm": peer * 2 + core})

        def relay(self, o):
            held = self.target(lax.rem(tm_x + n_x - o, n_x) * 2 + core)
            return remote(held, held, aqs.at[self.at, o - 1], aqr.at[self.at, o - 1], partner)

        def begin(self):
            for o in range(1, n_x):
                self.across(o).start()
            self.pair().start()
            self.own().start()

        def pass_on(self):
            for o in range(1, n_x):
                self.across(o).wait_recv()
                self.relay(o).start()

        def arrive(self):
            self.own().wait()
            self.pair().wait_recv()
            for o in range(1, n_x):
                self.relay(o).wait_recv()
                self.relay(o).wait_send()

        def end(self):
            self.pair().wait_send()
            for o in range(1, n_x):
                self.across(o).wait_send()

    guesses = Spread(0, guess, lambda t: guess_all.at[t])
    def firsts(half, sub, s):
        return Spread(
            1 + (half * subs + sub) * SPIN + s, tot.at[0, pl.ds(sub * SUBLANES, SUBLANES), s, half],
            lambda t: own_first.at[pl.ds(t * quarter + sub * SUBLANES, SUBLANES), s, half])

    def lasts(half, sub, s):
        return Spread(
            1 + ((halves + half) * subs + sub) * SPIN + s, tot.at[1, pl.ds(sub * SUBLANES, SUBLANES), s, half],
            lambda t: own_last.at[half, pl.ds(t * quarter + sub * SUBLANES, SUBLANES), s])

    def spread_rows(target, half, s, k, parts):
        for j, value in enumerate(block_transpose(parts, lane, width)):
            at = ((j * rows + half * SUBLANES) * SPIN + s) * local_k + k
            target[pl.ds(at, SUBLANES, stride=SPIN * local_k), :] = value

    def gather_rows(source, half, s, k):
        parts = []
        for t in range(n):
            at = ((t * rows + half * SUBLANES) * SPIN + s) * local_k + k
            parts.append(source[pl.ds(at, SUBLANES, stride=SPIN * local_k), :])
        return jnp.concatenate(block_transpose(parts, lane, width), axis=0)

    def first_layout(half):
        @pl.loop(0, local_k, unroll=4)
        def _(k):
            for s in range(SPIN):
                parts = [start[k, s, half * half_rows + g * SUBLANES:half * half_rows + (g + 1) * SUBLANES, :]
                         for g in range(n)]
                spread_rows(flat_snd, half, s, k, parts)

    def keep_stack(n_pass, k, s, half, value):
        for at, piece in enumerate((value, rot(value))):
            stacks[n_pass][k, s, 0, at, half], stacks[n_pass][k, s, 1, at, half] = split(piece)

    def stack_of(n_pass, k, s):
        return tuple(stacks[n_pass][k, s, at].reshape(2 * PANEL, LANES) for at in range(2))

    def first_stack(half):
        whole(rx_g.at[:, pl.ds(half * SUBLANES, SUBLANES)], gr.at[half]).wait()

        @pl.loop(0, local_k, unroll=4)
        def _(k):
            for s in range(SPIN):
                keep_stack(0, k, s, half, gather_rows(flat_rx_g, half, s, k))

    def sigma(q):
        @pl.loop(0, CHUNK)
        def _(d):
            i = q * CHUNK + d
            both = jnp.concatenate(
                [recv[i, s].reshape(K, LANES) for s in range(SPIN)], axis=1)
            sums = dot3((fwd_split[0], fwd_split[1]), split(both))
            site, mirrored = [], []
            for s in range(SPIN):
                with_cos = sums[:K, s * LANES:(s + 1) * LANES]
                turned = rot(sums[K:, s * LANES:(s + 1) * LANES])
                site.append(with_cos + turned)
                mirrored.append(with_cos - turned)
            first, second = site
            flipped = swap(second)
            pair = (first * jnp.where(low, second, flipped)
                    + rot(first) * jnp.where(low, flipped, second)) * wvec[...]
            pair_rot = rot(pair)
            tops, bottoms = [], []
            for s in range(SPIN):
                other = mirrored[1 - s]
                flipped = swap(other)
                value = pair * jnp.where(low, other, flipped) - pair_rot * jnp.where(low, flipped, other)
                tops.append(value)
                bottoms.append(-rot(value))
            stacked = jnp.concatenate(
                [jnp.concatenate(tops, axis=1), jnp.concatenate(bottoms, axis=1)], axis=0)
            result = dot3((back_split[0], back_split[1]), split(stacked))
            for s in range(SPIN):
                sig[i, s] = result[:, s * LANES:(s + 1) * LANES].reshape(sig.shape[2:])

    def send_sigma(n_pass, q):
        for o in range(1, n):
            sigma_out(n_pass, q, o).start()
        sigma_own(n_pass, q).start()

    def wait_sigma(n_pass, half):
        whole(rx_s.at[:, pl.ds(half * SUBLANES, SUBLANES)], sr.at[n_pass, half]).wait()

    def second_sigma(q):
        half = q // half_chunks

        @pl.when(q % half_chunks == 0)
        def _():
            whole(recv.at[pl.ds(half * SUBLANES, SUBLANES)], tr.at[half]).wait()

        sigma(q)
        send_sigma(1, q)

    def convolve(n_pass, p):
        half, sub, s, block = place(p)

        @pl.when(p % per_half == 0)
        def _():
            wait_sigma(n_pass, half)

        results = []
        for m in range(SUBLANES):
            k = block * quarter + sub * SUBLANES + m
            value = split(gather_rows(flat_rx_s, half, s, k))
            results.append((k, dot3(value, stack_of(n_pass, k, s), True)))
        for k, result in results:
            part[k, s, half] = result

    def each(p, body):
        half, sub, s, block = place(p)
        done = [body((block * quarter + sub * SUBLANES + m, s, half), sub * SUBLANES + m) for m in range(SUBLANES)]
        for stores in done:
            for target, at, value in stores:
                target[at] = value

    def flows(n_pass, p):
        block = place(p)[3]
        if n_pass == 0:
            yes = block >= 0
            return yes, yes, yes, yes, yes
        return block >= mom, block > mom, block <= mom, block < mom, block == mom

    def origin(n_pass, p):
        _, send_right, _, send_left, _ = flows(n_pass, p)

        @pl.when(mom == 0)
        def _():
            each(p, lambda at, m: [(rbuf, at, part[at])])

            @pl.when(send_right)
            def _():
                right_out(n_pass, p).start()

        @pl.when(mom == n - 1)
        def _():
            each(p, lambda at, m: [(lbuf, at, part[at])])

            @pl.when(send_left)
            def _():
                left_out(n_pass, p).start()

    def near_step(n_pass, p):
        from_left, send_right, from_right, send_left, _ = flows(n_pass, p)

        @pl.when(near_left & (mom > 0) & from_left)
        def _():
            right_out(n_pass, p).wait_recv()

            each(p, lambda at, m: [(rbuf, at, rbuf[at] + part[at])])

            @pl.when(send_right)
            def _():
                right_out(n_pass, p).start()

        @pl.when((mom >= n // 2) & (mom < n - 1) & from_right)
        def _():
            left_out(n_pass, p).wait_recv()

            each(p, lambda at, m: [(lbuf, at, lbuf[at] + part[at])])

            @pl.when(send_left)
            def _():
                left_out(n_pass, p).start()

    def far_step(n_pass, p):
        from_left, send_right, from_right, send_left, keep = flows(n_pass, p)

        def one(mine, other, outer, send, copy):
            copy.wait_recv()
            if n_pass == 0:
                each(p, lambda at, m: [
                    (other, at, other[at] + part[at]), (part, at, mine[at] + other[at])])
            else:
                @pl.when(send)
                def _():
                    each(p, lambda at, m: [(other, at, other[at] + part[at])])

                @pl.when(keep)
                def _():
                    each(p, lambda at, m: [(tot, (1, m) + at[1:], mine[at] + other[at])])

            @pl.when(outer & send)
            def _():
                copy.start()

        @pl.when(near_left & from_right)
        def _():
            one(rbuf, lbuf, mom > 0, send_left, left_out(n_pass, p))

        @pl.when((mom >= n // 2) & from_left)
        def _():
            one(lbuf, rbuf, mom < n - 1, send_right, right_out(n_pass, p))

    def update(p):
        half, sub, s, block = place(p)

        @pl.when(block == mom)
        def _():
            each(p, lambda at, m: [(tot, (0, m) + at[1:], part[at])])

            @pl.when(half < halves - 1)
            def _():
                firsts(half, sub, s).begin()

        results = []
        for m in range(SUBLANES):
            k = block * quarter + sub * SUBLANES + m
            old = stk_a[k, s, 0, 0, half].astype(jnp.float32) + stk_a[k, s, 1, 0, half].astype(jnp.float32)
            results.append((k, old + step_scale * dot3(split(part[k, s, half]), stack_of(0, k, s))))
        for k, new in results:
            keep_stack(1, k, s, half, new)
            spread_rows(flat_snd, half, s, k, [new[g * SUBLANES:(g + 1) * SUBLANES, :] for g in range(n)])

        for o in range(1, n):
            next_out(p, o).start()
        next_own(p).start()

    def own_panel(group):
        results = []
        for m in range(SUBLANES // 2):
            k = group * (SUBLANES // 2) + m
            for s in range(SPIN):
                first = start[k, s]
                right = split(jnp.concatenate([first, rot(first)], axis=0))
                new = first + step_scale * dot3(split(own_first[k, s].reshape(PANEL, LANES)), right)
                results.append((k, s, new))
        for k, s, new in results:
            own_first[k, s] = new.reshape(halves, half_rows, LANES)

    def store(sub, s):
        parts = (n, quarter, SPIN, PANEL, LANES)
        at = pl.ds(sub * SUBLANES, SUBLANES)
        return local(
            out.reshape(parts).at[:, at, s], result.reshape(parts).at[:, at, s], out_sem.at[sub * SPIN + s])

    def finish(sub, s):
        is_block = chosen > 0.5
        for half in range(halves):
            lasts(half, sub, s).pass_on()
        for half in range(halves):
            lasts(half, sub, s).arrive()

        @pl.loop(0, n)
        def _(t):
            results = []
            for m in range(SUBLANES):
                k = t * quarter + sub * SUBLANES + m
                whole = jnp.concatenate([own_last[half, k, s] for half in range(halves)], axis=0)
                d_rows = jnp.concatenate([guess_all[at, k, s] for at in range(n)], axis=0)
                right = jnp.where(is_block, whole, own_first[k, s].reshape(PANEL, LANES))
                left = jnp.where(is_block, d_rows, whole)
                right = split(jnp.concatenate([right, rot(right)], axis=0))
                new = jnp.where(is_block, d_rows, start[k, s]) + step_scale * dot3(split(left), right)
                results.append((k, new))
            for k, new in results:
                out[k, s] = new

        store(sub, s).start()

    def begin_forward(q):
        for o in range(1, n):
            forward(q, o).start()
        forward_own(q).start()

    first_layout(0)
    pl.semaphore_wait(barrier, 2 * n - 2)
    for q in range(min(AHEAD, half_chunks)):
        begin_forward(q)
    for half in range(1, halves):
        first_layout(half)

    for at, table in enumerate(tables(ordering[...])):
        fwd_split[0, at * K:(at + 1) * K, :], fwd_split[1, at * K:(at + 1) * K, :] = split(table)
        turned = split(table.T)
        back_split[0, :, at * K:(at + 1) * K], back_split[1, :, at * K:(at + 1) * K] = turned

    owners = slab_owner[...].astype(jnp.float32)
    slabs = lax.broadcasted_iota(jnp.int32, owners.shape, 1).astype(jnp.float32)
    oldest = expiring[...].astype(jnp.float32)
    mine = tm.astype(jnp.float32)
    slab_mine = jnp.sum(jnp.where(owners == mine, slabs, 0.0), axis=1, keepdims=True)
    owner_expiring = jnp.sum(jnp.where(slabs == oldest, owners, 0.0), axis=1, keepdims=True)
    position = slab_mine - oldest
    position = jnp.where(position < 0.0, position + n, position)
    held = (mom * rows + lane % rows).astype(jnp.float32)
    ahead = (n * PANEL - 1) - (position * PANEL + held)
    strength = coupling[...] * coupling[...]
    wvec[...] = strength * (jnp.exp(-1.5 * ahead / (n * PANEL)) / math.sqrt(n * PANEL))
    chosen = jnp.where(owner_expiring == mine, jnp.ones((1, LANES), jnp.float32), 0.0)

    @pl.loop(0, chunks + 1)
    def _(q):
        @pl.when(q < chunks)
        def _():
            whole(recv.at[span(q)], fr.at[q]).wait()

            @pl.when(q + AHEAD < chunks)
            def _():
                begin_forward(q + AHEAD)

            for o in range(1, n):
                panel_out(q, o).start()
            panel_own(q).start()
            sigma(q)
            send_sigma(0, q)

        for half in range(halves - 1):
            @pl.when(q == (half + 1) * half_chunks + 1)
            def _():
                first_stack(half)

        @pl.when(q == chunks)
        def _():
            first_stack(halves - 1)

    for o in range(1, n):
        whole(snd.at[0], fs.at[o]).wait()
        whole(recv.at[:, :, :, 0], gs.at[o]).wait()
        whole(sig.at[:, :, :, 0], ss.at[0, o]).wait()

    for o in range(1, n):
        pl.semaphore_signal(room, inc=1, device_id={"tm": lax.rem(tm + o, n)}, device_id_type=MESH)
    guesses.begin()

    def within(low, x, high):
        return (x >= low) & (x < high)

    lead, rest = LEAD[0], LEAD[1] + LAG
    told = lead + LAG
    first_sigma_at = told + per_half + ARRIVE
    last_sigma_at = told + pieces + 1
    last_at = told + per_half + ARRIVE + LAST_AT
    panel_at = last_at + (halves - 1) * (per_half + rest) + PANEL_AT
    period = per_half + rest

    def last_piece(u, body):
        seg, at = u // period, u % period

        @pl.when((u >= 0) & (seg < halves) & (at < per_half))
        def _():
            body(seg * per_half + at)

    def last_start(p):
        for half in range(halves):
            @pl.when(p == half * per_half)
            def _():
                @pl.when(mom > 0)
                def _():
                    pl.semaphore_wait(credit.at[half, 0], 1)

                @pl.when(mom < n - 1)
                def _():
                    pl.semaphore_wait(credit.at[half, 1], 1)

        convolve(1, p)
        origin(1, p)

    def last_far(p):
        far_step(1, p)
        half, sub, s, block = place(p)

        @pl.when(block == mom)
        def _():
            lasts(half, sub, s).begin()

        d = p - pieces + 2 * (subs * SPIN - 1)

        @pl.when((d >= 0) & (d % 2 == 0))
        def _():
            finish((d // 2) // SPIN, (d // 2) % SPIN)

    def free(half):
        @pl.when(mom < n - 1)
        def _():
            whole(rbuf.at[:, :, half], rs.at[0, half]).wait()

        @pl.when(mom > 0)
        def _():
            whole(lbuf.at[:, :, half], ls.at[0, half]).wait()

        @pl.when(mom > 0)
        def _():
            pl.semaphore_signal(
                credit.at[half, 1], inc=1, device_id={"mom": jnp.maximum(mom - 1, 0)}, device_id_type=MESH)

        @pl.when(mom < n - 1)
        def _():
            pl.semaphore_signal(
                credit.at[half, 0], inc=1, device_id={"mom": jnp.minimum(mom + 1, n - 1)}, device_id_type=MESH)

    @pl.loop(0, last_at + halves * period)
    def _(t):
        @pl.when(t < pieces)
        def _():
            convolve(0, t)
            origin(0, t)

        @pl.when(within(lead, t, lead + pieces))
        def _():
            near_step(0, t - lead)

        @pl.when(within(told, t, told + pieces))
        def _():
            p = t - told
            far_step(0, p)

            @pl.when(p == 0)
            def _():
                pl.semaphore_wait(room, n - 1)

            update(p)

        for half in range(halves):
            @pl.when(t == told + (half + 1) * per_half + ARRIVE + 1)
            def _():
                free(half)

        @pl.when(t == told + per_half)
        def _():
            guesses.pass_on()

        @pl.when(within(first_sigma_at, t, first_sigma_at + (halves - 1) * half_chunks))
        def _():
            second_sigma(t - first_sigma_at)

        last_piece(t - last_at, last_start)
        last_piece(t - last_at - LEAD[1], lambda p: near_step(1, p))
        last_piece(t - last_at - rest, last_far)

        @pl.when(within(last_sigma_at + ARRIVE - 1, t, last_sigma_at + ARRIVE + 1))
        def _():
            @pl.loop(0, half_chunks // 2)
            def _(d):
                second_sigma((halves - 1) * half_chunks + (t - last_sigma_at - ARRIVE + 1) * (half_chunks // 2) + d)

        @pl.when(t == last_sigma_at + ARRIVE + 1)
        def _():
            @pl.loop(0, subs * SPIN)
            def _(d):
                firsts(halves - 1, d // SPIN, d % SPIN).begin()

        @pl.when(t == panel_at)
        def _():
            @pl.loop(0, halves * subs * SPIN)
            def _(d):
                firsts(d // (subs * SPIN), d // SPIN % subs, d % SPIN).pass_on()

            @pl.loop(0, halves * subs * SPIN)
            def _(d):
                firsts(d // (subs * SPIN), d // SPIN % subs, d % SPIN).arrive()

            guesses.arrive()

        @pl.when(within(panel_at, t, panel_at + local_k // SUBLANES))
        def _():
            own_panel(2 * (t - panel_at))
            own_panel(2 * (t - panel_at) + 1)

    finish(subs - 1, SPIN - 1)

    for block in range(n):
        ks = pl.ds(block * quarter, quarter)

        @pl.when((mom < n - 1) & (block > mom))
        def _():
            whole(rbuf.at[ks], rs.at[1, block]).wait()

        @pl.when((mom > 0) & (block < mom))
        def _():
            whole(lbuf.at[ks], ls.at[1, block]).wait()

    for o in range(1, n):
        whole(snd.at[0], ts.at[o]).wait()
        whole(sig.at[:, :, :, 0], ss.at[1, o]).wait()

    @pl.loop(0, halves * subs * SPIN)
    def _(d):
        at = d // (subs * SPIN), d // SPIN % subs, d % SPIN
        firsts(*at).end()
        lasts(*at).end()

    guesses.end()
    for sub in range(subs):
        for s in range(SPIN):
            store(sub, s).wait()


def share_step(n, start, guess, ordering, coupling, slab_owner, expiring):
    local_k = start.shape[0]
    quarter, rows = local_k // n, PANEL // n
    halves, subs = rows // SUBLANES, quarter // SUBLANES
    pieces, chunks = halves * n * subs * SPIN, rows // CHUNK
    spreads, far = 1 + 2 * halves * subs * SPIN, max(n // 2 - 1, 1)
    half_rows = n * SUBLANES
    f32, bf16 = jnp.float32, jnp.bfloat16
    dma = pltpu.SemaphoreType.DMA
    vmem = pl.BlockSpec(memory_space=pltpu.VMEM)
    moved = pltpu.VMEM((n, rows, SPIN, n, quarter, LANES), f32)
    grid = pltpu.VMEM((rows, SPIN, n, n, quarter, LANES), f32)
    square = (local_k, SPIN, halves, half_rows, LANES)
    stack = pltpu.VMEM((local_k, SPIN, 2, 2, halves, half_rows, LANES), bf16)
    return pl.pallas_call(
        functools.partial(share_kernel, n),
        out_shape=jax.ShapeDtypeStruct(start.shape, f32),
        in_specs=[vmem] * 6,
        out_specs=pl.BlockSpec(memory_space=pl.ANY),
        scratch_shapes=[
            pltpu.VMEM(start.shape, f32), dma((subs * SPIN,)),
            moved, grid, grid, moved, moved,
            stack, stack, pltpu.VMEM((1, LANES), f32),
            pltpu.VMEM(square, f32), pltpu.VMEM(square, f32),
            pltpu.VMEM((PASSES, quarter) + square[1:], f32),
            pltpu.VMEM((n,) + guess.shape, f32),
            pltpu.VMEM((2, 2 * K, K), bf16),
            pltpu.VMEM((2, K, 2 * K), bf16),
            dma((n,)), dma((chunks,)), dma((n,)), dma((halves,)),
            dma((PASSES, n)), dma((PASSES, halves)), dma((n,)), dma((halves,)),
            dma((PASSES, max(n, halves))), dma((pieces,)), dma((PASSES, max(n, halves))), dma((pieces,)),
            pltpu.SemaphoreType.REGULAR((halves, 2)), pltpu.SemaphoreType.REGULAR,
            dma((spreads,)), dma((spreads,)), dma((spreads,)),
            dma((spreads, far)), dma((spreads, far)), dma((spreads, far)), dma((spreads, far)),
        ],
        compiler_params=pltpu.CompilerParams(
            collective_id=0, has_side_effects=True, vmem_limit_bytes=63 * 1024 * 1024),
        name="share_step",
    )(start, guess, ordering, coupling, slab_owner, expiring)


def body(panel_start, block_guess, coupling, slab_owner, expiring, ordering):
    slab_count = lax.axis_size("tm")
    n_mom = lax.axis_size("mom")
    local_k = panel_start.shape[0]
    unit = SUBLANES * slab_count
    if n_mom == slab_count and local_k % unit == 0 and PANEL % unit == 0:
        return share_step(
            n_mom, panel_start, block_guess, ordering[None, :], coupling[None, :], slab_owner[None, :], expiring[None, :])
    own_index = lax.axis_index("tm")
    blocks = jnp.arange(slab_count, dtype=jnp.int32)
    slab_mine = jnp.sum(blocks * (slab_owner == own_index).astype(jnp.int32))
    position = (slab_mine - expiring[0]) % slab_count
    window = slab_count * PANEL
    times = position * PANEL + jnp.arange(PANEL, dtype=jnp.int32)
    weights = jnp.exp(-1.5 * (window - 1 - times).astype(jnp.float32) / window) / math.sqrt(window)
    strength = coupling[0] * coupling[0]
    wvec = (strength * jnp.concatenate([weights, weights]))[None, :]
    owner_expiring = jnp.sum(slab_owner * (blocks == expiring[0]).astype(jnp.int32))
    chosen = jnp.broadcast_to((own_index == owner_expiring).astype(jnp.float32), (1, LANES))
    start = panel_start.reshape(local_k, SPIN, CHUNKS, PANEL // CHUNKS, LANES)
    result = panel_step(n_mom, slab_count, start, block_guess, ordering[None, :], wvec, chosen)
    return result.reshape(panel_start.shape)


def solution(mesh):
    return jax.shard_map(
        body,
        mesh=mesh,
        in_specs=(
            P("mom", "groups", None, "tm"),
            P("mom", "groups", "tm", None),
            P("groups"),
            P("groups"),
            P("groups"),
            P(),
        ),
        out_specs=P("mom", "groups", None, "tm"),
        check_vma=False,
    )
```

```python
import functools
import math

import jax
import jax.numpy as jnp
from jax import lax
from jax.experimental import pallas as pl
from jax.experimental.pallas import tpu as pltpu
from jax.sharding import PartitionSpec as P

LSIDE = 16
K = LSIDE * LSIDE
PANEL = 64
PASSES = 2
SPIN = 2
LANES = 2 * PANEL
CHUNKS = 2
MESH = pl.DeviceIdType.MESH


def tables(ordering):
    bits = LSIDE.bit_length() - 1
    site = lax.broadcasted_iota(jnp.int32, (K, K), 0)
    phases = ((site >> bits) * (ordering >> bits) + (site & (LSIDE - 1)) * (ordering & (LSIDE - 1))) & (LSIDE - 1)
    angles = phases.astype(jnp.float32) * (2.0 * math.pi / LSIDE)
    return jnp.cos(angles) / LSIDE, jnp.sin(angles) / LSIDE


def split(x):
    high = x.astype(jnp.bfloat16)
    return high, (x - high.astype(jnp.float32)).astype(jnp.bfloat16)


def dot3(left, right, transposed=False):
    dims = (((1,), (1 if transposed else 0,)), ((), ()))

    def one(a, b):
        return lax.dot_general(a, b, dims, preferred_element_type=jnp.float32)

    return one(left[0], right[0]) + (one(left[0], right[1]) + one(left[1], right[0]))


def step_kernel(
    n_mom, n_tm, start, guess, ordering, wvec, chosen,
    out, cur, recv, sig, ret, fwd_split, back_split, stk, part, conv, pair_buf, ring_buf, guess_all,
    local_sem, guess_own, fs, fr, rs, rr, ps, pr, ss, sr, gs, gr, qs, qr, ds, dr,
):
    mom, tm = lax.axis_index("mom"), lax.axis_index("tm")
    rows, local_k = cur.shape[3], cur.shape[4]
    group = n_mom * rows
    n_x = n_tm // 2
    half = local_k // 2
    share = half // n_x
    tm_x, core = tm // 2, tm % 2
    step_scale = 1.0 / math.sqrt(PANEL)
    lane = lax.broadcasted_iota(jnp.int32, (1, LANES), 1)
    low = lane < PANEL
    sign = jnp.where(low, -1.0, 1.0).astype(jnp.float32)
    flat_cur = cur.reshape(CHUNKS * SPIN * group * local_k, LANES)
    flat_ret = ret.reshape(CHUNKS * SPIN * group * local_k, LANES)

    def swap(x):
        return pltpu.roll(x, PANEL, 1)

    def rot(x):
        return swap(x) * sign

    barrier = pltpu.get_barrier_semaphore()
    for o in range(1, n_mom):
        pl.semaphore_signal(barrier, inc=1, device_id={"mom": lax.rem(mom + o, n_mom)}, device_id_type=MESH)
    for o in range(1, n_tm):
        pl.semaphore_signal(barrier, inc=1, device_id={"tm": lax.rem(tm + o, n_tm)}, device_id_type=MESH)

    mine = pl.ds(mom * local_k, local_k)
    other_half = pl.ds((1 - core) * half, half)
    share_at = core * half + tm_x * share
    own_share = pl.ds(share_at, share)
    partner = {"tm": tm_x * 2 + (1 - core)}

    def remote(source, target, send, recv_sem, device):
        return pltpu.make_async_remote_copy(
            src_ref=source, dst_ref=target, send_sem=send, recv_sem=recv_sem,
            device_id=device, device_id_type=MESH)

    def forward(n, c, o):
        peer = lax.rem(mom + o, n_mom)
        return remote(cur.at[c, :, peer], recv.at[c, :, :, mine, :], fs.at[n, c, o], fr.at[n, c, o], {"mom": peer})

    def forward_own(n, c):
        return pltpu.make_async_copy(cur.at[c, :, mom], recv.at[c, :, :, mine, :], local_sem.at[n, c, 0])

    def back(n, c, o):
        peer = lax.rem(mom + o, n_mom)
        return remote(
            sig.at[c, :, :, pl.ds(peer * local_k, local_k), :], ret.at[c, :, mom],
            rs.at[n, c, o], rr.at[n, c, o], {"mom": peer})

    def back_own(n, c):
        return pltpu.make_async_copy(sig.at[c, :, :, mine, :], ret.at[c, :, mom], local_sem.at[n, c, 1])

    def pair_up(n, c):
        return remote(part.at[c, other_half], pair_buf.at[c], ps.at[n, c], pr.at[n, c], partner)

    def scatter(n, c, o):
        peer = lax.rem(tm_x + o, n_x)
        return remote(
            part.at[c, pl.ds(core * half + peer * share, share)], ring_buf.at[c, o - 1],
            ss.at[n, c, o], sr.at[n, c, o], {"tm": peer * 2 + core})

    def gather(n, c, o):
        peer = lax.rem(tm_x + o, n_x)
        return remote(
            conv.at[c, own_share], conv.at[c, own_share],
            gs.at[n, c, o], gr.at[n, c, o], {"tm": peer * 2 + core})

    def pair_down(n, c, o):
        held = pl.ds(core * half + lax.rem(tm_x + n_x - o, n_x) * share, share)
        return remote(conv.at[c, held], conv.at[c, held], qs.at[n, c, o], qr.at[n, c, o], partner)

    def pair_down_recv(n, c):
        for o in range(n_x):
            pair_down(n, c, o).wait_recv()

    def guess_copy(o):
        return remote(guess, guess_all.at[tm], ds.at[o], dr.at[o], {"tm": lax.rem(tm + o, n_tm)})

    def guess_local():
        return pltpu.make_async_copy(guess, guess_all.at[tm], guess_own)

    def send_forward(n, c):
        for o in range(1, n_mom):
            forward(n, c, o).start()
        forward_own(n, c).start()

    def keep_stack(n, k, s, c, value):
        turned = rot(value)
        for at, piece in ((c * group, value), (PANEL + c * group, turned)):
            high, rest = split(piece)
            stk[n, 0, k, s, at:at + group, :] = high
            stk[n, 1, k, s, at:at + group, :] = rest

    def first_layout(c):
        @pl.loop(0, local_k)
        def _(k):
            for s in range(SPIN):
                at = ((c * SPIN + s) * group) * local_k + k
                flat_cur[pl.ds(at, group, stride=local_k), :] = start[k, s, c]

    def sigma(n, c):
        for o in range(1, n_mom):
            forward(n, c, o).wait_recv()
        forward_own(n, c).wait()
        if n > 0:
            for o in range(1, n_mom):
                back(n - 1, c, o).wait_send()

        @pl.loop(0, rows)
        def _(i):
            both = jnp.concatenate([recv[c, 0, i], recv[c, 1, i]], axis=1)
            sums = dot3((fwd_split[0], fwd_split[1]), split(both))
            site, mirrored = [], []
            for s in range(SPIN):
                with_cos = sums[:K, s * LANES:(s + 1) * LANES]
                turned = rot(sums[K:, s * LANES:(s + 1) * LANES])
                site.append(with_cos + turned)
                mirrored.append(with_cos - turned)
            first, second = site
            flipped = swap(second)
            pair = (first * jnp.where(low, second, flipped)
                    + rot(first) * jnp.where(low, flipped, second)) * wvec[...]
            pair_rot = rot(pair)
            tops, bottoms = [], []
            for s in range(SPIN):
                other = mirrored[1 - s]
                flipped = swap(other)
                value = pair * jnp.where(low, other, flipped) - pair_rot * jnp.where(low, flipped, other)
                tops.append(value)
                bottoms.append(-rot(value))
            stacked = jnp.concatenate(
                [jnp.concatenate(tops, axis=1), jnp.concatenate(bottoms, axis=1)], axis=0)
            result = dot3((back_split[0], back_split[1]), split(stacked))
            for s in range(SPIN):
                sig[c, s, i] = result[:, s * LANES:(s + 1) * LANES]

        for o in range(1, n_mom):
            back(n, c, o).start()
        back_own(n, c).start()

    def convolve(n, c):
        for o in range(1, n_mom):
            back(n, c, o).wait_recv()
        back_own(n, c).wait()
        if n > 0:
            pair_up(n - 1, c).wait_send()
            for o in range(n_x):
                pair_down(n - 1, c, o).wait_send()
            for o in range(1, n_x):
                scatter(n - 1, c, o).wait_send()
                gather(n - 1, c, o).wait_send()

        def some(base):
            @pl.loop(0, half, unroll=8)
            def _(i):
                k = base + i
                for s in range(SPIN):
                    at = ((c * SPIN + s) * group) * local_k + k
                    value = split(flat_ret[pl.ds(at, group, stride=local_k), :])
                    part[c, k, s] = dot3(value, (stk[n, 0, k, s], stk[n, 1, k, s]), True)

        some((1 - core) * half)
        pair_up(n, c).start()
        some(core * half)

    def reduce(n, c):
        pair_up(n, c).wait_recv()

        @pl.loop(0, half)
        def _(i):
            part[c, core * half + i] = part[c, core * half + i] + pair_buf[c, i]

        for o in range(1, n_x):
            scatter(n, c, o).start()
        for o in range(1, n_x):
            scatter(n, c, o).wait_recv()

        @pl.loop(0, share)
        def _(i):
            total = part[c, share_at + i]
            for o in range(1, n_x):
                total = total + ring_buf[c, o - 1, i]
            conv[c, share_at + i] = total

        for o in range(1, n_x):
            gather(n, c, o).start()
        pair_down(n, c, 0).start()
        for o in range(1, n_x):
            gather(n, c, o).wait_recv()
            pair_down(n, c, o).start()

    def update(n, c):
        for o in range(1, n_mom):
            forward(n, c, o).wait_send()

        def some(base):
            @pl.loop(0, half, unroll=8)
            def _(i):
                k = base + i
                for s in range(SPIN):
                    new = start[k, s, c] + step_scale * dot3(
                        split(conv[c, k, s]), (stk[n, 0, k, s], stk[n, 1, k, s]))
                    at = ((c * SPIN + s) * group) * local_k + k
                    flat_cur[pl.ds(at, group, stride=local_k), :] = new
                    keep_stack(n + 1, k, s, c, new)

        some(core * half)
        pair_down_recv(n, c)
        some((1 - core) * half)

    def finish(n):
        is_block = chosen[...] > 0.5

        def some(base):
            @pl.loop(0, half, unroll=4)
            def _(i):
                k = base + i
                for s in range(SPIN):
                    whole = jnp.concatenate([conv[c, k, s] for c in range(CHUNKS)], axis=0)
                    d = jnp.concatenate([guess_all[t, k, s] for t in range(n_tm)], axis=0)
                    first = jnp.concatenate([start[k, s, c] for c in range(CHUNKS)], axis=0)
                    panel = stk[n, 0, k, s].astype(jnp.float32) + stk[n, 1, k, s].astype(jnp.float32)
                    right = jnp.where(is_block, jnp.concatenate([whole, rot(whole)], axis=0), panel)
                    left = jnp.where(is_block, d, whole)
                    new = jnp.where(is_block, d, first) + step_scale * dot3(split(left), split(right))
                    for c in range(CHUNKS):
                        out[k, s, c] = new[c * group:(c + 1) * group, :]

        for c in range(CHUNKS - 1):
            pair_down_recv(n, c)
        some(core * half)
        pair_down_recv(n, CHUNKS - 1)
        some((1 - core) * half)

    first_layout(0)
    pl.semaphore_wait(barrier, n_mom + n_tm - 2)
    send_forward(0, 0)
    for c in range(1, CHUNKS):
        first_layout(c)
        send_forward(0, c)
    for o in range(1, n_tm):
        guess_copy(o).start()
    guess_local().start()

    for at, table in enumerate(tables(ordering[...])):
        fwd_split[0, at * K:(at + 1) * K, :], fwd_split[1, at * K:(at + 1) * K, :] = split(table)
        turned = split(table.T)
        back_split[0, :, at * K:(at + 1) * K], back_split[1, :, at * K:(at + 1) * K] = turned

    @pl.loop(0, local_k, unroll=4)
    def _(k):
        for s in range(SPIN):
            for c in range(CHUNKS):
                keep_stack(0, k, s, c, start[k, s, c])

    for n in range(PASSES):
        for c in range(CHUNKS):
            sigma(n, c)
        for c in range(CHUNKS):
            convolve(n, c)
            reduce(n, c)
            if n < PASSES - 1:
                update(n, c)
                send_forward(n + 1, c)

    for o in range(1, n_tm):
        guess_copy(o).wait_recv()
    guess_local().wait()
    finish(PASSES - 1)

    n = PASSES - 1
    for c in range(CHUNKS):
        pair_up(n, c).wait_send()
        for o in range(n_x):
            pair_down(n, c, o).wait_send()
        for o in range(1, n_x):
            scatter(n, c, o).wait_send()
            gather(n, c, o).wait_send()
        for o in range(1, n_mom):
            forward(n, c, o).wait_send()
            back(n, c, o).wait_send()
    for o in range(1, n_tm):
        guess_copy(o).wait_send()


def panel_step(n_mom, n_tm, start, guess, ordering, wvec, chosen):
    local_k = start.shape[0]
    group = start.shape[3]
    rows = group // n_mom
    share = local_k // n_tm
    panel = (CHUNKS, SPIN, n_mom, rows, local_k, LANES)
    sites = (CHUNKS, SPIN, rows, K, LANES)
    f32, bf16 = jnp.float32, jnp.bfloat16
    dma = pltpu.SemaphoreType.DMA
    vmem = pl.BlockSpec(memory_space=pltpu.VMEM)
    one, many_mom, many_x = (PASSES, CHUNKS), (PASSES, CHUNKS, n_mom), (PASSES, CHUNKS, n_tm // 2)
    return pl.pallas_call(
        functools.partial(step_kernel, n_mom, n_tm),
        out_shape=jax.ShapeDtypeStruct(start.shape, f32),
        in_specs=[vmem] * 5,
        out_specs=vmem,
        scratch_shapes=[
            pltpu.VMEM(panel, f32),
            pltpu.VMEM(sites, f32),
            pltpu.VMEM(sites, f32),
            pltpu.VMEM(panel, f32),
            pltpu.VMEM((2, 2 * K, K), bf16),
            pltpu.VMEM((2, K, 2 * K), bf16),
            pltpu.VMEM((PASSES, 2, local_k, SPIN, LANES, LANES), bf16),
            pltpu.VMEM((CHUNKS, local_k, SPIN, group, LANES), f32),
            pltpu.VMEM((CHUNKS, local_k, SPIN, group, LANES), f32),
            pltpu.VMEM((CHUNKS, local_k // 2, SPIN, group, LANES), f32),
            pltpu.VMEM((CHUNKS, max(n_tm // 2 - 1, 1), share, SPIN, group, LANES), f32),
            pltpu.VMEM((n_tm,) + guess.shape, f32),
            dma(one + (2,)), dma,
            dma(many_mom), dma(many_mom), dma(many_mom), dma(many_mom),
            dma(one), dma(one),
            dma(many_x), dma(many_x), dma(many_x), dma(many_x),
            dma(many_x), dma(many_x),
            dma((n_tm,)), dma((n_tm,)),
        ],
        compiler_params=pltpu.CompilerParams(
            collective_id=0, has_side_effects=True, vmem_limit_bytes=63 * 1024 * 1024),
        name="panel_step",
    )(start, guess, ordering, wvec, chosen)


SUBLANES = 8
CHUNK = 1
AHEAD = 2
LAG = 2
LEAD = (4, 7)
ARRIVE = 1
FINISH_AT = 7
BURST = 4
SIGMA_AT = 3
LAST_AT = 12
PANEL_AT = 6


def wide(left, right, transposed=False):
    rows = left[0].shape[0]
    dims = (((1,), (1 if transposed else 0,)), ((), ()))
    both = lax.dot_general(
        jnp.concatenate(left, axis=0), jnp.concatenate(right, axis=0 if transposed else 1), dims,
        preferred_element_type=jnp.float32)
    return both[:rows, :LANES] + (both[:rows, LANES:] + both[rows:, :LANES])


def block_transpose(blocks, lane, width):
    blocks = list(blocks)
    bit = 1
    while bit < len(blocks):
        keep = (lane // width) % (2 * bit) < bit
        for p in range(len(blocks)):
            if p & bit == 0:
                a, b = blocks[p], blocks[p + bit]
                blocks[p] = jnp.where(keep, a, pltpu.roll(b, bit * width, 1))
                blocks[p + bit] = jnp.where(keep, pltpu.roll(a, LANES - bit * width, 1), b)
        bit *= 2
    return blocks


def share_kernel(
    n, start, guess, ordering, coupling, slab_owner, expiring,
    result, out, out_sem, snd, recv, sig, rx_g, rx_s, stk_a, stk_b, wvec, rbuf, lbuf, tot, guess_all, fwd_split, back_split,
    fs, fr, gs, gr, ss, sr, ts, tr, rs, rr, ls, lr, credit, room,
    al, aps, apr, axs, axr, aqs, aqr,
):
    mom, tm = lax.axis_index("mom"), lax.axis_index("tm")
    local_k = start.shape[0]
    quarter = local_k // n
    rows = PANEL // n
    width = PANEL // n
    halves = rows // SUBLANES
    half_rows = n * SUBLANES
    subs = quarter // SUBLANES
    per_half = n * subs * SPIN
    pieces = halves * per_half
    chunks = rows // CHUNK
    half_chunks = SUBLANES // CHUNK
    n_x = n // 2
    tm_x, core = tm // 2, tm % 2
    partner = {"tm": tm_x * 2 + (1 - core)}
    step_scale = 1.0 / math.sqrt(PANEL)
    lane = lax.broadcasted_iota(jnp.int32, (1, LANES), 1)
    low = lane < PANEL
    sign = jnp.where(low, -1.0, 1.0).astype(jnp.float32)
    flat = n * rows * SPIN * local_k
    flat_snd = snd.reshape(flat, LANES)
    flat_rx_g = rx_g.reshape(flat, LANES)
    flat_rx_s = rx_s.reshape(flat, LANES)
    own_first = rx_g.reshape(local_k, SPIN, halves, half_rows, LANES)
    part = out.reshape(local_k, SPIN, halves, half_rows, LANES)
    stacks = (stk_a, stk_b)
    own_last = recv.reshape(halves, local_k, SPIN, half_rows, LANES)
    near_left = mom < n // 2

    def swap(x):
        return pltpu.roll(x, PANEL, 1)

    def rot(x):
        return swap(x) * sign

    barrier = pltpu.get_barrier_semaphore()
    for o in range(1, n):
        pl.semaphore_signal(barrier, inc=1, device_id={"mom": lax.rem(mom + o, n)}, device_id_type=MESH)
    for o in range(1, n):
        pl.semaphore_signal(barrier, inc=1, device_id={"tm": lax.rem(tm + o, n)}, device_id_type=MESH)

    def remote(source, target, send, recv_sem, device):
        return pltpu.make_async_remote_copy(
            src_ref=source, dst_ref=target, send_sem=send, recv_sem=recv_sem,
            device_id=device, device_id_type=MESH)

    def local(source, target, sem):
        return pltpu.make_async_copy(source, target, sem)

    def span(q):
        return pl.ds(q * CHUNK, CHUNK)

    def forward(q, o):
        peer = lax.rem(mom + o, n)
        return remote(snd.at[peer, span(q)], recv.at[span(q), :, mom], fs.at[o], fr.at[q], {"mom": peer})

    def forward_own(q):
        return local(snd.at[mom, span(q)], recv.at[span(q), :, mom], fr.at[q])

    def panel_out(q, o):
        peer = lax.rem(tm + o, n)
        return remote(recv.at[span(q), :, :, peer], rx_g.at[tm, span(q)], gs.at[o], gr.at[q // half_chunks], {"tm": peer})

    def panel_own(q):
        return local(recv.at[span(q), :, :, tm], rx_g.at[tm, span(q)], gr.at[q // half_chunks])

    def sigma_out(n_pass, q, o):
        peer = lax.rem(tm + o, n)
        return remote(
            sig.at[span(q), :, :, peer], rx_s.at[tm, span(q)], ss.at[n_pass, o], sr.at[n_pass, q // half_chunks],
            {"tm": peer})

    def sigma_own(n_pass, q):
        return local(sig.at[span(q), :, :, tm], rx_s.at[tm, span(q)], sr.at[n_pass, q // half_chunks])

    def place(p):
        half, rest = p // per_half, p % per_half
        group, turn = rest // n, rest % n
        odd = turn % 2
        block = (1 - odd) * (n - 1 - turn // 2) + odd * (turn // 2)
        return half, group // SPIN, group % SPIN, block

    def next_out(p, o):
        half, sub, s, block = place(p)
        peer = lax.rem(tm + o, n)
        at, ks = pl.ds(half * SUBLANES, SUBLANES), pl.ds(sub * SUBLANES, SUBLANES)
        return remote(
            snd.at[peer, at, s, block, ks], recv.at[at, s, block, tm, ks], ts.at[o], tr.at[half], {"tm": peer})

    def next_own(p):
        half, sub, s, block = place(p)
        at, ks = pl.ds(half * SUBLANES, SUBLANES), pl.ds(sub * SUBLANES, SUBLANES)
        return local(snd.at[tm, at, s, block, ks], recv.at[at, s, block, tm, ks], tr.at[half])

    def window(p):
        half, sub, s, block = place(p)
        return pl.ds(block * quarter + sub * SUBLANES, SUBLANES), s, half

    def whole(ref, sem):
        return local(ref, ref, sem)

    def sent(n_pass, p):
        half, _, _, block = place(p)
        return half if n_pass == 0 else block

    def right_out(n_pass, p):
        at = window(p)
        return remote(
            rbuf.at[at], rbuf.at[at], rs.at[n_pass, sent(n_pass, p)], rr.at[p],
            {"mom": jnp.minimum(mom + 1, n - 1)})

    def left_out(n_pass, p):
        at = window(p)
        return remote(
            lbuf.at[at], lbuf.at[at], ls.at[n_pass, sent(n_pass, p)], lr.at[p],
            {"mom": jnp.maximum(mom - 1, 0)})

    class Spread:
        def __init__(self, at, source, target):
            self.at, self.source, self.target = at, source, target

        def own(self):
            return local(self.source, self.target(tm), al.at[self.at])

        def pair(self):
            return remote(self.source, self.target(tm), aps.at[self.at], apr.at[self.at], partner)

        def across(self, o):
            peer = lax.rem(tm_x + o, n_x)
            return remote(
                self.source, self.target(tm), axs.at[self.at, o - 1], axr.at[self.at, o - 1], {"tm": peer * 2 + core})

        def relay(self, o):
            held = self.target(lax.rem(tm_x + n_x - o, n_x) * 2 + core)
            return remote(held, held, aqs.at[self.at, o - 1], aqr.at[self.at, o - 1], partner)

        def begin(self):
            for o in range(1, n_x):
                self.across(o).start()
            self.pair().start()
            self.own().start()

        def pass_on(self):
            for o in range(1, n_x):
                self.across(o).wait_recv()
                self.relay(o).start()

        def arrive(self):
            self.own().wait()
            self.pair().wait_recv()
            for o in range(1, n_x):
                self.relay(o).wait_recv()
                self.relay(o).wait_send()

        def end(self):
            self.pair().wait_send()
            for o in range(1, n_x):
                self.across(o).wait_send()

    guesses = Spread(0, guess, lambda t: guess_all.at[t])
    def firsts(half, sub, s):
        return Spread(
            1 + (half * subs + sub) * SPIN + s, tot.at[0, pl.ds(sub * SUBLANES, SUBLANES), s, half],
            lambda t: own_first.at[pl.ds(t * quarter + sub * SUBLANES, SUBLANES), s, half])

    def lasts(half, sub, s):
        return Spread(
            1 + ((halves + half) * subs + sub) * SPIN + s, tot.at[1, pl.ds(sub * SUBLANES, SUBLANES), s, half],
            lambda t: own_last.at[half, pl.ds(t * quarter + sub * SUBLANES, SUBLANES), s])

    def spread_rows(target, half, s, k, parts):
        for j, value in enumerate(block_transpose(parts, lane, width)):
            at = ((j * rows + half * SUBLANES) * SPIN + s) * local_k + k
            target[pl.ds(at, SUBLANES, stride=SPIN * local_k), :] = value

    def gather_rows(source, half, s, k):
        parts = []
        for t in range(n):
            at = ((t * rows + half * SUBLANES) * SPIN + s) * local_k + k
            parts.append(source[pl.ds(at, SUBLANES, stride=SPIN * local_k), :])
        return jnp.concatenate(block_transpose(parts, lane, width), axis=0)

    def first_layout(half):
        @pl.loop(0, local_k, unroll=4)
        def _(k):
            for s in range(SPIN):
                parts = [start[k, s, half * half_rows + g * SUBLANES:half * half_rows + (g + 1) * SUBLANES, :]
                         for g in range(n)]
                spread_rows(flat_snd, half, s, k, parts)

    def keep_stack(n_pass, k, s, half, value):
        for at, piece in enumerate((value, rot(value))):
            stacks[n_pass][k, s, 0, at, half], stacks[n_pass][k, s, 1, at, half] = split(piece)

    def stack_of(n_pass, k, s):
        return tuple(stacks[n_pass][k, s, at].reshape(2 * PANEL, LANES) for at in range(2))

    def first_stack(half):
        whole(rx_g.at[:, pl.ds(half * SUBLANES, SUBLANES)], gr.at[half]).wait()

        @pl.loop(0, local_k, unroll=4)
        def _(k):
            for s in range(SPIN):
                keep_stack(0, k, s, half, gather_rows(flat_rx_g, half, s, k))

    def sigma(q):
        @pl.loop(0, CHUNK)
        def _(d):
            i = q * CHUNK + d
            both = jnp.concatenate(
                [recv[i, s].reshape(K, LANES) for s in range(SPIN)], axis=1)
            sums = dot3((fwd_split[0], fwd_split[1]), split(both))
            site, mirrored = [], []
            for s in range(SPIN):
                with_cos = sums[:K, s * LANES:(s + 1) * LANES]
                turned = rot(sums[K:, s * LANES:(s + 1) * LANES])
                site.append(with_cos + turned)
                mirrored.append(with_cos - turned)
            first, second = site
            flipped = swap(second)
            pair = (first * jnp.where(low, second, flipped)
                    + rot(first) * jnp.where(low, flipped, second)) * wvec[...]
            pair_rot = rot(pair)
            tops, bottoms = [], []
            for s in range(SPIN):
                other = mirrored[1 - s]
                flipped = swap(other)
                value = pair * jnp.where(low, other, flipped) - pair_rot * jnp.where(low, flipped, other)
                tops.append(value)
                bottoms.append(-rot(value))
            stacked = jnp.concatenate(
                [jnp.concatenate(tops, axis=1), jnp.concatenate(bottoms, axis=1)], axis=0)
            result = dot3((back_split[0], back_split[1]), split(stacked))
            for s in range(SPIN):
                sig[i, s] = result[:, s * LANES:(s + 1) * LANES].reshape(sig.shape[2:])

    def send_sigma(n_pass, q):
        for o in range(1, n):
            sigma_out(n_pass, q, o).start()
        sigma_own(n_pass, q).start()

    def wait_sigma(n_pass, half):
        whole(rx_s.at[:, pl.ds(half * SUBLANES, SUBLANES)], sr.at[n_pass, half]).wait()

    def second_sigma(q):
        half = q // half_chunks

        @pl.when(q % half_chunks == 0)
        def _():
            whole(recv.at[pl.ds(half * SUBLANES, SUBLANES)], tr.at[half]).wait()

        sigma(q)
        send_sigma(1, q)

    def convolve(n_pass, p):
        half, sub, s, block = place(p)

        @pl.when(p % per_half == 0)
        def _():
            wait_sigma(n_pass, half)

        results = []
        for m in range(SUBLANES):
            k = block * quarter + sub * SUBLANES + m
            value = split(gather_rows(flat_rx_s, half, s, k))
            results.append((k, wide(value, stack_of(n_pass, k, s), True)))
        for k, result in results:
            part[k, s, half] = result

    def each(p, body):
        half, sub, s, block = place(p)
        done = [body((block * quarter + sub * SUBLANES + m, s, half), sub * SUBLANES + m) for m in range(SUBLANES)]
        for stores in done:
            for target, at, value in stores:
                target[at] = value

    def flows(n_pass, p):
        block = place(p)[3]
        if n_pass == 0:
            yes = block >= 0
            return yes, yes, yes, yes, yes
        return block >= mom, block > mom, block <= mom, block < mom, block == mom

    def origin(n_pass, p):
        _, send_right, _, send_left, _ = flows(n_pass, p)

        @pl.when(mom == 0)
        def _():
            each(p, lambda at, m: [(rbuf, at, part[at])])

            @pl.when(send_right)
            def _():
                right_out(n_pass, p).start()

        @pl.when(mom == n - 1)
        def _():
            each(p, lambda at, m: [(lbuf, at, part[at])])

            @pl.when(send_left)
            def _():
                left_out(n_pass, p).start()

    def near_step(n_pass, p):
        from_left, send_right, from_right, send_left, _ = flows(n_pass, p)

        @pl.when(near_left & (mom > 0) & from_left)
        def _():
            right_out(n_pass, p).wait_recv()

            each(p, lambda at, m: [(rbuf, at, rbuf[at] + part[at])])

            @pl.when(send_right)
            def _():
                right_out(n_pass, p).start()

        @pl.when((mom >= n // 2) & (mom < n - 1) & from_right)
        def _():
            left_out(n_pass, p).wait_recv()

            each(p, lambda at, m: [(lbuf, at, lbuf[at] + part[at])])

            @pl.when(send_left)
            def _():
                left_out(n_pass, p).start()

    def far_step(n_pass, p):
        from_left, send_right, from_right, send_left, keep = flows(n_pass, p)

        def one(mine, other, outer, send, copy):
            copy.wait_recv()
            if n_pass == 0:
                each(p, lambda at, m: [
                    (other, at, other[at] + part[at]), (part, at, mine[at] + other[at])])
            else:
                @pl.when(send)
                def _():
                    each(p, lambda at, m: [(other, at, other[at] + part[at])])

                @pl.when(keep)
                def _():
                    each(p, lambda at, m: [(tot, (1, m) + at[1:], mine[at] + other[at])])

            @pl.when(outer & send)
            def _():
                copy.start()

        @pl.when(near_left & from_right)
        def _():
            one(rbuf, lbuf, mom > 0, send_left, left_out(n_pass, p))

        @pl.when((mom >= n // 2) & from_left)
        def _():
            one(lbuf, rbuf, mom < n - 1, send_right, right_out(n_pass, p))

    def update(p):
        half, sub, s, block = place(p)

        @pl.when(block == mom)
        def _():
            each(p, lambda at, m: [(tot, (0, m) + at[1:], part[at])])

            @pl.when(half < halves - 1)
            def _():
                firsts(half, sub, s).begin()

        results = []
        for m in range(SUBLANES):
            k = block * quarter + sub * SUBLANES + m
            old = stk_a[k, s, 0, 0, half].astype(jnp.float32) + stk_a[k, s, 1, 0, half].astype(jnp.float32)
            results.append((k, old + step_scale * wide(split(part[k, s, half]), stack_of(0, k, s))))
        for k, new in results:
            keep_stack(1, k, s, half, new)
            spread_rows(flat_snd, half, s, k, [new[g * SUBLANES:(g + 1) * SUBLANES, :] for g in range(n)])

        for o in range(1, n):
            next_out(p, o).start()
        next_own(p).start()

    def own_panel(group):
        results = []
        for m in range(SUBLANES // 2):
            k = group * (SUBLANES // 2) + m
            for s in range(SPIN):
                first = start[k, s]
                right = split(jnp.concatenate([first, rot(first)], axis=0))
                new = first + step_scale * wide(split(own_first[k, s].reshape(PANEL, LANES)), right)
                results.append((k, s, new))
        for k, s, new in results:
            own_first[k, s] = new.reshape(halves, half_rows, LANES)

    def store(sub, s):
        parts = (n, quarter, SPIN, PANEL, LANES)
        at = pl.ds(sub * SUBLANES, SUBLANES)
        return local(
            out.reshape(parts).at[:, at, s], result.reshape(parts).at[:, at, s], out_sem.at[sub * SPIN + s])

    def finish(d):
        sub, s, t = d // n // SPIN, d // n % SPIN, d % n
        is_block = chosen > 0.5

        @pl.when(t == 0)
        def _():
            for half in range(halves):
                lasts(half, sub, s).pass_on()
            for half in range(halves):
                lasts(half, sub, s).arrive()

        results = []
        for m in range(SUBLANES):
            k = t * quarter + sub * SUBLANES + m
            whole = jnp.concatenate([own_last[half, k, s] for half in range(halves)], axis=0)
            d_rows = jnp.concatenate([guess_all[at, k, s] for at in range(n)], axis=0)
            right = jnp.where(is_block, whole, own_first[k, s].reshape(PANEL, LANES))
            left = jnp.where(is_block, d_rows, whole)
            right = split(jnp.concatenate([right, rot(right)], axis=0))
            new = jnp.where(is_block, d_rows, start[k, s]) + step_scale * wide(split(left), right)
            results.append((k, new))
        for k, new in results:
            out[k, s] = new

        @pl.when(t == n - 1)
        def _():
            store(sub, s).start()

    def begin_forward(q):
        for o in range(1, n):
            forward(q, o).start()
        forward_own(q).start()

    first_layout(0)
    pl.semaphore_wait(barrier, 2 * n - 2)
    for q in range(min(AHEAD, half_chunks)):
        begin_forward(q)
    for half in range(1, halves):
        first_layout(half)

    for at, table in enumerate(tables(ordering[...])):
        fwd_split[0, at * K:(at + 1) * K, :], fwd_split[1, at * K:(at + 1) * K, :] = split(table)
        turned = split(table.T)
        back_split[0, :, at * K:(at + 1) * K], back_split[1, :, at * K:(at + 1) * K] = turned

    owners = slab_owner[...].astype(jnp.float32)
    slabs = lax.broadcasted_iota(jnp.int32, owners.shape, 1).astype(jnp.float32)
    oldest = expiring[...].astype(jnp.float32)
    mine = tm.astype(jnp.float32)
    slab_mine = jnp.sum(jnp.where(owners == mine, slabs, 0.0), axis=1, keepdims=True)
    owner_expiring = jnp.sum(jnp.where(slabs == oldest, owners, 0.0), axis=1, keepdims=True)
    position = slab_mine - oldest
    position = jnp.where(position < 0.0, position + n, position)
    held = (mom * rows + lane % rows).astype(jnp.float32)
    ahead = (n * PANEL - 1) - (position * PANEL + held)
    strength = coupling[...] * coupling[...]
    wvec[...] = strength * (jnp.exp(-1.5 * ahead / (n * PANEL)) / math.sqrt(n * PANEL))
    chosen = jnp.where(owner_expiring == mine, jnp.ones((1, LANES), jnp.float32), 0.0)

    @pl.loop(0, chunks + 1)
    def _(q):
        @pl.when(q < chunks)
        def _():
            whole(recv.at[span(q)], fr.at[q]).wait()

            @pl.when(q + AHEAD < chunks)
            def _():
                begin_forward(q + AHEAD)

            for o in range(1, n):
                panel_out(q, o).start()
            panel_own(q).start()
            sigma(q)
            send_sigma(0, q)

        for half in range(halves - 1):
            @pl.when(q == (half + 1) * half_chunks + 1)
            def _():
                first_stack(half)

        @pl.when(q == chunks)
        def _():
            first_stack(halves - 1)

    for o in range(1, n):
        whole(snd.at[0], fs.at[o]).wait()
        whole(recv.at[:, :, :, 0], gs.at[o]).wait()
        whole(sig.at[:, :, :, 0], ss.at[0, o]).wait()

    for o in range(1, n):
        pl.semaphore_signal(room, inc=1, device_id={"tm": lax.rem(tm + o, n)}, device_id_type=MESH)
    guesses.begin()

    def within(low, x, high):
        return (x >= low) & (x < high)

    lead, rest = LEAD[0], LEAD[1] + LAG
    told = lead + LAG
    first_sigma_at = told + per_half + ARRIVE
    last_sigma_at = told + pieces + SIGMA_AT
    last_at = told + per_half + ARRIVE + LAST_AT
    panel_at = last_at + (halves - 1) * (per_half + rest) + PANEL_AT
    period = per_half + rest

    def last_piece(u, body):
        seg, at = u // period, u % period

        @pl.when((u >= 0) & (seg < halves) & (at < per_half))
        def _():
            body(seg * per_half + at)

    def last_start(p):
        for half in range(halves):
            @pl.when(p == half * per_half)
            def _():
                @pl.when(mom > 0)
                def _():
                    pl.semaphore_wait(credit.at[half, 0], 1)

                @pl.when(mom < n - 1)
                def _():
                    pl.semaphore_wait(credit.at[half, 1], 1)

        convolve(1, p)
        origin(1, p)

    def last_far(p):
        far_step(1, p)
        half, sub, s, block = place(p)

        @pl.when(block == mom)
        def _():
            lasts(half, sub, s).begin()

        d = p - (pieces - per_half) - FINISH_AT

        @pl.when(d >= 0)
        def _():
            finish(d)

    def free(half):
        @pl.when(mom < n - 1)
        def _():
            whole(rbuf.at[:, :, half], rs.at[0, half]).wait()

        @pl.when(mom > 0)
        def _():
            whole(lbuf.at[:, :, half], ls.at[0, half]).wait()

        @pl.when(mom > 0)
        def _():
            pl.semaphore_signal(
                credit.at[half, 1], inc=1, device_id={"mom": jnp.maximum(mom - 1, 0)}, device_id_type=MESH)

        @pl.when(mom < n - 1)
        def _():
            pl.semaphore_signal(
                credit.at[half, 0], inc=1, device_id={"mom": jnp.minimum(mom + 1, n - 1)}, device_id_type=MESH)

    @pl.loop(0, last_at + halves * period)
    def _(t):
        @pl.when(t < pieces)
        def _():
            convolve(0, t)
            origin(0, t)

        @pl.when(within(lead, t, lead + pieces))
        def _():
            near_step(0, t - lead)

        @pl.when(within(told, t, told + pieces))
        def _():
            p = t - told
            far_step(0, p)

            @pl.when(p == 0)
            def _():
                pl.semaphore_wait(room, n - 1)

            update(p)

        for half in range(halves):
            @pl.when(t == told + (half + 1) * per_half + ARRIVE + 1)
            def _():
                free(half)

        @pl.when(t == told + per_half)
        def _():
            guesses.pass_on()

        @pl.when(within(first_sigma_at, t, first_sigma_at + (halves - 1) * half_chunks))
        def _():
            second_sigma(t - first_sigma_at)

        last_piece(t - last_at, last_start)
        last_piece(t - last_at - LEAD[1], lambda p: near_step(1, p))
        last_piece(t - last_at - rest, last_far)

        @pl.when(within(last_sigma_at, t, last_sigma_at + half_chunks // BURST))
        def _():
            @pl.loop(0, BURST)
            def _(d):
                second_sigma((halves - 1) * half_chunks + (t - last_sigma_at) * BURST + d)

        @pl.when(t == last_sigma_at + half_chunks // BURST)
        def _():
            @pl.loop(0, subs * SPIN)
            def _(d):
                firsts(halves - 1, d // SPIN, d % SPIN).begin()

        @pl.when(t == panel_at)
        def _():
            @pl.loop(0, halves * subs * SPIN)
            def _(d):
                firsts(d // (subs * SPIN), d // SPIN % subs, d % SPIN).pass_on()

            @pl.loop(0, halves * subs * SPIN)
            def _(d):
                firsts(d // (subs * SPIN), d // SPIN % subs, d % SPIN).arrive()

            guesses.arrive()

        @pl.when(within(panel_at, t, panel_at + local_k // SUBLANES))
        def _():
            own_panel(2 * (t - panel_at))
            own_panel(2 * (t - panel_at) + 1)

    @pl.loop(per_half - FINISH_AT, per_half)
    def _(d):
        finish(d)

    for block in range(n):
        ks = pl.ds(block * quarter, quarter)

        @pl.when((mom < n - 1) & (block > mom))
        def _():
            whole(rbuf.at[ks], rs.at[1, block]).wait()

        @pl.when((mom > 0) & (block < mom))
        def _():
            whole(lbuf.at[ks], ls.at[1, block]).wait()

    for o in range(1, n):
        whole(snd.at[0], ts.at[o]).wait()
        whole(sig.at[:, :, :, 0], ss.at[1, o]).wait()

    @pl.loop(0, halves * subs * SPIN)
    def _(d):
        at = d // (subs * SPIN), d // SPIN % subs, d % SPIN
        firsts(*at).end()
        lasts(*at).end()

    guesses.end()
    for sub in range(subs):
        for s in range(SPIN):
            store(sub, s).wait()


def share_step(n, start, guess, ordering, coupling, slab_owner, expiring):
    local_k = start.shape[0]
    quarter, rows = local_k // n, PANEL // n
    halves, subs = rows // SUBLANES, quarter // SUBLANES
    pieces, chunks = halves * n * subs * SPIN, rows // CHUNK
    spreads, far = 1 + 2 * halves * subs * SPIN, max(n // 2 - 1, 1)
    half_rows = n * SUBLANES
    f32, bf16 = jnp.float32, jnp.bfloat16
    dma = pltpu.SemaphoreType.DMA
    vmem = pl.BlockSpec(memory_space=pltpu.VMEM)
    moved = pltpu.VMEM((n, rows, SPIN, n, quarter, LANES), f32)
    grid = pltpu.VMEM((rows, SPIN, n, n, quarter, LANES), f32)
    square = (local_k, SPIN, halves, half_rows, LANES)
    stack = pltpu.VMEM((local_k, SPIN, 2, 2, halves, half_rows, LANES), bf16)
    return pl.pallas_call(
        functools.partial(share_kernel, n),
        out_shape=jax.ShapeDtypeStruct(start.shape, f32),
        in_specs=[vmem] * 6,
        out_specs=pl.BlockSpec(memory_space=pl.ANY),
        scratch_shapes=[
            pltpu.VMEM(start.shape, f32), dma((subs * SPIN,)),
            moved, grid, grid, moved, moved,
            stack, stack, pltpu.VMEM((1, LANES), f32),
            pltpu.VMEM(square, f32), pltpu.VMEM(square, f32),
            pltpu.VMEM((PASSES, quarter) + square[1:], f32),
            pltpu.VMEM((n,) + guess.shape, f32),
            pltpu.VMEM((2, 2 * K, K), bf16),
            pltpu.VMEM((2, K, 2 * K), bf16),
            dma((n,)), dma((chunks,)), dma((n,)), dma((halves,)),
            dma((PASSES, n)), dma((PASSES, halves)), dma((n,)), dma((halves,)),
            dma((PASSES, max(n, halves))), dma((pieces,)), dma((PASSES, max(n, halves))), dma((pieces,)),
            pltpu.SemaphoreType.REGULAR((halves, 2)), pltpu.SemaphoreType.REGULAR,
            dma((spreads,)), dma((spreads,)), dma((spreads,)),
            dma((spreads, far)), dma((spreads, far)), dma((spreads, far)), dma((spreads, far)),
        ],
        compiler_params=pltpu.CompilerParams(
            collective_id=0, has_side_effects=True, vmem_limit_bytes=63 * 1024 * 1024),
        name="share_step",
    )(start, guess, ordering, coupling, slab_owner, expiring)


def body(panel_start, block_guess, coupling, slab_owner, expiring, ordering):
    slab_count = lax.axis_size("tm")
    n_mom = lax.axis_size("mom")
    local_k = panel_start.shape[0]
    unit = SUBLANES * slab_count
    if n_mom == slab_count and local_k % unit == 0 and PANEL % unit == 0:
        return share_step(
            n_mom, panel_start, block_guess, ordering[None, :], coupling[None, :], slab_owner[None, :], expiring[None, :])
    own_index = lax.axis_index("tm")
    blocks = jnp.arange(slab_count, dtype=jnp.int32)
    slab_mine = jnp.sum(blocks * (slab_owner == own_index).astype(jnp.int32))
    position = (slab_mine - expiring[0]) % slab_count
    window = slab_count * PANEL
    times = position * PANEL + jnp.arange(PANEL, dtype=jnp.int32)
    weights = jnp.exp(-1.5 * (window - 1 - times).astype(jnp.float32) / window) / math.sqrt(window)
    strength = coupling[0] * coupling[0]
    wvec = (strength * jnp.concatenate([weights, weights]))[None, :]
    owner_expiring = jnp.sum(slab_owner * (blocks == expiring[0]).astype(jnp.int32))
    chosen = jnp.broadcast_to((own_index == owner_expiring).astype(jnp.float32), (1, LANES))
    start = panel_start.reshape(local_k, SPIN, CHUNKS, PANEL // CHUNKS, LANES)
    result = panel_step(n_mom, slab_count, start, block_guess, ordering[None, :], wvec, chosen)
    return result.reshape(panel_start.shape)


def solution(mesh):
    return jax.shard_map(
        body,
        mesh=mesh,
        in_specs=(
            P("mom", "groups", None, "tm"),
            P("mom", "groups", "tm", None),
            P("groups"),
            P("groups"),
            P("groups"),
            P(),
        ),
        out_specs=P("mom", "groups", None, "tm"),
        check_vma=False,
    )
```

```python
import functools
import math

import jax
import jax.numpy as jnp
from jax import lax
from jax.experimental import pallas as pl
from jax.experimental.pallas import tpu as pltpu
from jax.sharding import PartitionSpec as P

LSIDE = 16
K = LSIDE * LSIDE
PANEL = 64
PASSES = 2
SPIN = 2
LANES = 2 * PANEL
CHUNKS = 2
MESH = pl.DeviceIdType.MESH


def tables(ordering):
    bits = LSIDE.bit_length() - 1
    site = lax.broadcasted_iota(jnp.int32, (K, K), 0)
    phases = ((site >> bits) * (ordering >> bits) + (site & (LSIDE - 1)) * (ordering & (LSIDE - 1))) & (LSIDE - 1)
    angles = phases.astype(jnp.float32) * (2.0 * math.pi / LSIDE)
    return jnp.cos(angles) / LSIDE, jnp.sin(angles) / LSIDE


def split(x):
    high = x.astype(jnp.bfloat16)
    return high, (x - high.astype(jnp.float32)).astype(jnp.bfloat16)


def dot3(left, right, transposed=False):
    dims = (((1,), (1 if transposed else 0,)), ((), ()))

    def one(a, b):
        return lax.dot_general(a, b, dims, preferred_element_type=jnp.float32)

    return one(left[0], right[0]) + (one(left[0], right[1]) + one(left[1], right[0]))


def step_kernel(
    n_mom, n_tm, start, guess, ordering, wvec, chosen,
    out, cur, recv, sig, ret, fwd_split, back_split, stk, part, conv, pair_buf, ring_buf, guess_all,
    local_sem, guess_own, fs, fr, rs, rr, ps, pr, ss, sr, gs, gr, qs, qr, ds, dr,
):
    mom, tm = lax.axis_index("mom"), lax.axis_index("tm")
    rows, local_k = cur.shape[3], cur.shape[4]
    group = n_mom * rows
    n_x = n_tm // 2
    half = local_k // 2
    share = half // n_x
    tm_x, core = tm // 2, tm % 2
    step_scale = 1.0 / math.sqrt(PANEL)
    lane = lax.broadcasted_iota(jnp.int32, (1, LANES), 1)
    low = lane < PANEL
    sign = jnp.where(low, -1.0, 1.0).astype(jnp.float32)
    flat_cur = cur.reshape(CHUNKS * SPIN * group * local_k, LANES)
    flat_ret = ret.reshape(CHUNKS * SPIN * group * local_k, LANES)

    def swap(x):
        return pltpu.roll(x, PANEL, 1)

    def rot(x):
        return swap(x) * sign

    barrier = pltpu.get_barrier_semaphore()
    for o in range(1, n_mom):
        pl.semaphore_signal(barrier, inc=1, device_id={"mom": lax.rem(mom + o, n_mom)}, device_id_type=MESH)
    for o in range(1, n_tm):
        pl.semaphore_signal(barrier, inc=1, device_id={"tm": lax.rem(tm + o, n_tm)}, device_id_type=MESH)

    mine = pl.ds(mom * local_k, local_k)
    other_half = pl.ds((1 - core) * half, half)
    share_at = core * half + tm_x * share
    own_share = pl.ds(share_at, share)
    partner = {"tm": tm_x * 2 + (1 - core)}

    def remote(source, target, send, recv_sem, device):
        return pltpu.make_async_remote_copy(
            src_ref=source, dst_ref=target, send_sem=send, recv_sem=recv_sem,
            device_id=device, device_id_type=MESH)

    def forward(n, c, o):
        peer = lax.rem(mom + o, n_mom)
        return remote(cur.at[c, :, peer], recv.at[c, :, :, mine, :], fs.at[n, c, o], fr.at[n, c, o], {"mom": peer})

    def forward_own(n, c):
        return pltpu.make_async_copy(cur.at[c, :, mom], recv.at[c, :, :, mine, :], local_sem.at[n, c, 0])

    def back(n, c, o):
        peer = lax.rem(mom + o, n_mom)
        return remote(
            sig.at[c, :, :, pl.ds(peer * local_k, local_k), :], ret.at[c, :, mom],
            rs.at[n, c, o], rr.at[n, c, o], {"mom": peer})

    def back_own(n, c):
        return pltpu.make_async_copy(sig.at[c, :, :, mine, :], ret.at[c, :, mom], local_sem.at[n, c, 1])

    def pair_up(n, c):
        return remote(part.at[c, other_half], pair_buf.at[c], ps.at[n, c], pr.at[n, c], partner)

    def scatter(n, c, o):
        peer = lax.rem(tm_x + o, n_x)
        return remote(
            part.at[c, pl.ds(core * half + peer * share, share)], ring_buf.at[c, o - 1],
            ss.at[n, c, o], sr.at[n, c, o], {"tm": peer * 2 + core})

    def gather(n, c, o):
        peer = lax.rem(tm_x + o, n_x)
        return remote(
            conv.at[c, own_share], conv.at[c, own_share],
            gs.at[n, c, o], gr.at[n, c, o], {"tm": peer * 2 + core})

    def pair_down(n, c, o):
        held = pl.ds(core * half + lax.rem(tm_x + n_x - o, n_x) * share, share)
        return remote(conv.at[c, held], conv.at[c, held], qs.at[n, c, o], qr.at[n, c, o], partner)

    def pair_down_recv(n, c):
        for o in range(n_x):
            pair_down(n, c, o).wait_recv()

    def guess_copy(o):
        return remote(guess, guess_all.at[tm], ds.at[o], dr.at[o], {"tm": lax.rem(tm + o, n_tm)})

    def guess_local():
        return pltpu.make_async_copy(guess, guess_all.at[tm], guess_own)

    def send_forward(n, c):
        for o in range(1, n_mom):
            forward(n, c, o).start()
        forward_own(n, c).start()

    def keep_stack(n, k, s, c, value):
        turned = rot(value)
        for at, piece in ((c * group, value), (PANEL + c * group, turned)):
            high, rest = split(piece)
            stk[n, 0, k, s, at:at + group, :] = high
            stk[n, 1, k, s, at:at + group, :] = rest

    def first_layout(c):
        @pl.loop(0, local_k)
        def _(k):
            for s in range(SPIN):
                at = ((c * SPIN + s) * group) * local_k + k
                flat_cur[pl.ds(at, group, stride=local_k), :] = start[k, s, c]

    def sigma(n, c):
        for o in range(1, n_mom):
            forward(n, c, o).wait_recv()
        forward_own(n, c).wait()
        if n > 0:
            for o in range(1, n_mom):
                back(n - 1, c, o).wait_send()

        @pl.loop(0, rows)
        def _(i):
            both = jnp.concatenate([recv[c, 0, i], recv[c, 1, i]], axis=1)
            sums = dot3((fwd_split[0], fwd_split[1]), split(both))
            site, mirrored = [], []
            for s in range(SPIN):
                with_cos = sums[:K, s * LANES:(s + 1) * LANES]
                turned = rot(sums[K:, s * LANES:(s + 1) * LANES])
                site.append(with_cos + turned)
                mirrored.append(with_cos - turned)
            first, second = site
            flipped = swap(second)
            pair = (first * jnp.where(low, second, flipped)
                    + rot(first) * jnp.where(low, flipped, second)) * wvec[...]
            pair_rot = rot(pair)
            tops, bottoms = [], []
            for s in range(SPIN):
                other = mirrored[1 - s]
                flipped = swap(other)
                value = pair * jnp.where(low, other, flipped) - pair_rot * jnp.where(low, flipped, other)
                tops.append(value)
                bottoms.append(-rot(value))
            stacked = jnp.concatenate(
                [jnp.concatenate(tops, axis=1), jnp.concatenate(bottoms, axis=1)], axis=0)
            result = dot3((back_split[0], back_split[1]), split(stacked))
            for s in range(SPIN):
                sig[c, s, i] = result[:, s * LANES:(s + 1) * LANES]

        for o in range(1, n_mom):
            back(n, c, o).start()
        back_own(n, c).start()

    def convolve(n, c):
        for o in range(1, n_mom):
            back(n, c, o).wait_recv()
        back_own(n, c).wait()
        if n > 0:
            pair_up(n - 1, c).wait_send()
            for o in range(n_x):
                pair_down(n - 1, c, o).wait_send()
            for o in range(1, n_x):
                scatter(n - 1, c, o).wait_send()
                gather(n - 1, c, o).wait_send()

        def some(base):
            @pl.loop(0, half, unroll=8)
            def _(i):
                k = base + i
                for s in range(SPIN):
                    at = ((c * SPIN + s) * group) * local_k + k
                    value = split(flat_ret[pl.ds(at, group, stride=local_k), :])
                    part[c, k, s] = dot3(value, (stk[n, 0, k, s], stk[n, 1, k, s]), True)

        some((1 - core) * half)
        pair_up(n, c).start()
        some(core * half)

    def reduce(n, c):
        pair_up(n, c).wait_recv()

        @pl.loop(0, half)
        def _(i):
            part[c, core * half + i] = part[c, core * half + i] + pair_buf[c, i]

        for o in range(1, n_x):
            scatter(n, c, o).start()
        for o in range(1, n_x):
            scatter(n, c, o).wait_recv()

        @pl.loop(0, share)
        def _(i):
            total = part[c, share_at + i]
            for o in range(1, n_x):
                total = total + ring_buf[c, o - 1, i]
            conv[c, share_at + i] = total

        for o in range(1, n_x):
            gather(n, c, o).start()
        pair_down(n, c, 0).start()
        for o in range(1, n_x):
            gather(n, c, o).wait_recv()
            pair_down(n, c, o).start()

    def update(n, c):
        for o in range(1, n_mom):
            forward(n, c, o).wait_send()

        def some(base):
            @pl.loop(0, half, unroll=8)
            def _(i):
                k = base + i
                for s in range(SPIN):
                    new = start[k, s, c] + step_scale * dot3(
                        split(conv[c, k, s]), (stk[n, 0, k, s], stk[n, 1, k, s]))
                    at = ((c * SPIN + s) * group) * local_k + k
                    flat_cur[pl.ds(at, group, stride=local_k), :] = new
                    keep_stack(n + 1, k, s, c, new)

        some(core * half)
        pair_down_recv(n, c)
        some((1 - core) * half)

    def finish(n):
        is_block = chosen[...] > 0.5

        def some(base):
            @pl.loop(0, half, unroll=4)
            def _(i):
                k = base + i
                for s in range(SPIN):
                    whole = jnp.concatenate([conv[c, k, s] for c in range(CHUNKS)], axis=0)
                    d = jnp.concatenate([guess_all[t, k, s] for t in range(n_tm)], axis=0)
                    first = jnp.concatenate([start[k, s, c] for c in range(CHUNKS)], axis=0)
                    panel = stk[n, 0, k, s].astype(jnp.float32) + stk[n, 1, k, s].astype(jnp.float32)
                    right = jnp.where(is_block, jnp.concatenate([whole, rot(whole)], axis=0), panel)
                    left = jnp.where(is_block, d, whole)
                    new = jnp.where(is_block, d, first) + step_scale * dot3(split(left), split(right))
                    for c in range(CHUNKS):
                        out[k, s, c] = new[c * group:(c + 1) * group, :]

        for c in range(CHUNKS - 1):
            pair_down_recv(n, c)
        some(core * half)
        pair_down_recv(n, CHUNKS - 1)
        some((1 - core) * half)

    first_layout(0)
    pl.semaphore_wait(barrier, n_mom + n_tm - 2)
    send_forward(0, 0)
    for c in range(1, CHUNKS):
        first_layout(c)
        send_forward(0, c)
    for o in range(1, n_tm):
        guess_copy(o).start()
    guess_local().start()

    for at, table in enumerate(tables(ordering[...])):
        fwd_split[0, at * K:(at + 1) * K, :], fwd_split[1, at * K:(at + 1) * K, :] = split(table)
        turned = split(table.T)
        back_split[0, :, at * K:(at + 1) * K], back_split[1, :, at * K:(at + 1) * K] = turned

    @pl.loop(0, local_k, unroll=4)
    def _(k):
        for s in range(SPIN):
            for c in range(CHUNKS):
                keep_stack(0, k, s, c, start[k, s, c])

    for n in range(PASSES):
        for c in range(CHUNKS):
            sigma(n, c)
        for c in range(CHUNKS):
            convolve(n, c)
            reduce(n, c)
            if n < PASSES - 1:
                update(n, c)
                send_forward(n + 1, c)

    for o in range(1, n_tm):
        guess_copy(o).wait_recv()
    guess_local().wait()
    finish(PASSES - 1)

    n = PASSES - 1
    for c in range(CHUNKS):
        pair_up(n, c).wait_send()
        for o in range(n_x):
            pair_down(n, c, o).wait_send()
        for o in range(1, n_x):
            scatter(n, c, o).wait_send()
            gather(n, c, o).wait_send()
        for o in range(1, n_mom):
            forward(n, c, o).wait_send()
            back(n, c, o).wait_send()
    for o in range(1, n_tm):
        guess_copy(o).wait_send()


def panel_step(n_mom, n_tm, start, guess, ordering, wvec, chosen):
    local_k = start.shape[0]
    group = start.shape[3]
    rows = group // n_mom
    share = local_k // n_tm
    panel = (CHUNKS, SPIN, n_mom, rows, local_k, LANES)
    sites = (CHUNKS, SPIN, rows, K, LANES)
    f32, bf16 = jnp.float32, jnp.bfloat16
    dma = pltpu.SemaphoreType.DMA
    vmem = pl.BlockSpec(memory_space=pltpu.VMEM)
    one, many_mom, many_x = (PASSES, CHUNKS), (PASSES, CHUNKS, n_mom), (PASSES, CHUNKS, n_tm // 2)
    return pl.pallas_call(
        functools.partial(step_kernel, n_mom, n_tm),
        out_shape=jax.ShapeDtypeStruct(start.shape, f32),
        in_specs=[vmem] * 5,
        out_specs=vmem,
        scratch_shapes=[
            pltpu.VMEM(panel, f32),
            pltpu.VMEM(sites, f32),
            pltpu.VMEM(sites, f32),
            pltpu.VMEM(panel, f32),
            pltpu.VMEM((2, 2 * K, K), bf16),
            pltpu.VMEM((2, K, 2 * K), bf16),
            pltpu.VMEM((PASSES, 2, local_k, SPIN, LANES, LANES), bf16),
            pltpu.VMEM((CHUNKS, local_k, SPIN, group, LANES), f32),
            pltpu.VMEM((CHUNKS, local_k, SPIN, group, LANES), f32),
            pltpu.VMEM((CHUNKS, local_k // 2, SPIN, group, LANES), f32),
            pltpu.VMEM((CHUNKS, max(n_tm // 2 - 1, 1), share, SPIN, group, LANES), f32),
            pltpu.VMEM((n_tm,) + guess.shape, f32),
            dma(one + (2,)), dma,
            dma(many_mom), dma(many_mom), dma(many_mom), dma(many_mom),
            dma(one), dma(one),
            dma(many_x), dma(many_x), dma(many_x), dma(many_x),
            dma(many_x), dma(many_x),
            dma((n_tm,)), dma((n_tm,)),
        ],
        compiler_params=pltpu.CompilerParams(
            collective_id=0, has_side_effects=True, vmem_limit_bytes=63 * 1024 * 1024),
        name="panel_step",
    )(start, guess, ordering, wvec, chosen)


SUBLANES = 8
CHUNK = 1
AHEAD = 2
LAG = 2
LEAD = (4, 7)
ARRIVE = 1
FINISH_AT = 7
BURST = 4
SIGMA_AT = 3
LAST_AT = 12
PANEL_AT = 6


def wide(left, right, transposed=False):
    rows = left[0].shape[0]
    dims = (((1,), (1 if transposed else 0,)), ((), ()))
    both = lax.dot_general(
        jnp.concatenate(left, axis=0), jnp.concatenate(right, axis=0 if transposed else 1), dims,
        preferred_element_type=jnp.float32)
    return both[:rows, :LANES] + (both[:rows, LANES:] + both[rows:, :LANES])


def block_transpose(blocks, lane, width):
    blocks = list(blocks)
    bit = 1
    while bit < len(blocks):
        keep = (lane // width) % (2 * bit) < bit
        for p in range(len(blocks)):
            if p & bit == 0:
                a, b = blocks[p], blocks[p + bit]
                blocks[p] = jnp.where(keep, a, pltpu.roll(b, bit * width, 1))
                blocks[p + bit] = jnp.where(keep, pltpu.roll(a, LANES - bit * width, 1), b)
        bit *= 2
    return blocks


def share_kernel(
    n, start, guess, ordering, coupling, slab_owner, expiring,
    result, out, out_sem, snd, recv, sig, rx_g, rx_s, stk_a, stk_b, wvec, rbuf, lbuf, tot, guess_all, fwd_split, back_split,
    fs, fr, gs, gr, ss, sr, ts, tr, rs, rr, ls, lr, credit, room,
    al, aps, apr, axs, axr, aqs, aqr,
):
    mom, tm = lax.axis_index("mom"), lax.axis_index("tm")
    local_k = start.shape[0]
    quarter = local_k // n
    rows = PANEL // n
    width = PANEL // n
    halves = rows // SUBLANES
    half_rows = n * SUBLANES
    subs = quarter // SUBLANES
    per_half = n * subs * SPIN
    pieces = halves * per_half
    chunks = rows // CHUNK
    half_chunks = SUBLANES // CHUNK
    n_x = n // 2
    tm_x, core = tm // 2, tm % 2
    partner = {"tm": tm_x * 2 + (1 - core)}
    step_scale = 1.0 / math.sqrt(PANEL)
    lane = lax.broadcasted_iota(jnp.int32, (1, LANES), 1)
    low = lane < PANEL
    sign = jnp.where(low, -1.0, 1.0).astype(jnp.float32)
    flat = n * rows * SPIN * local_k
    flat_snd = snd.reshape(flat, LANES)
    flat_rx_g = rx_g.reshape(flat, LANES)
    flat_rx_s = rx_s.reshape(flat, LANES)
    own_first = rx_g.reshape(local_k, SPIN, halves, half_rows, LANES)
    part = out.reshape(local_k, SPIN, halves, half_rows, LANES)
    stacks = (stk_a, stk_b)
    own_last = recv.reshape(halves, local_k, SPIN, half_rows, LANES)
    near_left = mom < n // 2

    def swap(x):
        return pltpu.roll(x, PANEL, 1)

    def rot(x):
        return swap(x) * sign

    barrier = pltpu.get_barrier_semaphore()
    for o in range(1, n):
        pl.semaphore_signal(barrier, inc=1, device_id={"mom": lax.rem(mom + o, n)}, device_id_type=MESH)
    for o in range(1, n):
        pl.semaphore_signal(barrier, inc=1, device_id={"tm": lax.rem(tm + o, n)}, device_id_type=MESH)

    def remote(source, target, send, recv_sem, device):
        return pltpu.make_async_remote_copy(
            src_ref=source, dst_ref=target, send_sem=send, recv_sem=recv_sem,
            device_id=device, device_id_type=MESH)

    def local(source, target, sem):
        return pltpu.make_async_copy(source, target, sem)

    def span(q):
        return pl.ds(q * CHUNK, CHUNK)

    def forward(q, o):
        peer = lax.rem(mom + o, n)
        return remote(snd.at[peer, span(q)], recv.at[span(q), :, mom], fs.at[o], fr.at[q], {"mom": peer})

    def forward_own(q):
        return local(snd.at[mom, span(q)], recv.at[span(q), :, mom], fr.at[q])

    def panel_out(q, o):
        peer = lax.rem(tm + o, n)
        return remote(recv.at[span(q), :, :, peer], rx_g.at[tm, span(q)], gs.at[o], gr.at[q // half_chunks], {"tm": peer})

    def panel_own(q):
        return local(recv.at[span(q), :, :, tm], rx_g.at[tm, span(q)], gr.at[q // half_chunks])

    def sigma_out(n_pass, q, o):
        peer = lax.rem(tm + o, n)
        return remote(
            sig.at[span(q), :, :, peer], rx_s.at[tm, span(q)], ss.at[n_pass, o], sr.at[n_pass, q // half_chunks],
            {"tm": peer})

    def sigma_own(n_pass, q):
        return local(sig.at[span(q), :, :, tm], rx_s.at[tm, span(q)], sr.at[n_pass, q // half_chunks])

    def place(p):
        half, rest = p // per_half, p % per_half
        group, turn = rest // n, rest % n
        odd = turn % 2
        block = (1 - odd) * (n - 1 - turn // 2) + odd * (turn // 2)
        return half, group // SPIN, group % SPIN, block

    def next_out(p, o):
        half, sub, s, block = place(p)
        peer = lax.rem(tm + o, n)
        at, ks = pl.ds(half * SUBLANES, SUBLANES), pl.ds(sub * SUBLANES, SUBLANES)
        return remote(
            snd.at[peer, at, s, block, ks], recv.at[at, s, block, tm, ks], ts.at[o], tr.at[half], {"tm": peer})

    def next_own(p):
        half, sub, s, block = place(p)
        at, ks = pl.ds(half * SUBLANES, SUBLANES), pl.ds(sub * SUBLANES, SUBLANES)
        return local(snd.at[tm, at, s, block, ks], recv.at[at, s, block, tm, ks], tr.at[half])

    def window(p):
        half, sub, s, block = place(p)
        return pl.ds(block * quarter + sub * SUBLANES, SUBLANES), s, half

    def whole(ref, sem):
        return local(ref, ref, sem)

    def sent(n_pass, p):
        half, _, _, block = place(p)
        return half if n_pass == 0 else block

    def right_out(n_pass, p):
        at = window(p)
        return remote(
            rbuf.at[at], rbuf.at[at], rs.at[n_pass, sent(n_pass, p)], rr.at[p],
            {"mom": jnp.minimum(mom + 1, n - 1)})

    def left_out(n_pass, p):
        at = window(p)
        return remote(
            lbuf.at[at], lbuf.at[at], ls.at[n_pass, sent(n_pass, p)], lr.at[p],
            {"mom": jnp.maximum(mom - 1, 0)})

    class Spread:
        def __init__(self, at, source, target):
            self.at, self.source, self.target = at, source, target

        def own(self):
            return local(self.source, self.target(tm), al.at[self.at])

        def pair(self):
            return remote(self.source, self.target(tm), aps.at[self.at], apr.at[self.at], partner)

        def across(self, o):
            peer = lax.rem(tm_x + o, n_x)
            return remote(
                self.source, self.target(tm), axs.at[self.at, o - 1], axr.at[self.at, o - 1], {"tm": peer * 2 + core})

        def relay(self, o):
            held = self.target(lax.rem(tm_x + n_x - o, n_x) * 2 + core)
            return remote(held, held, aqs.at[self.at, o - 1], aqr.at[self.at, o - 1], partner)

        def begin(self):
            for o in range(1, n_x):
                self.across(o).start()
            self.pair().start()
            self.own().start()

        def pass_on(self):
            for o in range(1, n_x):
                self.across(o).wait_recv()
                self.relay(o).start()

        def arrive(self):
            self.own().wait()
            self.pair().wait_recv()
            for o in range(1, n_x):
                self.relay(o).wait_recv()
                self.relay(o).wait_send()

        def end(self):
            self.pair().wait_send()
            for o in range(1, n_x):
                self.across(o).wait_send()

    guesses = Spread(0, guess, lambda t: guess_all.at[t])
    def firsts(half, sub, s):
        return Spread(
            1 + (half * subs + sub) * SPIN + s, tot.at[0, pl.ds(sub * SUBLANES, SUBLANES), s, half],
            lambda t: own_first.at[pl.ds(t * quarter + sub * SUBLANES, SUBLANES), s, half])

    def lasts(half, sub, s):
        return Spread(
            1 + ((halves + half) * subs + sub) * SPIN + s, tot.at[1, pl.ds(sub * SUBLANES, SUBLANES), s, half],
            lambda t: own_last.at[half, pl.ds(t * quarter + sub * SUBLANES, SUBLANES), s])

    def spread_rows(target, half, s, k, parts):
        for j, value in enumerate(block_transpose(parts, lane, width)):
            at = ((j * rows + half * SUBLANES) * SPIN + s) * local_k + k
            target[pl.ds(at, SUBLANES, stride=SPIN * local_k), :] = value

    def gather_rows(source, half, s, k):
        parts = []
        for t in range(n):
            at = ((t * rows + half * SUBLANES) * SPIN + s) * local_k + k
            parts.append(source[pl.ds(at, SUBLANES, stride=SPIN * local_k), :])
        return jnp.concatenate(block_transpose(parts, lane, width), axis=0)

    def first_layout(half):
        @pl.loop(0, local_k, unroll=4)
        def _(k):
            for s in range(SPIN):
                parts = [start[k, s, half * half_rows + g * SUBLANES:half * half_rows + (g + 1) * SUBLANES, :]
                         for g in range(n)]
                spread_rows(flat_snd, half, s, k, parts)

    def keep_stack(n_pass, k, s, half, value):
        for at, piece in enumerate((value, rot(value))):
            stacks[n_pass][k, s, 0, at, half], stacks[n_pass][k, s, 1, at, half] = split(piece)

    def stack_of(n_pass, k, s):
        return tuple(stacks[n_pass][k, s, at].reshape(2 * PANEL, LANES) for at in range(2))

    def first_stack(half):
        whole(rx_g.at[:, pl.ds(half * SUBLANES, SUBLANES)], gr.at[half]).wait()

        @pl.loop(0, local_k, unroll=4)
        def _(k):
            for s in range(SPIN):
                keep_stack(0, k, s, half, gather_rows(flat_rx_g, half, s, k))

    def sigma(q):
        @pl.loop(0, CHUNK)
        def _(d):
            i = q * CHUNK + d
            both = jnp.concatenate(
                [recv[i, s].reshape(K, LANES) for s in range(SPIN)], axis=1)
            sums = dot3((fwd_split[0], fwd_split[1]), split(both))
            site, mirrored = [], []
            for s in range(SPIN):
                with_cos = sums[:K, s * LANES:(s + 1) * LANES]
                turned = rot(sums[K:, s * LANES:(s + 1) * LANES])
                site.append(with_cos + turned)
                mirrored.append(with_cos - turned)
            first, second = site
            flipped = swap(second)
            pair = (first * jnp.where(low, second, flipped)
                    + rot(first) * jnp.where(low, flipped, second)) * wvec[...]
            pair_rot = rot(pair)
            tops, bottoms = [], []
            for s in range(SPIN):
                other = mirrored[1 - s]
                flipped = swap(other)
                value = pair * jnp.where(low, other, flipped) - pair_rot * jnp.where(low, flipped, other)
                tops.append(value)
                bottoms.append(-rot(value))
            stacked = jnp.concatenate(
                [jnp.concatenate(tops, axis=1), jnp.concatenate(bottoms, axis=1)], axis=0)
            result = dot3((back_split[0], back_split[1]), split(stacked))
            for s in range(SPIN):
                sig[i, s] = result[:, s * LANES:(s + 1) * LANES].reshape(sig.shape[2:])

    def send_sigma(n_pass, q):
        for o in range(1, n):
            sigma_out(n_pass, q, o).start()
        sigma_own(n_pass, q).start()

    def wait_sigma(n_pass, half):
        whole(rx_s.at[:, pl.ds(half * SUBLANES, SUBLANES)], sr.at[n_pass, half]).wait()

    def second_sigma(q):
        half = q // half_chunks

        @pl.when(q == 0)
        def _():
            for o in range(1, n):
                whole(sig.at[:, :, :, 0], ss.at[0, o]).wait()

        @pl.when(q % half_chunks == 0)
        def _():
            whole(recv.at[pl.ds(half * SUBLANES, SUBLANES)], tr.at[half]).wait()

        sigma(q)
        send_sigma(1, q)

    def convolve(n_pass, p):
        half, sub, s, block = place(p)

        @pl.when(p % per_half == 0)
        def _():
            wait_sigma(n_pass, half)

        results = []
        for m in range(SUBLANES):
            k = block * quarter + sub * SUBLANES + m
            value = split(gather_rows(flat_rx_s, half, s, k))
            results.append((k, wide(value, stack_of(n_pass, k, s), True)))
        for k, result in results:
            part[k, s, half] = result

    def each(p, body):
        half, sub, s, block = place(p)
        done = [body((block * quarter + sub * SUBLANES + m, s, half), sub * SUBLANES + m) for m in range(SUBLANES)]
        for stores in done:
            for target, at, value in stores:
                target[at] = value

    def flows(n_pass, p):
        block = place(p)[3]
        if n_pass == 0:
            yes = block >= 0
            return yes, yes, yes, yes, yes
        return block >= mom, block > mom, block <= mom, block < mom, block == mom

    def origin(n_pass, p):
        _, send_right, _, send_left, _ = flows(n_pass, p)

        @pl.when(mom == 0)
        def _():
            each(p, lambda at, m: [(rbuf, at, part[at])])

            @pl.when(send_right)
            def _():
                right_out(n_pass, p).start()

        @pl.when(mom == n - 1)
        def _():
            each(p, lambda at, m: [(lbuf, at, part[at])])

            @pl.when(send_left)
            def _():
                left_out(n_pass, p).start()

    def near_step(n_pass, p):
        from_left, send_right, from_right, send_left, _ = flows(n_pass, p)

        @pl.when(near_left & (mom > 0) & from_left)
        def _():
            right_out(n_pass, p).wait_recv()

            each(p, lambda at, m: [(rbuf, at, rbuf[at] + part[at])])

            @pl.when(send_right)
            def _():
                right_out(n_pass, p).start()

        @pl.when((mom >= n // 2) & (mom < n - 1) & from_right)
        def _():
            left_out(n_pass, p).wait_recv()

            each(p, lambda at, m: [(lbuf, at, lbuf[at] + part[at])])

            @pl.when(send_left)
            def _():
                left_out(n_pass, p).start()

    def far_step(n_pass, p):
        from_left, send_right, from_right, send_left, keep = flows(n_pass, p)

        def one(mine, other, outer, send, copy):
            copy.wait_recv()
            if n_pass == 0:
                each(p, lambda at, m: [
                    (other, at, other[at] + part[at]), (part, at, mine[at] + other[at])])
            else:
                @pl.when(send)
                def _():
                    each(p, lambda at, m: [(other, at, other[at] + part[at])])

                @pl.when(keep)
                def _():
                    each(p, lambda at, m: [(tot, (1, m) + at[1:], mine[at] + other[at])])

            @pl.when(outer & send)
            def _():
                copy.start()

        @pl.when(near_left & from_right)
        def _():
            one(rbuf, lbuf, mom > 0, send_left, left_out(n_pass, p))

        @pl.when((mom >= n // 2) & from_left)
        def _():
            one(lbuf, rbuf, mom < n - 1, send_right, right_out(n_pass, p))

    def update(p):
        half, sub, s, block = place(p)

        @pl.when(block == mom)
        def _():
            each(p, lambda at, m: [(tot, (0, m) + at[1:], part[at])])

            @pl.when(half < halves - 1)
            def _():
                firsts(half, sub, s).begin()

        results = []
        for m in range(SUBLANES):
            k = block * quarter + sub * SUBLANES + m
            old = stk_a[k, s, 0, 0, half].astype(jnp.float32) + stk_a[k, s, 1, 0, half].astype(jnp.float32)
            results.append((k, old + step_scale * wide(split(part[k, s, half]), stack_of(0, k, s))))
        for k, new in results:
            keep_stack(1, k, s, half, new)
            spread_rows(flat_snd, half, s, k, [new[g * SUBLANES:(g + 1) * SUBLANES, :] for g in range(n)])

        for o in range(1, n):
            next_out(p, o).start()
        next_own(p).start()

    def own_panel(group):
        results = []
        for m in range(SUBLANES // 2):
            k = group * (SUBLANES // 2) + m
            for s in range(SPIN):
                first = start[k, s]
                right = split(jnp.concatenate([first, rot(first)], axis=0))
                new = first + step_scale * wide(split(own_first[k, s].reshape(PANEL, LANES)), right)
                results.append((k, s, new))
        for k, s, new in results:
            own_first[k, s] = new.reshape(halves, half_rows, LANES)

    def store(sub, s):
        parts = (n, quarter, SPIN, PANEL, LANES)
        at = pl.ds(sub * SUBLANES, SUBLANES)
        return local(
            out.reshape(parts).at[:, at, s], result.reshape(parts).at[:, at, s], out_sem.at[sub * SPIN + s])

    def finish(d):
        sub, s, t = d // n // SPIN, d // n % SPIN, d % n
        is_block = chosen > 0.5

        @pl.when(t == 0)
        def _():
            for half in range(halves):
                lasts(half, sub, s).pass_on()
            for half in range(halves):
                lasts(half, sub, s).arrive()

        results = []
        for m in range(SUBLANES):
            k = t * quarter + sub * SUBLANES + m
            whole = jnp.concatenate([own_last[half, k, s] for half in range(halves)], axis=0)
            d_rows = jnp.concatenate([guess_all[at, k, s] for at in range(n)], axis=0)
            right = jnp.where(is_block, whole, own_first[k, s].reshape(PANEL, LANES))
            left = jnp.where(is_block, d_rows, whole)
            right = split(jnp.concatenate([right, rot(right)], axis=0))
            new = jnp.where(is_block, d_rows, start[k, s]) + step_scale * wide(split(left), right)
            results.append((k, new))
        for k, new in results:
            out[k, s] = new

        @pl.when(t == n - 1)
        def _():
            store(sub, s).start()

    def begin_forward(q):
        for o in range(1, n):
            forward(q, o).start()
        forward_own(q).start()

    first_layout(0)
    pl.semaphore_wait(barrier, 2 * n - 2)
    for q in range(min(AHEAD, half_chunks)):
        begin_forward(q)
    for half in range(1, halves):
        first_layout(half)

    for at, table in enumerate(tables(ordering[...])):
        fwd_split[0, at * K:(at + 1) * K, :], fwd_split[1, at * K:(at + 1) * K, :] = split(table)
        turned = split(table.T)
        back_split[0, :, at * K:(at + 1) * K], back_split[1, :, at * K:(at + 1) * K] = turned

    owners = slab_owner[...].astype(jnp.float32)
    slabs = lax.broadcasted_iota(jnp.int32, owners.shape, 1).astype(jnp.float32)
    oldest = expiring[...].astype(jnp.float32)
    mine = tm.astype(jnp.float32)
    slab_mine = jnp.sum(jnp.where(owners == mine, slabs, 0.0), axis=1, keepdims=True)
    owner_expiring = jnp.sum(jnp.where(slabs == oldest, owners, 0.0), axis=1, keepdims=True)
    position = slab_mine - oldest
    position = jnp.where(position < 0.0, position + n, position)
    held = (mom * rows + lane % rows).astype(jnp.float32)
    ahead = (n * PANEL - 1) - (position * PANEL + held)
    strength = coupling[...] * coupling[...]
    wvec[...] = strength * (jnp.exp(-1.5 * ahead / (n * PANEL)) / math.sqrt(n * PANEL))
    chosen = jnp.where(owner_expiring == mine, jnp.ones((1, LANES), jnp.float32), 0.0)

    @pl.loop(0, chunks + 1)
    def _(q):
        @pl.when(q < chunks)
        def _():
            whole(recv.at[span(q)], fr.at[q]).wait()

            @pl.when(q + AHEAD < chunks)
            def _():
                begin_forward(q + AHEAD)

            for o in range(1, n):
                panel_out(q, o).start()
            panel_own(q).start()
            sigma(q)
            send_sigma(0, q)

        for half in range(halves - 1):
            @pl.when(q == (half + 1) * half_chunks + 1)
            def _():
                first_stack(half)

        @pl.when(q == chunks)
        def _():
            first_stack(halves - 1)

    for o in range(1, n):
        whole(snd.at[0], fs.at[o]).wait()
        whole(recv.at[:, :, :, 0], gs.at[o]).wait()

    for o in range(1, n):
        pl.semaphore_signal(room, inc=1, device_id={"tm": lax.rem(tm + o, n)}, device_id_type=MESH)
    guesses.begin()

    def within(low, x, high):
        return (x >= low) & (x < high)

    lead, rest = LEAD[0], LEAD[1] + LAG
    told = lead + LAG
    first_sigma_at = told + per_half + ARRIVE
    last_sigma_at = told + pieces + SIGMA_AT
    last_at = told + per_half + ARRIVE + LAST_AT
    panel_at = last_at + (halves - 1) * (per_half + rest) + PANEL_AT
    period = per_half + rest

    def last_piece(u, body):
        seg, at = u // period, u % period

        @pl.when((u >= 0) & (seg < halves) & (at < per_half))
        def _():
            body(seg * per_half + at)

    def last_start(p):
        for half in range(halves):
            @pl.when(p == half * per_half)
            def _():
                @pl.when(mom > 0)
                def _():
                    pl.semaphore_wait(credit.at[half, 0], 1)

                @pl.when(mom < n - 1)
                def _():
                    pl.semaphore_wait(credit.at[half, 1], 1)

        convolve(1, p)
        origin(1, p)

    def last_far(p):
        far_step(1, p)
        half, sub, s, block = place(p)

        @pl.when(block == mom)
        def _():
            lasts(half, sub, s).begin()

        d = p - (pieces - per_half) - FINISH_AT

        @pl.when(d >= 0)
        def _():
            finish(d)

    def free(half):
        @pl.when(mom < n - 1)
        def _():
            whole(rbuf.at[:, :, half], rs.at[0, half]).wait()

        @pl.when(mom > 0)
        def _():
            whole(lbuf.at[:, :, half], ls.at[0, half]).wait()

        @pl.when(mom > 0)
        def _():
            pl.semaphore_signal(
                credit.at[half, 1], inc=1, device_id={"mom": jnp.maximum(mom - 1, 0)}, device_id_type=MESH)

        @pl.when(mom < n - 1)
        def _():
            pl.semaphore_signal(
                credit.at[half, 0], inc=1, device_id={"mom": jnp.minimum(mom + 1, n - 1)}, device_id_type=MESH)

    @pl.loop(0, last_at + halves * period)
    def _(t):
        @pl.when(t < pieces)
        def _():
            convolve(0, t)
            origin(0, t)

        @pl.when(within(lead, t, lead + pieces))
        def _():
            near_step(0, t - lead)

        @pl.when(within(told, t, told + pieces))
        def _():
            p = t - told
            far_step(0, p)

            @pl.when(p == 0)
            def _():
                pl.semaphore_wait(room, n - 1)

            update(p)

        for half in range(halves):
            @pl.when(t == told + (half + 1) * per_half + ARRIVE + 1)
            def _():
                free(half)

        @pl.when(t == told + per_half)
        def _():
            guesses.pass_on()

        @pl.when(within(first_sigma_at, t, first_sigma_at + (halves - 1) * half_chunks))
        def _():
            second_sigma(t - first_sigma_at)

        last_piece(t - last_at, last_start)
        last_piece(t - last_at - LEAD[1], lambda p: near_step(1, p))
        last_piece(t - last_at - rest, last_far)

        @pl.when(within(last_sigma_at, t, last_sigma_at + half_chunks // BURST))
        def _():
            @pl.loop(0, BURST)
            def _(d):
                second_sigma((halves - 1) * half_chunks + (t - last_sigma_at) * BURST + d)

        @pl.when(t == last_sigma_at + half_chunks // BURST)
        def _():
            @pl.loop(0, subs * SPIN)
            def _(d):
                firsts(halves - 1, d // SPIN, d % SPIN).begin()

        @pl.when(t == panel_at)
        def _():
            @pl.loop(0, halves * subs * SPIN)
            def _(d):
                firsts(d // (subs * SPIN), d // SPIN % subs, d % SPIN).pass_on()

            @pl.loop(0, halves * subs * SPIN)
            def _(d):
                firsts(d // (subs * SPIN), d // SPIN % subs, d % SPIN).arrive()

            guesses.arrive()

        @pl.when(within(panel_at, t, panel_at + local_k // SUBLANES))
        def _():
            own_panel(2 * (t - panel_at))
            own_panel(2 * (t - panel_at) + 1)

    @pl.loop(per_half - FINISH_AT, per_half)
    def _(d):
        finish(d)

    for block in range(n):
        ks = pl.ds(block * quarter, quarter)

        @pl.when((mom < n - 1) & (block > mom))
        def _():
            whole(rbuf.at[ks], rs.at[1, block]).wait()

        @pl.when((mom > 0) & (block < mom))
        def _():
            whole(lbuf.at[ks], ls.at[1, block]).wait()

    for o in range(1, n):
        whole(snd.at[0], ts.at[o]).wait()
        whole(sig.at[:, :, :, 0], ss.at[1, o]).wait()

    @pl.loop(0, halves * subs * SPIN)
    def _(d):
        at = d // (subs * SPIN), d // SPIN % subs, d % SPIN
        firsts(*at).end()
        lasts(*at).end()

    guesses.end()
    for sub in range(subs):
        for s in range(SPIN):
            store(sub, s).wait()


def share_step(n, start, guess, ordering, coupling, slab_owner, expiring):
    local_k = start.shape[0]
    quarter, rows = local_k // n, PANEL // n
    halves, subs = rows // SUBLANES, quarter // SUBLANES
    pieces, chunks = halves * n * subs * SPIN, rows // CHUNK
    spreads, far = 1 + 2 * halves * subs * SPIN, max(n // 2 - 1, 1)
    half_rows = n * SUBLANES
    f32, bf16 = jnp.float32, jnp.bfloat16
    dma = pltpu.SemaphoreType.DMA
    vmem = pl.BlockSpec(memory_space=pltpu.VMEM)
    moved = pltpu.VMEM((n, rows, SPIN, n, quarter, LANES), f32)
    grid = pltpu.VMEM((rows, SPIN, n, n, quarter, LANES), f32)
    square = (local_k, SPIN, halves, half_rows, LANES)
    stack = pltpu.VMEM((local_k, SPIN, 2, 2, halves, half_rows, LANES), bf16)
    return pl.pallas_call(
        functools.partial(share_kernel, n),
        out_shape=jax.ShapeDtypeStruct(start.shape, f32),
        in_specs=[vmem] * 6,
        out_specs=pl.BlockSpec(memory_space=pl.ANY),
        scratch_shapes=[
            pltpu.VMEM(start.shape, f32), dma((subs * SPIN,)),
            moved, grid, grid, moved, moved,
            stack, stack, pltpu.VMEM((1, LANES), f32),
            pltpu.VMEM(square, f32), pltpu.VMEM(square, f32),
            pltpu.VMEM((PASSES, quarter) + square[1:], f32),
            pltpu.VMEM((n,) + guess.shape, f32),
            pltpu.VMEM((2, 2 * K, K), bf16),
            pltpu.VMEM((2, K, 2 * K), bf16),
            dma((n,)), dma((chunks,)), dma((n,)), dma((halves,)),
            dma((PASSES, n)), dma((PASSES, halves)), dma((n,)), dma((halves,)),
            dma((PASSES, max(n, halves))), dma((pieces,)), dma((PASSES, max(n, halves))), dma((pieces,)),
            pltpu.SemaphoreType.REGULAR((halves, 2)), pltpu.SemaphoreType.REGULAR,
            dma((spreads,)), dma((spreads,)), dma((spreads,)),
            dma((spreads, far)), dma((spreads, far)), dma((spreads, far)), dma((spreads, far)),
        ],
        compiler_params=pltpu.CompilerParams(
            collective_id=0, has_side_effects=True, vmem_limit_bytes=63 * 1024 * 1024),
        name="share_step",
    )(start, guess, ordering, coupling, slab_owner, expiring)


def body(panel_start, block_guess, coupling, slab_owner, expiring, ordering):
    slab_count = lax.axis_size("tm")
    n_mom = lax.axis_size("mom")
    local_k = panel_start.shape[0]
    unit = SUBLANES * slab_count
    if n_mom == slab_count and local_k % unit == 0 and PANEL % unit == 0:
        return share_step(
            n_mom, panel_start, block_guess, ordering[None, :], coupling[None, :], slab_owner[None, :], expiring[None, :])
    own_index = lax.axis_index("tm")
    blocks = jnp.arange(slab_count, dtype=jnp.int32)
    slab_mine = jnp.sum(blocks * (slab_owner == own_index).astype(jnp.int32))
    position = (slab_mine - expiring[0]) % slab_count
    window = slab_count * PANEL
    times = position * PANEL + jnp.arange(PANEL, dtype=jnp.int32)
    weights = jnp.exp(-1.5 * (window - 1 - times).astype(jnp.float32) / window) / math.sqrt(window)
    strength = coupling[0] * coupling[0]
    wvec = (strength * jnp.concatenate([weights, weights]))[None, :]
    owner_expiring = jnp.sum(slab_owner * (blocks == expiring[0]).astype(jnp.int32))
    chosen = jnp.broadcast_to((own_index == owner_expiring).astype(jnp.float32), (1, LANES))
    start = panel_start.reshape(local_k, SPIN, CHUNKS, PANEL // CHUNKS, LANES)
    result = panel_step(n_mom, slab_count, start, block_guess, ordering[None, :], wvec, chosen)
    return result.reshape(panel_start.shape)


def solution(mesh):
    return jax.shard_map(
        body,
        mesh=mesh,
        in_specs=(
            P("mom", "groups", None, "tm"),
            P("mom", "groups", "tm", None),
            P("groups"),
            P("groups"),
            P("groups"),
            P(),
        ),
        out_specs=P("mom", "groups", None, "tm"),
        check_vma=False,
    )
```

```python
import functools
import math

import jax
import jax.numpy as jnp
from jax import lax
from jax.experimental import pallas as pl
from jax.experimental.pallas import tpu as pltpu
from jax.sharding import PartitionSpec as P

LSIDE = 16
K = LSIDE * LSIDE
PANEL = 64
PASSES = 2
SPIN = 2
LANES = 2 * PANEL
CHUNKS = 2
MESH = pl.DeviceIdType.MESH


def tables(ordering):
    bits = LSIDE.bit_length() - 1
    site = lax.broadcasted_iota(jnp.int32, (K, K), 0)
    phases = ((site >> bits) * (ordering >> bits) + (site & (LSIDE - 1)) * (ordering & (LSIDE - 1))) & (LSIDE - 1)
    angles = phases.astype(jnp.float32) * (2.0 * math.pi / LSIDE)
    return jnp.cos(angles) / LSIDE, jnp.sin(angles) / LSIDE


def split(x):
    high = x.astype(jnp.bfloat16)
    return high, (x - high.astype(jnp.float32)).astype(jnp.bfloat16)


def dot3(left, right, transposed=False):
    dims = (((1,), (1 if transposed else 0,)), ((), ()))

    def one(a, b):
        return lax.dot_general(a, b, dims, preferred_element_type=jnp.float32)

    return one(left[0], right[0]) + (one(left[0], right[1]) + one(left[1], right[0]))


def step_kernel(
    n_mom, n_tm, start, guess, ordering, wvec, chosen,
    out, cur, recv, sig, ret, fwd_split, back_split, stk, part, conv, pair_buf, ring_buf, guess_all,
    local_sem, guess_own, fs, fr, rs, rr, ps, pr, ss, sr, gs, gr, qs, qr, ds, dr,
):
    mom, tm = lax.axis_index("mom"), lax.axis_index("tm")
    rows, local_k = cur.shape[3], cur.shape[4]
    group = n_mom * rows
    n_x = n_tm // 2
    half = local_k // 2
    share = half // n_x
    tm_x, core = tm // 2, tm % 2
    step_scale = 1.0 / math.sqrt(PANEL)
    lane = lax.broadcasted_iota(jnp.int32, (1, LANES), 1)
    low = lane < PANEL
    sign = jnp.where(low, -1.0, 1.0).astype(jnp.float32)
    flat_cur = cur.reshape(CHUNKS * SPIN * group * local_k, LANES)
    flat_ret = ret.reshape(CHUNKS * SPIN * group * local_k, LANES)

    def swap(x):
        return pltpu.roll(x, PANEL, 1)

    def rot(x):
        return swap(x) * sign

    barrier = pltpu.get_barrier_semaphore()
    for o in range(1, n_mom):
        pl.semaphore_signal(barrier, inc=1, device_id={"mom": lax.rem(mom + o, n_mom)}, device_id_type=MESH)
    for o in range(1, n_tm):
        pl.semaphore_signal(barrier, inc=1, device_id={"tm": lax.rem(tm + o, n_tm)}, device_id_type=MESH)

    mine = pl.ds(mom * local_k, local_k)
    other_half = pl.ds((1 - core) * half, half)
    share_at = core * half + tm_x * share
    own_share = pl.ds(share_at, share)
    partner = {"tm": tm_x * 2 + (1 - core)}

    def remote(source, target, send, recv_sem, device):
        return pltpu.make_async_remote_copy(
            src_ref=source, dst_ref=target, send_sem=send, recv_sem=recv_sem,
            device_id=device, device_id_type=MESH)

    def forward(n, c, o):
        peer = lax.rem(mom + o, n_mom)
        return remote(cur.at[c, :, peer], recv.at[c, :, :, mine, :], fs.at[n, c, o], fr.at[n, c, o], {"mom": peer})

    def forward_own(n, c):
        return pltpu.make_async_copy(cur.at[c, :, mom], recv.at[c, :, :, mine, :], local_sem.at[n, c, 0])

    def back(n, c, o):
        peer = lax.rem(mom + o, n_mom)
        return remote(
            sig.at[c, :, :, pl.ds(peer * local_k, local_k), :], ret.at[c, :, mom],
            rs.at[n, c, o], rr.at[n, c, o], {"mom": peer})

    def back_own(n, c):
        return pltpu.make_async_copy(sig.at[c, :, :, mine, :], ret.at[c, :, mom], local_sem.at[n, c, 1])

    def pair_up(n, c):
        return remote(part.at[c, other_half], pair_buf.at[c], ps.at[n, c], pr.at[n, c], partner)

    def scatter(n, c, o):
        peer = lax.rem(tm_x + o, n_x)
        return remote(
            part.at[c, pl.ds(core * half + peer * share, share)], ring_buf.at[c, o - 1],
            ss.at[n, c, o], sr.at[n, c, o], {"tm": peer * 2 + core})

    def gather(n, c, o):
        peer = lax.rem(tm_x + o, n_x)
        return remote(
            conv.at[c, own_share], conv.at[c, own_share],
            gs.at[n, c, o], gr.at[n, c, o], {"tm": peer * 2 + core})

    def pair_down(n, c, o):
        held = pl.ds(core * half + lax.rem(tm_x + n_x - o, n_x) * share, share)
        return remote(conv.at[c, held], conv.at[c, held], qs.at[n, c, o], qr.at[n, c, o], partner)

    def pair_down_recv(n, c):
        for o in range(n_x):
            pair_down(n, c, o).wait_recv()

    def guess_copy(o):
        return remote(guess, guess_all.at[tm], ds.at[o], dr.at[o], {"tm": lax.rem(tm + o, n_tm)})

    def guess_local():
        return pltpu.make_async_copy(guess, guess_all.at[tm], guess_own)

    def send_forward(n, c):
        for o in range(1, n_mom):
            forward(n, c, o).start()
        forward_own(n, c).start()

    def keep_stack(n, k, s, c, value):
        turned = rot(value)
        for at, piece in ((c * group, value), (PANEL + c * group, turned)):
            high, rest = split(piece)
            stk[n, 0, k, s, at:at + group, :] = high
            stk[n, 1, k, s, at:at + group, :] = rest

    def first_layout(c):
        @pl.loop(0, local_k)
        def _(k):
            for s in range(SPIN):
                at = ((c * SPIN + s) * group) * local_k + k
                flat_cur[pl.ds(at, group, stride=local_k), :] = start[k, s, c]

    def sigma(n, c):
        for o in range(1, n_mom):
            forward(n, c, o).wait_recv()
        forward_own(n, c).wait()
        if n > 0:
            for o in range(1, n_mom):
                back(n - 1, c, o).wait_send()

        @pl.loop(0, rows)
        def _(i):
            both = jnp.concatenate([recv[c, 0, i], recv[c, 1, i]], axis=1)
            sums = dot3((fwd_split[0], fwd_split[1]), split(both))
            site, mirrored = [], []
            for s in range(SPIN):
                with_cos = sums[:K, s * LANES:(s + 1) * LANES]
                turned = rot(sums[K:, s * LANES:(s + 1) * LANES])
                site.append(with_cos + turned)
                mirrored.append(with_cos - turned)
            first, second = site
            flipped = swap(second)
            pair = (first * jnp.where(low, second, flipped)
                    + rot(first) * jnp.where(low, flipped, second)) * wvec[...]
            pair_rot = rot(pair)
            tops, bottoms = [], []
            for s in range(SPIN):
                other = mirrored[1 - s]
                flipped = swap(other)
                value = pair * jnp.where(low, other, flipped) - pair_rot * jnp.where(low, flipped, other)
                tops.append(value)
                bottoms.append(-rot(value))
            stacked = jnp.concatenate(
                [jnp.concatenate(tops, axis=1), jnp.concatenate(bottoms, axis=1)], axis=0)
            result = dot3((back_split[0], back_split[1]), split(stacked))
            for s in range(SPIN):
                sig[c, s, i] = result[:, s * LANES:(s + 1) * LANES]

        for o in range(1, n_mom):
            back(n, c, o).start()
        back_own(n, c).start()

    def convolve(n, c):
        for o in range(1, n_mom):
            back(n, c, o).wait_recv()
        back_own(n, c).wait()
        if n > 0:
            pair_up(n - 1, c).wait_send()
            for o in range(n_x):
                pair_down(n - 1, c, o).wait_send()
            for o in range(1, n_x):
                scatter(n - 1, c, o).wait_send()
                gather(n - 1, c, o).wait_send()

        def some(base):
            @pl.loop(0, half, unroll=8)
            def _(i):
                k = base + i
                for s in range(SPIN):
                    at = ((c * SPIN + s) * group) * local_k + k
                    value = split(flat_ret[pl.ds(at, group, stride=local_k), :])
                    part[c, k, s] = dot3(value, (stk[n, 0, k, s], stk[n, 1, k, s]), True)

        some((1 - core) * half)
        pair_up(n, c).start()
        some(core * half)

    def reduce(n, c):
        pair_up(n, c).wait_recv()

        @pl.loop(0, half)
        def _(i):
            part[c, core * half + i] = part[c, core * half + i] + pair_buf[c, i]

        for o in range(1, n_x):
            scatter(n, c, o).start()
        for o in range(1, n_x):
            scatter(n, c, o).wait_recv()

        @pl.loop(0, share)
        def _(i):
            total = part[c, share_at + i]
            for o in range(1, n_x):
                total = total + ring_buf[c, o - 1, i]
            conv[c, share_at + i] = total

        for o in range(1, n_x):
            gather(n, c, o).start()
        pair_down(n, c, 0).start()
        for o in range(1, n_x):
            gather(n, c, o).wait_recv()
            pair_down(n, c, o).start()

    def update(n, c):
        for o in range(1, n_mom):
            forward(n, c, o).wait_send()

        def some(base):
            @pl.loop(0, half, unroll=8)
            def _(i):
                k = base + i
                for s in range(SPIN):
                    new = start[k, s, c] + step_scale * dot3(
                        split(conv[c, k, s]), (stk[n, 0, k, s], stk[n, 1, k, s]))
                    at = ((c * SPIN + s) * group) * local_k + k
                    flat_cur[pl.ds(at, group, stride=local_k), :] = new
                    keep_stack(n + 1, k, s, c, new)

        some(core * half)
        pair_down_recv(n, c)
        some((1 - core) * half)

    def finish(n):
        is_block = chosen[...] > 0.5

        def some(base):
            @pl.loop(0, half, unroll=4)
            def _(i):
                k = base + i
                for s in range(SPIN):
                    whole = jnp.concatenate([conv[c, k, s] for c in range(CHUNKS)], axis=0)
                    d = jnp.concatenate([guess_all[t, k, s] for t in range(n_tm)], axis=0)
                    first = jnp.concatenate([start[k, s, c] for c in range(CHUNKS)], axis=0)
                    panel = stk[n, 0, k, s].astype(jnp.float32) + stk[n, 1, k, s].astype(jnp.float32)
                    right = jnp.where(is_block, jnp.concatenate([whole, rot(whole)], axis=0), panel)
                    left = jnp.where(is_block, d, whole)
                    new = jnp.where(is_block, d, first) + step_scale * dot3(split(left), split(right))
                    for c in range(CHUNKS):
                        out[k, s, c] = new[c * group:(c + 1) * group, :]

        for c in range(CHUNKS - 1):
            pair_down_recv(n, c)
        some(core * half)
        pair_down_recv(n, CHUNKS - 1)
        some((1 - core) * half)

    first_layout(0)
    pl.semaphore_wait(barrier, n_mom + n_tm - 2)
    send_forward(0, 0)
    for c in range(1, CHUNKS):
        first_layout(c)
        send_forward(0, c)
    for o in range(1, n_tm):
        guess_copy(o).start()
    guess_local().start()

    for at, table in enumerate(tables(ordering[...])):
        fwd_split[0, at * K:(at + 1) * K, :], fwd_split[1, at * K:(at + 1) * K, :] = split(table)
        turned = split(table.T)
        back_split[0, :, at * K:(at + 1) * K], back_split[1, :, at * K:(at + 1) * K] = turned

    @pl.loop(0, local_k, unroll=4)
    def _(k):
        for s in range(SPIN):
            for c in range(CHUNKS):
                keep_stack(0, k, s, c, start[k, s, c])

    for n in range(PASSES):
        for c in range(CHUNKS):
            sigma(n, c)
        for c in range(CHUNKS):
            convolve(n, c)
            reduce(n, c)
            if n < PASSES - 1:
                update(n, c)
                send_forward(n + 1, c)

    for o in range(1, n_tm):
        guess_copy(o).wait_recv()
    guess_local().wait()
    finish(PASSES - 1)

    n = PASSES - 1
    for c in range(CHUNKS):
        pair_up(n, c).wait_send()
        for o in range(n_x):
            pair_down(n, c, o).wait_send()
        for o in range(1, n_x):
            scatter(n, c, o).wait_send()
            gather(n, c, o).wait_send()
        for o in range(1, n_mom):
            forward(n, c, o).wait_send()
            back(n, c, o).wait_send()
    for o in range(1, n_tm):
        guess_copy(o).wait_send()


def panel_step(n_mom, n_tm, start, guess, ordering, wvec, chosen):
    local_k = start.shape[0]
    group = start.shape[3]
    rows = group // n_mom
    share = local_k // n_tm
    panel = (CHUNKS, SPIN, n_mom, rows, local_k, LANES)
    sites = (CHUNKS, SPIN, rows, K, LANES)
    f32, bf16 = jnp.float32, jnp.bfloat16
    dma = pltpu.SemaphoreType.DMA
    vmem = pl.BlockSpec(memory_space=pltpu.VMEM)
    one, many_mom, many_x = (PASSES, CHUNKS), (PASSES, CHUNKS, n_mom), (PASSES, CHUNKS, n_tm // 2)
    return pl.pallas_call(
        functools.partial(step_kernel, n_mom, n_tm),
        out_shape=jax.ShapeDtypeStruct(start.shape, f32),
        in_specs=[vmem] * 5,
        out_specs=vmem,
        scratch_shapes=[
            pltpu.VMEM(panel, f32),
            pltpu.VMEM(sites, f32),
            pltpu.VMEM(sites, f32),
            pltpu.VMEM(panel, f32),
            pltpu.VMEM((2, 2 * K, K), bf16),
            pltpu.VMEM((2, K, 2 * K), bf16),
            pltpu.VMEM((PASSES, 2, local_k, SPIN, LANES, LANES), bf16),
            pltpu.VMEM((CHUNKS, local_k, SPIN, group, LANES), f32),
            pltpu.VMEM((CHUNKS, local_k, SPIN, group, LANES), f32),
            pltpu.VMEM((CHUNKS, local_k // 2, SPIN, group, LANES), f32),
            pltpu.VMEM((CHUNKS, max(n_tm // 2 - 1, 1), share, SPIN, group, LANES), f32),
            pltpu.VMEM((n_tm,) + guess.shape, f32),
            dma(one + (2,)), dma,
            dma(many_mom), dma(many_mom), dma(many_mom), dma(many_mom),
            dma(one), dma(one),
            dma(many_x), dma(many_x), dma(many_x), dma(many_x),
            dma(many_x), dma(many_x),
            dma((n_tm,)), dma((n_tm,)),
        ],
        compiler_params=pltpu.CompilerParams(
            collective_id=0, has_side_effects=True, vmem_limit_bytes=63 * 1024 * 1024),
        name="panel_step",
    )(start, guess, ordering, wvec, chosen)


SUBLANES = 8
CHUNK = 1
AHEAD = 2
LAG = 2
LEAD = (4, 7)
ARRIVE = 1
FINISH_AT = 7
BURST = 4
SIGMA_AT = 3
LAST_AT = 12
PANEL_AT = 6


def wide(left, right, transposed=False):
    rows = left[0].shape[0]
    dims = (((1,), (1 if transposed else 0,)), ((), ()))
    both = lax.dot_general(
        jnp.concatenate(left, axis=0), jnp.concatenate(right, axis=0 if transposed else 1), dims,
        preferred_element_type=jnp.float32)
    return both[:rows, :LANES] + (both[:rows, LANES:] + both[rows:, :LANES])


def block_transpose(blocks, lane, width):
    blocks = list(blocks)
    bit = 1
    while bit < len(blocks):
        keep = (lane // width) % (2 * bit) < bit
        for p in range(len(blocks)):
            if p & bit == 0:
                a, b = blocks[p], blocks[p + bit]
                blocks[p] = jnp.where(keep, a, pltpu.roll(b, bit * width, 1))
                blocks[p + bit] = jnp.where(keep, pltpu.roll(a, LANES - bit * width, 1), b)
        bit *= 2
    return blocks


def share_kernel(
    n, start, guess, ordering, coupling, slab_owner, expiring,
    result, out, out_sem, snd, recv, sig, rx_g, rx_s, stk_a, stk_b, wvec, rbuf, lbuf, tot, guess_all, fwd_split, back_split,
    fs, fr, gs, gr, ss, sr, ts, tr, rs, rr, ls, lr, credit, room,
    al, aps, apr, axs, axr, aqs, aqr,
):
    mom, tm = lax.axis_index("mom"), lax.axis_index("tm")
    local_k = start.shape[0]
    quarter = local_k // n
    rows = PANEL // n
    width = PANEL // n
    halves = rows // SUBLANES
    half_rows = n * SUBLANES
    subs = quarter // SUBLANES
    per_half = n * subs * SPIN
    pieces = halves * per_half
    chunks = rows // CHUNK
    half_chunks = SUBLANES // CHUNK
    n_x = n // 2
    tm_x, core = tm // 2, tm % 2
    partner = {"tm": tm_x * 2 + (1 - core)}
    step_scale = 1.0 / math.sqrt(PANEL)
    lane = lax.broadcasted_iota(jnp.int32, (1, LANES), 1)
    low = lane < PANEL
    sign = jnp.where(low, -1.0, 1.0).astype(jnp.float32)
    flat = n * rows * SPIN * local_k
    flat_snd = snd.reshape(flat, LANES)
    flat_rx_g = rx_g.reshape(flat, LANES)
    flat_rx_s = rx_s.reshape(flat, LANES)
    own_first = rx_g.reshape(local_k, SPIN, halves, half_rows, LANES)
    part = out.reshape(local_k, SPIN, halves, half_rows, LANES)
    stacks = (stk_a, stk_b)
    own_last = recv.reshape(halves, local_k, SPIN, half_rows, LANES)
    near_left = mom < n // 2

    def swap(x):
        return pltpu.roll(x, PANEL, 1)

    def rot(x):
        return swap(x) * sign

    barrier = pltpu.get_barrier_semaphore()
    for o in range(1, n):
        pl.semaphore_signal(barrier, inc=1, device_id={"mom": lax.rem(mom + o, n)}, device_id_type=MESH)
    for o in range(1, n):
        pl.semaphore_signal(barrier, inc=1, device_id={"tm": lax.rem(tm + o, n)}, device_id_type=MESH)

    def remote(source, target, send, recv_sem, device):
        return pltpu.make_async_remote_copy(
            src_ref=source, dst_ref=target, send_sem=send, recv_sem=recv_sem,
            device_id=device, device_id_type=MESH)

    def local(source, target, sem):
        return pltpu.make_async_copy(source, target, sem)

    def span(q):
        return pl.ds(q * CHUNK, CHUNK)

    def forward(q, o):
        peer = lax.rem(mom + o, n)
        return remote(snd.at[peer, span(q)], recv.at[span(q), :, mom], fs.at[o], fr.at[q], {"mom": peer})

    def forward_own(q):
        return local(snd.at[mom, span(q)], recv.at[span(q), :, mom], fr.at[q])

    def panel_out(q, o):
        peer = lax.rem(tm + o, n)
        return remote(recv.at[span(q), :, :, peer], rx_g.at[tm, span(q)], gs.at[o], gr.at[q // half_chunks], {"tm": peer})

    def panel_own(q):
        return local(recv.at[span(q), :, :, tm], rx_g.at[tm, span(q)], gr.at[q // half_chunks])

    def sigma_out(n_pass, q, o):
        peer = lax.rem(tm + o, n)
        return remote(
            sig.at[span(q), :, :, peer], rx_s.at[tm, span(q)], ss.at[n_pass, o], sr.at[n_pass, q // half_chunks],
            {"tm": peer})

    def sigma_own(n_pass, q):
        return local(sig.at[span(q), :, :, tm], rx_s.at[tm, span(q)], sr.at[n_pass, q // half_chunks])

    def place(p):
        half, rest = p // per_half, p % per_half
        group, turn = rest // n, rest % n
        odd = turn % 2
        block = (1 - odd) * (n - 1 - turn // 2) + odd * (turn // 2)
        return half, group // SPIN, group % SPIN, block

    def next_out(p, o):
        half, sub, s, block = place(p)
        peer = lax.rem(tm + o, n)
        at, ks = pl.ds(half * SUBLANES, SUBLANES), pl.ds(sub * SUBLANES, SUBLANES)
        return remote(
            snd.at[peer, at, s, block, ks], recv.at[at, s, block, tm, ks], ts.at[o], tr.at[half], {"tm": peer})

    def next_own(p):
        half, sub, s, block = place(p)
        at, ks = pl.ds(half * SUBLANES, SUBLANES), pl.ds(sub * SUBLANES, SUBLANES)
        return local(snd.at[tm, at, s, block, ks], recv.at[at, s, block, tm, ks], tr.at[half])

    def window(p):
        half, sub, s, block = place(p)
        return pl.ds(block * quarter + sub * SUBLANES, SUBLANES), s, half

    def whole(ref, sem):
        return local(ref, ref, sem)

    def sent(n_pass, p):
        half, _, _, block = place(p)
        return half if n_pass == 0 else block

    def right_out(n_pass, p):
        at = window(p)
        return remote(
            rbuf.at[at], rbuf.at[at], rs.at[n_pass, sent(n_pass, p)], rr.at[p],
            {"mom": jnp.minimum(mom + 1, n - 1)})

    def left_out(n_pass, p):
        at = window(p)
        return remote(
            lbuf.at[at], lbuf.at[at], ls.at[n_pass, sent(n_pass, p)], lr.at[p],
            {"mom": jnp.maximum(mom - 1, 0)})

    class Spread:
        def __init__(self, at, source, target):
            self.at, self.source, self.target = at, source, target

        def own(self):
            return local(self.source, self.target(tm), al.at[self.at])

        def pair(self):
            return remote(self.source, self.target(tm), aps.at[self.at], apr.at[self.at], partner)

        def across(self, o):
            peer = lax.rem(tm_x + o, n_x)
            return remote(
                self.source, self.target(tm), axs.at[self.at, o - 1], axr.at[self.at, o - 1], {"tm": peer * 2 + core})

        def relay(self, o):
            held = self.target(lax.rem(tm_x + n_x - o, n_x) * 2 + core)
            return remote(held, held, aqs.at[self.at, o - 1], aqr.at[self.at, o - 1], partner)

        def begin(self):
            for o in range(1, n_x):
                self.across(o).start()
            self.pair().start()
            self.own().start()

        def pass_on(self):
            for o in range(1, n_x):
                self.across(o).wait_recv()
                self.relay(o).start()

        def arrive(self):
            self.own().wait()
            self.pair().wait_recv()
            for o in range(1, n_x):
                self.relay(o).wait_recv()
                self.relay(o).wait_send()

        def end(self):
            self.pair().wait_send()
            for o in range(1, n_x):
                self.across(o).wait_send()

    guesses = Spread(0, guess, lambda t: guess_all.at[t])
    def firsts(half, sub, s):
        return Spread(
            1 + (half * subs + sub) * SPIN + s, tot.at[0, pl.ds(sub * SUBLANES, SUBLANES), s, half],
            lambda t: own_first.at[pl.ds(t * quarter + sub * SUBLANES, SUBLANES), s, half])

    def lasts(half, sub, s):
        return Spread(
            1 + ((halves + half) * subs + sub) * SPIN + s, tot.at[1, pl.ds(sub * SUBLANES, SUBLANES), s, half],
            lambda t: own_last.at[half, pl.ds(t * quarter + sub * SUBLANES, SUBLANES), s])

    def spread_rows(target, half, s, k, parts):
        for j, value in enumerate(block_transpose(parts, lane, width)):
            at = ((j * rows + half * SUBLANES) * SPIN + s) * local_k + k
            target[pl.ds(at, SUBLANES, stride=SPIN * local_k), :] = value

    def gather_rows(source, half, s, k):
        parts = []
        for t in range(n):
            at = ((t * rows + half * SUBLANES) * SPIN + s) * local_k + k
            parts.append(source[pl.ds(at, SUBLANES, stride=SPIN * local_k), :])
        return jnp.concatenate(block_transpose(parts, lane, width), axis=0)

    def first_layout(half):
        @pl.loop(0, local_k, unroll=8)
        def _(k):
            for s in range(SPIN):
                parts = [start[k, s, half * half_rows + g * SUBLANES:half * half_rows + (g + 1) * SUBLANES, :]
                         for g in range(n)]
                spread_rows(flat_snd, half, s, k, parts)

    def keep_stack(n_pass, k, s, half, value):
        for at, piece in enumerate((value, rot(value))):
            stacks[n_pass][k, s, 0, at, half], stacks[n_pass][k, s, 1, at, half] = split(piece)

    def stack_of(n_pass, k, s):
        return tuple(stacks[n_pass][k, s, at].reshape(2 * PANEL, LANES) for at in range(2))

    def first_stack(half):
        whole(rx_g.at[:, pl.ds(half * SUBLANES, SUBLANES)], gr.at[half]).wait()

        @pl.loop(0, local_k, unroll=4)
        def _(k):
            for s in range(SPIN):
                keep_stack(0, k, s, half, gather_rows(flat_rx_g, half, s, k))

    def sigma(q):
        @pl.loop(0, CHUNK)
        def _(d):
            i = q * CHUNK + d
            both = jnp.concatenate(
                [recv[i, s].reshape(K, LANES) for s in range(SPIN)], axis=1)
            sums = dot3((fwd_split[0], fwd_split[1]), split(both))
            site, mirrored = [], []
            for s in range(SPIN):
                with_cos = sums[:K, s * LANES:(s + 1) * LANES]
                turned = rot(sums[K:, s * LANES:(s + 1) * LANES])
                site.append(with_cos + turned)
                mirrored.append(with_cos - turned)
            first, second = site
            flipped = swap(second)
            pair = (first * jnp.where(low, second, flipped)
                    + rot(first) * jnp.where(low, flipped, second)) * wvec[...]
            pair_rot = rot(pair)
            tops, bottoms = [], []
            for s in range(SPIN):
                other = mirrored[1 - s]
                flipped = swap(other)
                value = pair * jnp.where(low, other, flipped) - pair_rot * jnp.where(low, flipped, other)
                tops.append(value)
                bottoms.append(-rot(value))
            stacked = jnp.concatenate(
                [jnp.concatenate(tops, axis=1), jnp.concatenate(bottoms, axis=1)], axis=0)
            result = dot3((back_split[0], back_split[1]), split(stacked))
            for s in range(SPIN):
                sig[i, s] = result[:, s * LANES:(s + 1) * LANES].reshape(sig.shape[2:])

    def send_sigma(n_pass, q):
        for o in range(1, n):
            sigma_out(n_pass, q, o).start()
        sigma_own(n_pass, q).start()

    def wait_sigma(n_pass, half):
        whole(rx_s.at[:, pl.ds(half * SUBLANES, SUBLANES)], sr.at[n_pass, half]).wait()

    def second_sigma(q):
        half = q // half_chunks

        @pl.when(q == 0)
        def _():
            for o in range(1, n):
                whole(sig.at[:, :, :, 0], ss.at[0, o]).wait()

        @pl.when(q % half_chunks == 0)
        def _():
            whole(recv.at[pl.ds(half * SUBLANES, SUBLANES)], tr.at[half]).wait()

        sigma(q)
        send_sigma(1, q)

    def convolve(n_pass, p):
        half, sub, s, block = place(p)

        @pl.when(p % per_half == 0)
        def _():
            wait_sigma(n_pass, half)

        results = []
        for m in range(SUBLANES):
            k = block * quarter + sub * SUBLANES + m
            value = split(gather_rows(flat_rx_s, half, s, k))
            results.append((k, wide(value, stack_of(n_pass, k, s), True)))
        for k, result in results:
            part[k, s, half] = result

    def each(p, body):
        half, sub, s, block = place(p)
        done = [body((block * quarter + sub * SUBLANES + m, s, half), sub * SUBLANES + m) for m in range(SUBLANES)]
        for stores in done:
            for target, at, value in stores:
                target[at] = value

    def flows(n_pass, p):
        block = place(p)[3]
        if n_pass == 0:
            yes = block >= 0
            return yes, yes, yes, yes, yes
        return block >= mom, block > mom, block <= mom, block < mom, block == mom

    def origin(n_pass, p):
        _, send_right, _, send_left, _ = flows(n_pass, p)

        @pl.when(mom == 0)
        def _():
            each(p, lambda at, m: [(rbuf, at, part[at])])

            @pl.when(send_right)
            def _():
                right_out(n_pass, p).start()

        @pl.when(mom == n - 1)
        def _():
            each(p, lambda at, m: [(lbuf, at, part[at])])

            @pl.when(send_left)
            def _():
                left_out(n_pass, p).start()

    def near_step(n_pass, p):
        from_left, send_right, from_right, send_left, _ = flows(n_pass, p)

        @pl.when(near_left & (mom > 0) & from_left)
        def _():
            right_out(n_pass, p).wait_recv()

            each(p, lambda at, m: [(rbuf, at, rbuf[at] + part[at])])

            @pl.when(send_right)
            def _():
                right_out(n_pass, p).start()

        @pl.when((mom >= n // 2) & (mom < n - 1) & from_right)
        def _():
            left_out(n_pass, p).wait_recv()

            each(p, lambda at, m: [(lbuf, at, lbuf[at] + part[at])])

            @pl.when(send_left)
            def _():
                left_out(n_pass, p).start()

    def far_step(n_pass, p):
        from_left, send_right, from_right, send_left, keep = flows(n_pass, p)

        def one(mine, other, outer, send, copy):
            copy.wait_recv()
            if n_pass == 0:
                each(p, lambda at, m: [
                    (other, at, other[at] + part[at]), (part, at, mine[at] + other[at])])
            else:
                @pl.when(send)
                def _():
                    each(p, lambda at, m: [(other, at, other[at] + part[at])])

                @pl.when(keep)
                def _():
                    each(p, lambda at, m: [(tot, (1, m) + at[1:], mine[at] + other[at])])

            @pl.when(outer & send)
            def _():
                copy.start()

        @pl.when(near_left & from_right)
        def _():
            one(rbuf, lbuf, mom > 0, send_left, left_out(n_pass, p))

        @pl.when((mom >= n // 2) & from_left)
        def _():
            one(lbuf, rbuf, mom < n - 1, send_right, right_out(n_pass, p))

    def update(p):
        half, sub, s, block = place(p)

        @pl.when(block == mom)
        def _():
            each(p, lambda at, m: [(tot, (0, m) + at[1:], part[at])])

            @pl.when(half < halves - 1)
            def _():
                firsts(half, sub, s).begin()

        results = []
        for m in range(SUBLANES):
            k = block * quarter + sub * SUBLANES + m
            old = stk_a[k, s, 0, 0, half].astype(jnp.float32) + stk_a[k, s, 1, 0, half].astype(jnp.float32)
            results.append((k, old + step_scale * wide(split(part[k, s, half]), stack_of(0, k, s))))
        for k, new in results:
            keep_stack(1, k, s, half, new)
            spread_rows(flat_snd, half, s, k, [new[g * SUBLANES:(g + 1) * SUBLANES, :] for g in range(n)])

        for o in range(1, n):
            next_out(p, o).start()
        next_own(p).start()

    def own_panel(group):
        results = []
        for m in range(SUBLANES // 2):
            k = group * (SUBLANES // 2) + m
            for s in range(SPIN):
                first = start[k, s]
                right = split(jnp.concatenate([first, rot(first)], axis=0))
                new = first + step_scale * wide(split(own_first[k, s].reshape(PANEL, LANES)), right)
                results.append((k, s, new))
        for k, s, new in results:
            own_first[k, s] = new.reshape(halves, half_rows, LANES)

    def store(sub, s):
        parts = (n, quarter, SPIN, PANEL, LANES)
        at = pl.ds(sub * SUBLANES, SUBLANES)
        return local(
            out.reshape(parts).at[:, at, s], result.reshape(parts).at[:, at, s], out_sem.at[sub * SPIN + s])

    def finish(d):
        sub, s, t = d // n // SPIN, d // n % SPIN, d % n
        is_block = chosen > 0.5

        @pl.when(t == 0)
        def _():
            for half in range(halves):
                lasts(half, sub, s).pass_on()
            for half in range(halves):
                lasts(half, sub, s).arrive()

        results = []
        for m in range(SUBLANES):
            k = t * quarter + sub * SUBLANES + m
            whole = jnp.concatenate([own_last[half, k, s] for half in range(halves)], axis=0)
            d_rows = jnp.concatenate([guess_all[at, k, s] for at in range(n)], axis=0)
            right = jnp.where(is_block, whole, own_first[k, s].reshape(PANEL, LANES))
            left = jnp.where(is_block, d_rows, whole)
            right = split(jnp.concatenate([right, rot(right)], axis=0))
            new = jnp.where(is_block, d_rows, start[k, s]) + step_scale * wide(split(left), right)
            results.append((k, new))
        for k, new in results:
            out[k, s] = new

        @pl.when(t == n - 1)
        def _():
            store(sub, s).start()

    def begin_forward(q):
        for o in range(1, n):
            forward(q, o).start()
        forward_own(q).start()

    first_layout(0)
    pl.semaphore_wait(barrier, 2 * n - 2)
    for q in range(min(AHEAD, half_chunks)):
        begin_forward(q)
    for half in range(1, halves):
        first_layout(half)

    for at, table in enumerate(tables(ordering[...])):
        fwd_split[0, at * K:(at + 1) * K, :], fwd_split[1, at * K:(at + 1) * K, :] = split(table)
        turned = split(table.T)
        back_split[0, :, at * K:(at + 1) * K], back_split[1, :, at * K:(at + 1) * K] = turned

    owners = slab_owner[...].astype(jnp.float32)
    slabs = lax.broadcasted_iota(jnp.int32, owners.shape, 1).astype(jnp.float32)
    oldest = expiring[...].astype(jnp.float32)
    mine = tm.astype(jnp.float32)
    slab_mine = jnp.sum(jnp.where(owners == mine, slabs, 0.0), axis=1, keepdims=True)
    owner_expiring = jnp.sum(jnp.where(slabs == oldest, owners, 0.0), axis=1, keepdims=True)
    position = slab_mine - oldest
    position = jnp.where(position < 0.0, position + n, position)
    held = (mom * rows + lane % rows).astype(jnp.float32)
    ahead = (n * PANEL - 1) - (position * PANEL + held)
    strength = coupling[...] * coupling[...]
    wvec[...] = strength * (jnp.exp(-1.5 * ahead / (n * PANEL)) / math.sqrt(n * PANEL))
    chosen = jnp.where(owner_expiring == mine, jnp.ones((1, LANES), jnp.float32), 0.0)

    @pl.loop(0, chunks + 1)
    def _(q):
        @pl.when(q < chunks)
        def _():
            whole(recv.at[span(q)], fr.at[q]).wait()

            @pl.when(q + AHEAD < chunks)
            def _():
                begin_forward(q + AHEAD)

            for o in range(1, n):
                panel_out(q, o).start()
            panel_own(q).start()
            sigma(q)
            send_sigma(0, q)

        for half in range(halves - 1):
            @pl.when(q == (half + 1) * half_chunks + 1)
            def _():
                first_stack(half)

        @pl.when(q == chunks)
        def _():
            first_stack(halves - 1)

    for o in range(1, n):
        whole(snd.at[0], fs.at[o]).wait()
        whole(recv.at[:, :, :, 0], gs.at[o]).wait()

    for o in range(1, n):
        pl.semaphore_signal(room, inc=1, device_id={"tm": lax.rem(tm + o, n)}, device_id_type=MESH)
    guesses.begin()

    def within(low, x, high):
        return (x >= low) & (x < high)

    lead, rest = LEAD[0], LEAD[1] + LAG
    told = lead + LAG
    first_sigma_at = told + per_half + ARRIVE
    last_sigma_at = told + pieces + SIGMA_AT
    last_at = told + per_half + ARRIVE + LAST_AT
    panel_at = last_at + (halves - 1) * (per_half + rest) + PANEL_AT
    period = per_half + rest

    def last_piece(u, body):
        seg, at = u // period, u % period

        @pl.when((u >= 0) & (seg < halves) & (at < per_half))
        def _():
            body(seg * per_half + at)

    def last_start(p):
        for half in range(halves):
            @pl.when(p == half * per_half)
            def _():
                @pl.when(mom > 0)
                def _():
                    pl.semaphore_wait(credit.at[half, 0], 1)

                @pl.when(mom < n - 1)
                def _():
                    pl.semaphore_wait(credit.at[half, 1], 1)

        convolve(1, p)
        origin(1, p)

    def last_far(p):
        far_step(1, p)
        half, sub, s, block = place(p)

        @pl.when(block == mom)
        def _():
            lasts(half, sub, s).begin()

        d = p - (pieces - per_half) - FINISH_AT

        @pl.when(d >= 0)
        def _():
            finish(d)

    def free(half):
        @pl.when(mom < n - 1)
        def _():
            whole(rbuf.at[:, :, half], rs.at[0, half]).wait()

        @pl.when(mom > 0)
        def _():
            whole(lbuf.at[:, :, half], ls.at[0, half]).wait()

        @pl.when(mom > 0)
        def _():
            pl.semaphore_signal(
                credit.at[half, 1], inc=1, device_id={"mom": jnp.maximum(mom - 1, 0)}, device_id_type=MESH)

        @pl.when(mom < n - 1)
        def _():
            pl.semaphore_signal(
                credit.at[half, 0], inc=1, device_id={"mom": jnp.minimum(mom + 1, n - 1)}, device_id_type=MESH)

    @pl.loop(0, last_at + halves * period)
    def _(t):
        @pl.when(t < pieces)
        def _():
            convolve(0, t)
            origin(0, t)

        @pl.when(within(lead, t, lead + pieces))
        def _():
            near_step(0, t - lead)

        @pl.when(within(told, t, told + pieces))
        def _():
            p = t - told
            far_step(0, p)

            @pl.when(p == 0)
            def _():
                pl.semaphore_wait(room, n - 1)

            update(p)

        for half in range(halves):
            @pl.when(t == told + (half + 1) * per_half + ARRIVE + 1)
            def _():
                free(half)

        @pl.when(t == told + per_half)
        def _():
            guesses.pass_on()

        @pl.when(within(first_sigma_at, t, first_sigma_at + (halves - 1) * half_chunks))
        def _():
            second_sigma(t - first_sigma_at)

        last_piece(t - last_at, last_start)
        last_piece(t - last_at - LEAD[1], lambda p: near_step(1, p))
        last_piece(t - last_at - rest, last_far)

        @pl.when(within(last_sigma_at, t, last_sigma_at + half_chunks // BURST))
        def _():
            @pl.loop(0, BURST)
            def _(d):
                second_sigma((halves - 1) * half_chunks + (t - last_sigma_at) * BURST + d)

        @pl.when(t == last_sigma_at + half_chunks // BURST)
        def _():
            @pl.loop(0, subs * SPIN)
            def _(d):
                firsts(halves - 1, d // SPIN, d % SPIN).begin()

        @pl.when(t == panel_at)
        def _():
            @pl.loop(0, halves * subs * SPIN)
            def _(d):
                firsts(d // (subs * SPIN), d // SPIN % subs, d % SPIN).pass_on()

            @pl.loop(0, halves * subs * SPIN)
            def _(d):
                firsts(d // (subs * SPIN), d // SPIN % subs, d % SPIN).arrive()

            guesses.arrive()

        @pl.when(within(panel_at, t, panel_at + local_k // SUBLANES))
        def _():
            own_panel(2 * (t - panel_at))
            own_panel(2 * (t - panel_at) + 1)

    @pl.loop(per_half - FINISH_AT, per_half)
    def _(d):
        finish(d)

    for block in range(n):
        ks = pl.ds(block * quarter, quarter)

        @pl.when((mom < n - 1) & (block > mom))
        def _():
            whole(rbuf.at[ks], rs.at[1, block]).wait()

        @pl.when((mom > 0) & (block < mom))
        def _():
            whole(lbuf.at[ks], ls.at[1, block]).wait()

    for o in range(1, n):
        whole(snd.at[0], ts.at[o]).wait()
        whole(sig.at[:, :, :, 0], ss.at[1, o]).wait()

    @pl.loop(0, halves * subs * SPIN)
    def _(d):
        at = d // (subs * SPIN), d // SPIN % subs, d % SPIN
        firsts(*at).end()
        lasts(*at).end()

    guesses.end()
    for sub in range(subs):
        for s in range(SPIN):
            store(sub, s).wait()


def share_step(n, start, guess, ordering, coupling, slab_owner, expiring):
    local_k = start.shape[0]
    quarter, rows = local_k // n, PANEL // n
    halves, subs = rows // SUBLANES, quarter // SUBLANES
    pieces, chunks = halves * n * subs * SPIN, rows // CHUNK
    spreads, far = 1 + 2 * halves * subs * SPIN, max(n // 2 - 1, 1)
    half_rows = n * SUBLANES
    f32, bf16 = jnp.float32, jnp.bfloat16
    dma = pltpu.SemaphoreType.DMA
    vmem = pl.BlockSpec(memory_space=pltpu.VMEM)
    moved = pltpu.VMEM((n, rows, SPIN, n, quarter, LANES), f32)
    grid = pltpu.VMEM((rows, SPIN, n, n, quarter, LANES), f32)
    square = (local_k, SPIN, halves, half_rows, LANES)
    stack = pltpu.VMEM((local_k, SPIN, 2, 2, halves, half_rows, LANES), bf16)
    return pl.pallas_call(
        functools.partial(share_kernel, n),
        out_shape=jax.ShapeDtypeStruct(start.shape, f32),
        in_specs=[vmem, pl.BlockSpec(memory_space=pl.ANY)] + [vmem] * 4,
        out_specs=pl.BlockSpec(memory_space=pl.ANY),
        scratch_shapes=[
            pltpu.VMEM(start.shape, f32), dma((subs * SPIN,)),
            moved, grid, grid, moved, moved,
            stack, stack, pltpu.VMEM((1, LANES), f32),
            pltpu.VMEM(square, f32), pltpu.VMEM(square, f32),
            pltpu.VMEM((PASSES, quarter) + square[1:], f32),
            pltpu.VMEM((n,) + guess.shape, f32),
            pltpu.VMEM((2, 2 * K, K), bf16),
            pltpu.VMEM((2, K, 2 * K), bf16),
            dma((n,)), dma((chunks,)), dma((n,)), dma((halves,)),
            dma((PASSES, n)), dma((PASSES, halves)), dma((n,)), dma((halves,)),
            dma((PASSES, max(n, halves))), dma((pieces,)), dma((PASSES, max(n, halves))), dma((pieces,)),
            pltpu.SemaphoreType.REGULAR((halves, 2)), pltpu.SemaphoreType.REGULAR,
            dma((spreads,)), dma((spreads,)), dma((spreads,)),
            dma((spreads, far)), dma((spreads, far)), dma((spreads, far)), dma((spreads, far)),
        ],
        compiler_params=pltpu.CompilerParams(
            collective_id=0, has_side_effects=True, vmem_limit_bytes=63 * 1024 * 1024),
        name="share_step",
    )(start, guess, ordering, coupling, slab_owner, expiring)


def body(panel_start, block_guess, coupling, slab_owner, expiring, ordering):
    slab_count = lax.axis_size("tm")
    n_mom = lax.axis_size("mom")
    local_k = panel_start.shape[0]
    unit = SUBLANES * slab_count
    if n_mom == slab_count and local_k % unit == 0 and PANEL % unit == 0:
        return share_step(
            n_mom, panel_start, block_guess, ordering[None, :], coupling[None, :], slab_owner[None, :], expiring[None, :])
    own_index = lax.axis_index("tm")
    blocks = jnp.arange(slab_count, dtype=jnp.int32)
    slab_mine = jnp.sum(blocks * (slab_owner == own_index).astype(jnp.int32))
    position = (slab_mine - expiring[0]) % slab_count
    window = slab_count * PANEL
    times = position * PANEL + jnp.arange(PANEL, dtype=jnp.int32)
    weights = jnp.exp(-1.5 * (window - 1 - times).astype(jnp.float32) / window) / math.sqrt(window)
    strength = coupling[0] * coupling[0]
    wvec = (strength * jnp.concatenate([weights, weights]))[None, :]
    owner_expiring = jnp.sum(slab_owner * (blocks == expiring[0]).astype(jnp.int32))
    chosen = jnp.broadcast_to((own_index == owner_expiring).astype(jnp.float32), (1, LANES))
    start = panel_start.reshape(local_k, SPIN, CHUNKS, PANEL // CHUNKS, LANES)
    result = panel_step(n_mom, slab_count, start, block_guess, ordering[None, :], wvec, chosen)
    return result.reshape(panel_start.shape)


def solution(mesh):
    return jax.shard_map(
        body,
        mesh=mesh,
        in_specs=(
            P("mom", "groups", None, "tm"),
            P("mom", "groups", "tm", None),
            P("groups"),
            P("groups"),
            P("groups"),
            P(),
        ),
        out_specs=P("mom", "groups", None, "tm"),
        check_vma=False,
    )
```

```python
import functools
import math

import jax
import jax.numpy as jnp
from jax import lax
from jax.experimental import pallas as pl
from jax.experimental.pallas import tpu as pltpu
from jax.sharding import PartitionSpec as P

LSIDE = 16
K = LSIDE * LSIDE
PANEL = 64
PASSES = 2
SPIN = 2
LANES = 2 * PANEL
CHUNKS = 2
MESH = pl.DeviceIdType.MESH


def tables(ordering):
    bits = LSIDE.bit_length() - 1
    site = lax.broadcasted_iota(jnp.int32, (K, K), 0)
    phases = ((site >> bits) * (ordering >> bits) + (site & (LSIDE - 1)) * (ordering & (LSIDE - 1))) & (LSIDE - 1)
    angles = phases.astype(jnp.float32) * (2.0 * math.pi / LSIDE)
    return jnp.cos(angles) / LSIDE, jnp.sin(angles) / LSIDE


def split(x):
    high = x.astype(jnp.bfloat16)
    return high, (x - high.astype(jnp.float32)).astype(jnp.bfloat16)


def dot3(left, right, transposed=False):
    dims = (((1,), (1 if transposed else 0,)), ((), ()))

    def one(a, b):
        return lax.dot_general(a, b, dims, preferred_element_type=jnp.float32)

    return one(left[0], right[0]) + (one(left[0], right[1]) + one(left[1], right[0]))


def step_kernel(
    n_mom, n_tm, start, guess, ordering, wvec, chosen,
    out, cur, recv, sig, ret, fwd_split, back_split, stk, part, conv, pair_buf, ring_buf, guess_all,
    local_sem, guess_own, fs, fr, rs, rr, ps, pr, ss, sr, gs, gr, qs, qr, ds, dr,
):
    mom, tm = lax.axis_index("mom"), lax.axis_index("tm")
    rows, local_k = cur.shape[3], cur.shape[4]
    group = n_mom * rows
    n_x = n_tm // 2
    half = local_k // 2
    share = half // n_x
    tm_x, core = tm // 2, tm % 2
    step_scale = 1.0 / math.sqrt(PANEL)
    lane = lax.broadcasted_iota(jnp.int32, (1, LANES), 1)
    low = lane < PANEL
    sign = jnp.where(low, -1.0, 1.0).astype(jnp.float32)
    flat_cur = cur.reshape(CHUNKS * SPIN * group * local_k, LANES)
    flat_ret = ret.reshape(CHUNKS * SPIN * group * local_k, LANES)

    def swap(x):
        return pltpu.roll(x, PANEL, 1)

    def rot(x):
        return swap(x) * sign

    barrier = pltpu.get_barrier_semaphore()
    for o in range(1, n_mom):
        pl.semaphore_signal(barrier, inc=1, device_id={"mom": lax.rem(mom + o, n_mom)}, device_id_type=MESH)
    for o in range(1, n_tm):
        pl.semaphore_signal(barrier, inc=1, device_id={"tm": lax.rem(tm + o, n_tm)}, device_id_type=MESH)

    mine = pl.ds(mom * local_k, local_k)
    other_half = pl.ds((1 - core) * half, half)
    share_at = core * half + tm_x * share
    own_share = pl.ds(share_at, share)
    partner = {"tm": tm_x * 2 + (1 - core)}

    def remote(source, target, send, recv_sem, device):
        return pltpu.make_async_remote_copy(
            src_ref=source, dst_ref=target, send_sem=send, recv_sem=recv_sem,
            device_id=device, device_id_type=MESH)

    def forward(n, c, o):
        peer = lax.rem(mom + o, n_mom)
        return remote(cur.at[c, :, peer], recv.at[c, :, :, mine, :], fs.at[n, c, o], fr.at[n, c, o], {"mom": peer})

    def forward_own(n, c):
        return pltpu.make_async_copy(cur.at[c, :, mom], recv.at[c, :, :, mine, :], local_sem.at[n, c, 0])

    def back(n, c, o):
        peer = lax.rem(mom + o, n_mom)
        return remote(
            sig.at[c, :, :, pl.ds(peer * local_k, local_k), :], ret.at[c, :, mom],
            rs.at[n, c, o], rr.at[n, c, o], {"mom": peer})

    def back_own(n, c):
        return pltpu.make_async_copy(sig.at[c, :, :, mine, :], ret.at[c, :, mom], local_sem.at[n, c, 1])

    def pair_up(n, c):
        return remote(part.at[c, other_half], pair_buf.at[c], ps.at[n, c], pr.at[n, c], partner)

    def scatter(n, c, o):
        peer = lax.rem(tm_x + o, n_x)
        return remote(
            part.at[c, pl.ds(core * half + peer * share, share)], ring_buf.at[c, o - 1],
            ss.at[n, c, o], sr.at[n, c, o], {"tm": peer * 2 + core})

    def gather(n, c, o):
        peer = lax.rem(tm_x + o, n_x)
        return remote(
            conv.at[c, own_share], conv.at[c, own_share],
            gs.at[n, c, o], gr.at[n, c, o], {"tm": peer * 2 + core})

    def pair_down(n, c, o):
        held = pl.ds(core * half + lax.rem(tm_x + n_x - o, n_x) * share, share)
        return remote(conv.at[c, held], conv.at[c, held], qs.at[n, c, o], qr.at[n, c, o], partner)

    def pair_down_recv(n, c):
        for o in range(n_x):
            pair_down(n, c, o).wait_recv()

    def guess_copy(o):
        return remote(guess, guess_all.at[tm], ds.at[o], dr.at[o], {"tm": lax.rem(tm + o, n_tm)})

    def guess_local():
        return pltpu.make_async_copy(guess, guess_all.at[tm], guess_own)

    def send_forward(n, c):
        for o in range(1, n_mom):
            forward(n, c, o).start()
        forward_own(n, c).start()

    def keep_stack(n, k, s, c, value):
        turned = rot(value)
        for at, piece in ((c * group, value), (PANEL + c * group, turned)):
            high, rest = split(piece)
            stk[n, 0, k, s, at:at + group, :] = high
            stk[n, 1, k, s, at:at + group, :] = rest

    def first_layout(c):
        @pl.loop(0, local_k)
        def _(k):
            for s in range(SPIN):
                at = ((c * SPIN + s) * group) * local_k + k
                flat_cur[pl.ds(at, group, stride=local_k), :] = start[k, s, c]

    def sigma(n, c):
        for o in range(1, n_mom):
            forward(n, c, o).wait_recv()
        forward_own(n, c).wait()
        if n > 0:
            for o in range(1, n_mom):
                back(n - 1, c, o).wait_send()

        @pl.loop(0, rows)
        def _(i):
            both = jnp.concatenate([recv[c, 0, i], recv[c, 1, i]], axis=1)
            sums = dot3((fwd_split[0], fwd_split[1]), split(both))
            site, mirrored = [], []
            for s in range(SPIN):
                with_cos = sums[:K, s * LANES:(s + 1) * LANES]
                turned = rot(sums[K:, s * LANES:(s + 1) * LANES])
                site.append(with_cos + turned)
                mirrored.append(with_cos - turned)
            first, second = site
            flipped = swap(second)
            pair = (first * jnp.where(low, second, flipped)
                    + rot(first) * jnp.where(low, flipped, second)) * wvec[...]
            pair_rot = rot(pair)
            tops, bottoms = [], []
            for s in range(SPIN):
                other = mirrored[1 - s]
                flipped = swap(other)
                value = pair * jnp.where(low, other, flipped) - pair_rot * jnp.where(low, flipped, other)
                tops.append(value)
                bottoms.append(-rot(value))
            stacked = jnp.concatenate(
                [jnp.concatenate(tops, axis=1), jnp.concatenate(bottoms, axis=1)], axis=0)
            result = dot3((back_split[0], back_split[1]), split(stacked))
            for s in range(SPIN):
                sig[c, s, i] = result[:, s * LANES:(s + 1) * LANES]

        for o in range(1, n_mom):
            back(n, c, o).start()
        back_own(n, c).start()

    def convolve(n, c):
        for o in range(1, n_mom):
            back(n, c, o).wait_recv()
        back_own(n, c).wait()
        if n > 0:
            pair_up(n - 1, c).wait_send()
            for o in range(n_x):
                pair_down(n - 1, c, o).wait_send()
            for o in range(1, n_x):
                scatter(n - 1, c, o).wait_send()
                gather(n - 1, c, o).wait_send()

        def some(base):
            @pl.loop(0, half, unroll=8)
            def _(i):
                k = base + i
                for s in range(SPIN):
                    at = ((c * SPIN + s) * group) * local_k + k
                    value = split(flat_ret[pl.ds(at, group, stride=local_k), :])
                    part[c, k, s] = dot3(value, (stk[n, 0, k, s], stk[n, 1, k, s]), True)

        some((1 - core) * half)
        pair_up(n, c).start()
        some(core * half)

    def reduce(n, c):
        pair_up(n, c).wait_recv()

        @pl.loop(0, half)
        def _(i):
            part[c, core * half + i] = part[c, core * half + i] + pair_buf[c, i]

        for o in range(1, n_x):
            scatter(n, c, o).start()
        for o in range(1, n_x):
            scatter(n, c, o).wait_recv()

        @pl.loop(0, share)
        def _(i):
            total = part[c, share_at + i]
            for o in range(1, n_x):
                total = total + ring_buf[c, o - 1, i]
            conv[c, share_at + i] = total

        for o in range(1, n_x):
            gather(n, c, o).start()
        pair_down(n, c, 0).start()
        for o in range(1, n_x):
            gather(n, c, o).wait_recv()
            pair_down(n, c, o).start()

    def update(n, c):
        for o in range(1, n_mom):
            forward(n, c, o).wait_send()

        def some(base):
            @pl.loop(0, half, unroll=8)
            def _(i):
                k = base + i
                for s in range(SPIN):
                    new = start[k, s, c] + step_scale * dot3(
                        split(conv[c, k, s]), (stk[n, 0, k, s], stk[n, 1, k, s]))
                    at = ((c * SPIN + s) * group) * local_k + k
                    flat_cur[pl.ds(at, group, stride=local_k), :] = new
                    keep_stack(n + 1, k, s, c, new)

        some(core * half)
        pair_down_recv(n, c)
        some((1 - core) * half)

    def finish(n):
        is_block = chosen[...] > 0.5

        def some(base):
            @pl.loop(0, half, unroll=4)
            def _(i):
                k = base + i
                for s in range(SPIN):
                    whole = jnp.concatenate([conv[c, k, s] for c in range(CHUNKS)], axis=0)
                    d = jnp.concatenate([guess_all[t, k, s] for t in range(n_tm)], axis=0)
                    first = jnp.concatenate([start[k, s, c] for c in range(CHUNKS)], axis=0)
                    panel = stk[n, 0, k, s].astype(jnp.float32) + stk[n, 1, k, s].astype(jnp.float32)
                    right = jnp.where(is_block, jnp.concatenate([whole, rot(whole)], axis=0), panel)
                    left = jnp.where(is_block, d, whole)
                    new = jnp.where(is_block, d, first) + step_scale * dot3(split(left), split(right))
                    for c in range(CHUNKS):
                        out[k, s, c] = new[c * group:(c + 1) * group, :]

        for c in range(CHUNKS - 1):
            pair_down_recv(n, c)
        some(core * half)
        pair_down_recv(n, CHUNKS - 1)
        some((1 - core) * half)

    first_layout(0)
    pl.semaphore_wait(barrier, n_mom + n_tm - 2)
    send_forward(0, 0)
    for c in range(1, CHUNKS):
        first_layout(c)
        send_forward(0, c)
    for o in range(1, n_tm):
        guess_copy(o).start()
    guess_local().start()

    for at, table in enumerate(tables(ordering[...])):
        fwd_split[0, at * K:(at + 1) * K, :], fwd_split[1, at * K:(at + 1) * K, :] = split(table)
        turned = split(table.T)
        back_split[0, :, at * K:(at + 1) * K], back_split[1, :, at * K:(at + 1) * K] = turned

    @pl.loop(0, local_k, unroll=4)
    def _(k):
        for s in range(SPIN):
            for c in range(CHUNKS):
                keep_stack(0, k, s, c, start[k, s, c])

    for n in range(PASSES):
        for c in range(CHUNKS):
            sigma(n, c)
        for c in range(CHUNKS):
            convolve(n, c)
            reduce(n, c)
            if n < PASSES - 1:
                update(n, c)
                send_forward(n + 1, c)

    for o in range(1, n_tm):
        guess_copy(o).wait_recv()
    guess_local().wait()
    finish(PASSES - 1)

    n = PASSES - 1
    for c in range(CHUNKS):
        pair_up(n, c).wait_send()
        for o in range(n_x):
            pair_down(n, c, o).wait_send()
        for o in range(1, n_x):
            scatter(n, c, o).wait_send()
            gather(n, c, o).wait_send()
        for o in range(1, n_mom):
            forward(n, c, o).wait_send()
            back(n, c, o).wait_send()
    for o in range(1, n_tm):
        guess_copy(o).wait_send()


def panel_step(n_mom, n_tm, start, guess, ordering, wvec, chosen):
    local_k = start.shape[0]
    group = start.shape[3]
    rows = group // n_mom
    share = local_k // n_tm
    panel = (CHUNKS, SPIN, n_mom, rows, local_k, LANES)
    sites = (CHUNKS, SPIN, rows, K, LANES)
    f32, bf16 = jnp.float32, jnp.bfloat16
    dma = pltpu.SemaphoreType.DMA
    vmem = pl.BlockSpec(memory_space=pltpu.VMEM)
    one, many_mom, many_x = (PASSES, CHUNKS), (PASSES, CHUNKS, n_mom), (PASSES, CHUNKS, n_tm // 2)
    return pl.pallas_call(
        functools.partial(step_kernel, n_mom, n_tm),
        out_shape=jax.ShapeDtypeStruct(start.shape, f32),
        in_specs=[vmem] * 5,
        out_specs=vmem,
        scratch_shapes=[
            pltpu.VMEM(panel, f32),
            pltpu.VMEM(sites, f32),
            pltpu.VMEM(sites, f32),
            pltpu.VMEM(panel, f32),
            pltpu.VMEM((2, 2 * K, K), bf16),
            pltpu.VMEM((2, K, 2 * K), bf16),
            pltpu.VMEM((PASSES, 2, local_k, SPIN, LANES, LANES), bf16),
            pltpu.VMEM((CHUNKS, local_k, SPIN, group, LANES), f32),
            pltpu.VMEM((CHUNKS, local_k, SPIN, group, LANES), f32),
            pltpu.VMEM((CHUNKS, local_k // 2, SPIN, group, LANES), f32),
            pltpu.VMEM((CHUNKS, max(n_tm // 2 - 1, 1), share, SPIN, group, LANES), f32),
            pltpu.VMEM((n_tm,) + guess.shape, f32),
            dma(one + (2,)), dma,
            dma(many_mom), dma(many_mom), dma(many_mom), dma(many_mom),
            dma(one), dma(one),
            dma(many_x), dma(many_x), dma(many_x), dma(many_x),
            dma(many_x), dma(many_x),
            dma((n_tm,)), dma((n_tm,)),
        ],
        compiler_params=pltpu.CompilerParams(
            collective_id=0, has_side_effects=True, vmem_limit_bytes=63 * 1024 * 1024),
        name="panel_step",
    )(start, guess, ordering, wvec, chosen)


SUBLANES = 8
CHUNK = 1
AHEAD = 2
LAG = 2
LEAD = (4, 7)
ARRIVE = 1
FINISH_AT = 7
BURST = 4
SIGMA_AT = 3
LAST_AT = 12
PANEL_AT = 6


def wide(left, right, transposed=False):
    rows = left[0].shape[0]
    dims = (((1,), (1 if transposed else 0,)), ((), ()))
    both = lax.dot_general(
        jnp.concatenate(left, axis=0), jnp.concatenate(right, axis=0 if transposed else 1), dims,
        preferred_element_type=jnp.float32)
    return both[:rows, :LANES] + (both[:rows, LANES:] + both[rows:, :LANES])


def block_transpose(blocks, lane, width):
    blocks = list(blocks)
    bit = 1
    while bit < len(blocks):
        keep = (lane // width) % (2 * bit) < bit
        for p in range(len(blocks)):
            if p & bit == 0:
                a, b = blocks[p], blocks[p + bit]
                blocks[p] = jnp.where(keep, a, pltpu.roll(b, bit * width, 1))
                blocks[p + bit] = jnp.where(keep, pltpu.roll(a, LANES - bit * width, 1), b)
        bit *= 2
    return blocks


def share_kernel(
    n, start, guess, ordering, coupling, slab_owner, expiring,
    result, out, out_sem, snd, recv, sig, rx_g, rx_s, stk_a, stk_b, wvec, rbuf, lbuf, tot, guess_all, fwd_split, back_split,
    fs, fr, gs, gr, ss, sr, ts, tr, rs, rr, ls, lr, credit, room,
    al, aps, apr, axs, axr, aqs, aqr,
):
    mom, tm = lax.axis_index("mom"), lax.axis_index("tm")
    local_k = start.shape[0]
    quarter = local_k // n
    rows = PANEL // n
    width = PANEL // n
    halves = rows // SUBLANES
    half_rows = n * SUBLANES
    subs = quarter // SUBLANES
    per_half = n * subs * SPIN
    pieces = halves * per_half
    chunks = rows // CHUNK
    half_chunks = SUBLANES // CHUNK
    n_x = n // 2
    tm_x, core = tm // 2, tm % 2
    partner = {"tm": tm_x * 2 + (1 - core)}
    step_scale = 1.0 / math.sqrt(PANEL)
    lane = lax.broadcasted_iota(jnp.int32, (1, LANES), 1)
    low = lane < PANEL
    sign = jnp.where(low, -1.0, 1.0).astype(jnp.float32)
    flat = n * rows * SPIN * local_k
    flat_snd = snd.reshape(flat, LANES)
    flat_rx_g = rx_g.reshape(flat, LANES)
    flat_rx_s = rx_s.reshape(flat, LANES)
    own_first = rx_g.reshape(local_k, SPIN, halves, half_rows, LANES)
    part = out.reshape(local_k, SPIN, halves, half_rows, LANES)
    stacks = (stk_a, stk_b)
    own_last = recv.reshape(halves, local_k, SPIN, half_rows, LANES)
    near_left = mom < n // 2

    def swap(x):
        return pltpu.roll(x, PANEL, 1)

    def rot(x):
        return swap(x) * sign

    barrier = pltpu.get_barrier_semaphore()
    for o in range(1, n):
        pl.semaphore_signal(barrier, inc=1, device_id={"mom": lax.rem(mom + o, n)}, device_id_type=MESH)
    for o in range(1, n):
        pl.semaphore_signal(barrier, inc=1, device_id={"tm": lax.rem(tm + o, n)}, device_id_type=MESH)

    def remote(source, target, send, recv_sem, device):
        return pltpu.make_async_remote_copy(
            src_ref=source, dst_ref=target, send_sem=send, recv_sem=recv_sem,
            device_id=device, device_id_type=MESH)

    def local(source, target, sem):
        return pltpu.make_async_copy(source, target, sem)

    def span(q):
        return pl.ds(q * CHUNK, CHUNK)

    def forward(q, o):
        peer = lax.rem(mom + o, n)
        return remote(snd.at[peer, span(q)], recv.at[span(q), :, mom], fs.at[o], fr.at[q], {"mom": peer})

    def forward_own(q):
        return local(snd.at[mom, span(q)], recv.at[span(q), :, mom], fr.at[q])

    def panel_out(q, o):
        peer = lax.rem(tm + o, n)
        return remote(recv.at[span(q), :, :, peer], rx_g.at[tm, span(q)], gs.at[o], gr.at[q // half_chunks], {"tm": peer})

    def panel_own(q):
        return local(recv.at[span(q), :, :, tm], rx_g.at[tm, span(q)], gr.at[q // half_chunks])

    def sigma_out(n_pass, q, o):
        peer = lax.rem(tm + o, n)
        return remote(
            sig.at[span(q), :, :, peer], rx_s.at[tm, span(q)], ss.at[n_pass, o], sr.at[n_pass, q // half_chunks],
            {"tm": peer})

    def sigma_own(n_pass, q):
        return local(sig.at[span(q), :, :, tm], rx_s.at[tm, span(q)], sr.at[n_pass, q // half_chunks])

    def place(p):
        half, rest = p // per_half, p % per_half
        group, turn = rest // n, rest % n
        odd = turn % 2
        block = (1 - odd) * (n - 1 - turn // 2) + odd * (turn // 2)
        return half, group // SPIN, group % SPIN, block

    def next_out(p, o):
        half, sub, s, block = place(p)
        peer = lax.rem(tm + o, n)
        at, ks = pl.ds(half * SUBLANES, SUBLANES), pl.ds(sub * SUBLANES, SUBLANES)
        return remote(
            snd.at[peer, at, s, block, ks], recv.at[at, s, block, tm, ks], ts.at[o], tr.at[half], {"tm": peer})

    def next_own(p):
        half, sub, s, block = place(p)
        at, ks = pl.ds(half * SUBLANES, SUBLANES), pl.ds(sub * SUBLANES, SUBLANES)
        return local(snd.at[tm, at, s, block, ks], recv.at[at, s, block, tm, ks], tr.at[half])

    def window(p):
        half, sub, s, block = place(p)
        return pl.ds(block * quarter + sub * SUBLANES, SUBLANES), s, half

    def whole(ref, sem):
        return local(ref, ref, sem)

    def sent(n_pass, p):
        half, _, _, block = place(p)
        return half if n_pass == 0 else block

    def right_out(n_pass, p):
        at = window(p)
        return remote(
            rbuf.at[at], rbuf.at[at], rs.at[n_pass, sent(n_pass, p)], rr.at[p],
            {"mom": jnp.minimum(mom + 1, n - 1)})

    def left_out(n_pass, p):
        at = window(p)
        return remote(
            lbuf.at[at], lbuf.at[at], ls.at[n_pass, sent(n_pass, p)], lr.at[p],
            {"mom": jnp.maximum(mom - 1, 0)})

    class Spread:
        def __init__(self, at, source, target):
            self.at, self.source, self.target = at, source, target

        def own(self):
            return local(self.source, self.target(tm), al.at[self.at])

        def pair(self):
            return remote(self.source, self.target(tm), aps.at[self.at], apr.at[self.at], partner)

        def across(self, o):
            peer = lax.rem(tm_x + o, n_x)
            return remote(
                self.source, self.target(tm), axs.at[self.at, o - 1], axr.at[self.at, o - 1], {"tm": peer * 2 + core})

        def relay(self, o):
            held = self.target(lax.rem(tm_x + n_x - o, n_x) * 2 + core)
            return remote(held, held, aqs.at[self.at, o - 1], aqr.at[self.at, o - 1], partner)

        def begin(self):
            for o in range(1, n_x):
                self.across(o).start()
            self.pair().start()
            self.own().start()

        def pass_on(self):
            for o in range(1, n_x):
                self.across(o).wait_recv()
                self.relay(o).start()

        def arrive(self):
            self.own().wait()
            self.pair().wait_recv()
            for o in range(1, n_x):
                self.relay(o).wait_recv()
                self.relay(o).wait_send()

        def end(self):
            self.pair().wait_send()
            for o in range(1, n_x):
                self.across(o).wait_send()

    guesses = Spread(0, guess, lambda t: guess_all.at[t])
    def firsts(half, sub, s):
        return Spread(
            1 + (half * subs + sub) * SPIN + s, tot.at[0, pl.ds(sub * SUBLANES, SUBLANES), s, half],
            lambda t: own_first.at[pl.ds(t * quarter + sub * SUBLANES, SUBLANES), s, half])

    def lasts(half, sub, s):
        return Spread(
            1 + ((halves + half) * subs + sub) * SPIN + s, tot.at[1, pl.ds(sub * SUBLANES, SUBLANES), s, half],
            lambda t: own_last.at[half, pl.ds(t * quarter + sub * SUBLANES, SUBLANES), s])

    def spread_rows(target, half, s, k, parts):
        for j, value in enumerate(block_transpose(parts, lane, width)):
            at = ((j * rows + half * SUBLANES) * SPIN + s) * local_k + k
            target[pl.ds(at, SUBLANES, stride=SPIN * local_k), :] = value

    def gather_rows(source, half, s, k):
        parts = []
        for t in range(n):
            at = ((t * rows + half * SUBLANES) * SPIN + s) * local_k + k
            parts.append(source[pl.ds(at, SUBLANES, stride=SPIN * local_k), :])
        return jnp.concatenate(block_transpose(parts, lane, width), axis=0)

    def first_layout(half):
        @pl.loop(0, local_k, unroll=8)
        def _(k):
            for s in range(SPIN):
                parts = [start[k, s, half * half_rows + g * SUBLANES:half * half_rows + (g + 1) * SUBLANES, :]
                         for g in range(n)]
                spread_rows(flat_snd, half, s, k, parts)

    def keep_stack(n_pass, k, s, half, value):
        for at, piece in enumerate((value, rot(value))):
            stacks[n_pass][k, s, 0, at, half], stacks[n_pass][k, s, 1, at, half] = split(piece)

    def stack_of(n_pass, k, s):
        return tuple(stacks[n_pass][k, s, at].reshape(2 * PANEL, LANES) for at in range(2))

    def first_stack(half):
        whole(rx_g.at[:, pl.ds(half * SUBLANES, SUBLANES)], gr.at[half]).wait()

        @pl.loop(0, local_k, unroll=8)
        def _(k):
            for s in range(SPIN):
                keep_stack(0, k, s, half, gather_rows(flat_rx_g, half, s, k))

    def sigma(q):
        @pl.loop(0, CHUNK)
        def _(d):
            i = q * CHUNK + d
            both = jnp.concatenate(
                [recv[i, s].reshape(K, LANES) for s in range(SPIN)], axis=1)
            sums = dot3((fwd_split[0], fwd_split[1]), split(both))
            site, mirrored = [], []
            for s in range(SPIN):
                with_cos = sums[:K, s * LANES:(s + 1) * LANES]
                turned = rot(sums[K:, s * LANES:(s + 1) * LANES])
                site.append(with_cos + turned)
                mirrored.append(with_cos - turned)
            first, second = site
            flipped = swap(second)
            pair = (first * jnp.where(low, second, flipped)
                    + rot(first) * jnp.where(low, flipped, second)) * wvec[...]
            pair_rot = rot(pair)
            tops, bottoms = [], []
            for s in range(SPIN):
                other = mirrored[1 - s]
                flipped = swap(other)
                value = pair * jnp.where(low, other, flipped) - pair_rot * jnp.where(low, flipped, other)
                tops.append(value)
                bottoms.append(-rot(value))
            stacked = jnp.concatenate(
                [jnp.concatenate(tops, axis=1), jnp.concatenate(bottoms, axis=1)], axis=0)
            result = dot3((back_split[0], back_split[1]), split(stacked))
            for s in range(SPIN):
                sig[i, s] = result[:, s * LANES:(s + 1) * LANES].reshape(sig.shape[2:])

    def send_sigma(n_pass, q):
        for o in range(1, n):
            sigma_out(n_pass, q, o).start()
        sigma_own(n_pass, q).start()

    def wait_sigma(n_pass, half):
        whole(rx_s.at[:, pl.ds(half * SUBLANES, SUBLANES)], sr.at[n_pass, half]).wait()

    def second_sigma(q):
        half = q // half_chunks

        @pl.when(q == 0)
        def _():
            for o in range(1, n):
                whole(sig.at[:, :, :, 0], ss.at[0, o]).wait()

        @pl.when(q % half_chunks == 0)
        def _():
            whole(recv.at[pl.ds(half * SUBLANES, SUBLANES)], tr.at[half]).wait()

        sigma(q)
        send_sigma(1, q)

    def convolve(n_pass, p):
        half, sub, s, block = place(p)

        @pl.when(p % per_half == 0)
        def _():
            wait_sigma(n_pass, half)

        results = []
        for m in range(SUBLANES):
            k = block * quarter + sub * SUBLANES + m
            value = split(gather_rows(flat_rx_s, half, s, k))
            results.append((k, wide(value, stack_of(n_pass, k, s), True)))
        for k, result in results:
            part[k, s, half] = result

    def each(p, body):
        half, sub, s, block = place(p)
        done = [body((block * quarter + sub * SUBLANES + m, s, half), sub * SUBLANES + m) for m in range(SUBLANES)]
        for stores in done:
            for target, at, value in stores:
                target[at] = value

    def flows(n_pass, p):
        block = place(p)[3]
        if n_pass == 0:
            yes = block >= 0
            return yes, yes, yes, yes, yes
        return block >= mom, block > mom, block <= mom, block < mom, block == mom

    def origin(n_pass, p):
        _, send_right, _, send_left, _ = flows(n_pass, p)

        @pl.when(mom == 0)
        def _():
            each(p, lambda at, m: [(rbuf, at, part[at])])

            @pl.when(send_right)
            def _():
                right_out(n_pass, p).start()

        @pl.when(mom == n - 1)
        def _():
            each(p, lambda at, m: [(lbuf, at, part[at])])

            @pl.when(send_left)
            def _():
                left_out(n_pass, p).start()

    def near_step(n_pass, p):
        from_left, send_right, from_right, send_left, _ = flows(n_pass, p)

        @pl.when(near_left & (mom > 0) & from_left)
        def _():
            right_out(n_pass, p).wait_recv()

            each(p, lambda at, m: [(rbuf, at, rbuf[at] + part[at])])

            @pl.when(send_right)
            def _():
                right_out(n_pass, p).start()

        @pl.when((mom >= n // 2) & (mom < n - 1) & from_right)
        def _():
            left_out(n_pass, p).wait_recv()

            each(p, lambda at, m: [(lbuf, at, lbuf[at] + part[at])])

            @pl.when(send_left)
            def _():
                left_out(n_pass, p).start()

    def far_step(n_pass, p):
        from_left, send_right, from_right, send_left, keep = flows(n_pass, p)

        def one(mine, other, outer, send, copy):
            copy.wait_recv()
            if n_pass == 0:
                each(p, lambda at, m: [
                    (other, at, other[at] + part[at]), (part, at, mine[at] + other[at])])
            else:
                @pl.when(send)
                def _():
                    each(p, lambda at, m: [(other, at, other[at] + part[at])])

                @pl.when(keep)
                def _():
                    each(p, lambda at, m: [(tot, (1, m) + at[1:], mine[at] + other[at])])

            @pl.when(outer & send)
            def _():
                copy.start()

        @pl.when(near_left & from_right)
        def _():
            one(rbuf, lbuf, mom > 0, send_left, left_out(n_pass, p))

        @pl.when((mom >= n // 2) & from_left)
        def _():
            one(lbuf, rbuf, mom < n - 1, send_right, right_out(n_pass, p))

    def update(p):
        half, sub, s, block = place(p)

        @pl.when(block == mom)
        def _():
            each(p, lambda at, m: [(tot, (0, m) + at[1:], part[at])])

            @pl.when(half < halves - 1)
            def _():
                firsts(half, sub, s).begin()

        results = []
        for m in range(SUBLANES):
            k = block * quarter + sub * SUBLANES + m
            old = stk_a[k, s, 0, 0, half].astype(jnp.float32) + stk_a[k, s, 1, 0, half].astype(jnp.float32)
            results.append((k, old + step_scale * wide(split(part[k, s, half]), stack_of(0, k, s))))
        for k, new in results:
            keep_stack(1, k, s, half, new)
            spread_rows(flat_snd, half, s, k, [new[g * SUBLANES:(g + 1) * SUBLANES, :] for g in range(n)])

        for o in range(1, n):
            next_out(p, o).start()
        next_own(p).start()

    def own_panel(group):
        results = []
        for m in range(SUBLANES // 2):
            k = group * (SUBLANES // 2) + m
            for s in range(SPIN):
                first = start[k, s]
                right = split(jnp.concatenate([first, rot(first)], axis=0))
                new = first + step_scale * wide(split(own_first[k, s].reshape(PANEL, LANES)), right)
                results.append((k, s, new))
        for k, s, new in results:
            own_first[k, s] = new.reshape(halves, half_rows, LANES)

    def store(sub, s):
        parts = (n, quarter, SPIN, PANEL, LANES)
        at = pl.ds(sub * SUBLANES, SUBLANES)
        return local(
            out.reshape(parts).at[:, at, s], result.reshape(parts).at[:, at, s], out_sem.at[sub * SPIN + s])

    def finish(d):
        sub, s, t = d // n // SPIN, d // n % SPIN, d % n
        is_block = chosen > 0.5

        @pl.when(t == 0)
        def _():
            for half in range(halves):
                lasts(half, sub, s).pass_on()
            for half in range(halves):
                lasts(half, sub, s).arrive()

        results = []
        for m in range(SUBLANES):
            k = t * quarter + sub * SUBLANES + m
            whole = jnp.concatenate([own_last[half, k, s] for half in range(halves)], axis=0)
            d_rows = jnp.concatenate([guess_all[at, k, s] for at in range(n)], axis=0)
            right = jnp.where(is_block, whole, own_first[k, s].reshape(PANEL, LANES))
            left = jnp.where(is_block, d_rows, whole)
            right = split(jnp.concatenate([right, rot(right)], axis=0))
            new = jnp.where(is_block, d_rows, start[k, s]) + step_scale * wide(split(left), right)
            results.append((k, new))
        for k, new in results:
            out[k, s] = new

        @pl.when(t == n - 1)
        def _():
            store(sub, s).start()

    def begin_forward(q):
        for o in range(1, n):
            forward(q, o).start()
        forward_own(q).start()

    first_layout(0)
    pl.semaphore_wait(barrier, 2 * n - 2)
    for q in range(min(AHEAD, half_chunks)):
        begin_forward(q)
    for half in range(1, halves):
        first_layout(half)

    for at, table in enumerate(tables(ordering[...])):
        fwd_split[0, at * K:(at + 1) * K, :], fwd_split[1, at * K:(at + 1) * K, :] = split(table)
        turned = split(table.T)
        back_split[0, :, at * K:(at + 1) * K], back_split[1, :, at * K:(at + 1) * K] = turned

    owners = slab_owner[...].astype(jnp.float32)
    slabs = lax.broadcasted_iota(jnp.int32, owners.shape, 1).astype(jnp.float32)
    oldest = expiring[...].astype(jnp.float32)
    mine = tm.astype(jnp.float32)
    slab_mine = jnp.sum(jnp.where(owners == mine, slabs, 0.0), axis=1, keepdims=True)
    owner_expiring = jnp.sum(jnp.where(slabs == oldest, owners, 0.0), axis=1, keepdims=True)
    position = slab_mine - oldest
    position = jnp.where(position < 0.0, position + n, position)
    held = (mom * rows + lane % rows).astype(jnp.float32)
    ahead = (n * PANEL - 1) - (position * PANEL + held)
    strength = coupling[...] * coupling[...]
    wvec[...] = strength * (jnp.exp(-1.5 * ahead / (n * PANEL)) / math.sqrt(n * PANEL))
    chosen = jnp.where(owner_expiring == mine, jnp.ones((1, LANES), jnp.float32), 0.0)

    @pl.loop(0, chunks + 1)
    def _(q):
        @pl.when(q < chunks)
        def _():
            whole(recv.at[span(q)], fr.at[q]).wait()

            @pl.when(q + AHEAD < chunks)
            def _():
                begin_forward(q + AHEAD)

            for o in range(1, n):
                panel_out(q, o).start()
            panel_own(q).start()
            sigma(q)
            send_sigma(0, q)

        for half in range(halves - 1):
            @pl.when(q == (half + 1) * half_chunks + 1)
            def _():
                first_stack(half)

        @pl.when(q == chunks)
        def _():
            first_stack(halves - 1)

    for o in range(1, n):
        whole(snd.at[0], fs.at[o]).wait()
        whole(recv.at[:, :, :, 0], gs.at[o]).wait()

    for o in range(1, n):
        pl.semaphore_signal(room, inc=1, device_id={"tm": lax.rem(tm + o, n)}, device_id_type=MESH)
    guesses.begin()

    def within(low, x, high):
        return (x >= low) & (x < high)

    lead, rest = LEAD[0], LEAD[1] + LAG
    told = lead + LAG
    first_sigma_at = told + per_half + ARRIVE
    last_sigma_at = told + pieces + SIGMA_AT
    last_at = told + per_half + ARRIVE + LAST_AT
    panel_at = last_at + (halves - 1) * (per_half + rest) + PANEL_AT
    period = per_half + rest

    def last_piece(u, body):
        seg, at = u // period, u % period

        @pl.when((u >= 0) & (seg < halves) & (at < per_half))
        def _():
            body(seg * per_half + at)

    def last_start(p):
        for half in range(halves):
            @pl.when(p == half * per_half)
            def _():
                @pl.when(mom > 0)
                def _():
                    pl.semaphore_wait(credit.at[half, 0], 1)

                @pl.when(mom < n - 1)
                def _():
                    pl.semaphore_wait(credit.at[half, 1], 1)

        convolve(1, p)
        origin(1, p)

    def last_far(p):
        far_step(1, p)
        half, sub, s, block = place(p)

        @pl.when(block == mom)
        def _():
            lasts(half, sub, s).begin()

        d = p - (pieces - per_half) - FINISH_AT

        @pl.when(d >= 0)
        def _():
            finish(d)

    def free(half):
        @pl.when(mom < n - 1)
        def _():
            whole(rbuf.at[:, :, half], rs.at[0, half]).wait()

        @pl.when(mom > 0)
        def _():
            whole(lbuf.at[:, :, half], ls.at[0, half]).wait()

        @pl.when(mom > 0)
        def _():
            pl.semaphore_signal(
                credit.at[half, 1], inc=1, device_id={"mom": jnp.maximum(mom - 1, 0)}, device_id_type=MESH)

        @pl.when(mom < n - 1)
        def _():
            pl.semaphore_signal(
                credit.at[half, 0], inc=1, device_id={"mom": jnp.minimum(mom + 1, n - 1)}, device_id_type=MESH)

    @pl.loop(0, last_at + halves * period)
    def _(t):
        @pl.when(t < pieces)
        def _():
            convolve(0, t)
            origin(0, t)

        @pl.when(within(lead, t, lead + pieces))
        def _():
            near_step(0, t - lead)

        @pl.when(within(told, t, told + pieces))
        def _():
            p = t - told
            far_step(0, p)

            @pl.when(p == 0)
            def _():
                pl.semaphore_wait(room, n - 1)

            update(p)

        for half in range(halves):
            @pl.when(t == told + (half + 1) * per_half + ARRIVE + 1)
            def _():
                free(half)

        @pl.when(t == told + per_half)
        def _():
            guesses.pass_on()

        @pl.when(within(first_sigma_at, t, first_sigma_at + (halves - 1) * half_chunks))
        def _():
            second_sigma(t - first_sigma_at)

        last_piece(t - last_at, last_start)
        last_piece(t - last_at - LEAD[1], lambda p: near_step(1, p))
        last_piece(t - last_at - rest, last_far)

        @pl.when(within(last_sigma_at, t, last_sigma_at + half_chunks // BURST))
        def _():
            @pl.loop(0, BURST)
            def _(d):
                second_sigma((halves - 1) * half_chunks + (t - last_sigma_at) * BURST + d)

        @pl.when(t == last_sigma_at + half_chunks // BURST)
        def _():
            @pl.loop(0, subs * SPIN)
            def _(d):
                firsts(halves - 1, d // SPIN, d % SPIN).begin()

        @pl.when(t == panel_at)
        def _():
            @pl.loop(0, halves * subs * SPIN)
            def _(d):
                firsts(d // (subs * SPIN), d // SPIN % subs, d % SPIN).pass_on()

            @pl.loop(0, halves * subs * SPIN)
            def _(d):
                firsts(d // (subs * SPIN), d // SPIN % subs, d % SPIN).arrive()

            guesses.arrive()

        @pl.when(within(panel_at, t, panel_at + local_k // SUBLANES))
        def _():
            own_panel(2 * (t - panel_at))
            own_panel(2 * (t - panel_at) + 1)

    @pl.loop(per_half - FINISH_AT, per_half)
    def _(d):
        finish(d)

    for block in range(n):
        ks = pl.ds(block * quarter, quarter)

        @pl.when((mom < n - 1) & (block > mom))
        def _():
            whole(rbuf.at[ks], rs.at[1, block]).wait()

        @pl.when((mom > 0) & (block < mom))
        def _():
            whole(lbuf.at[ks], ls.at[1, block]).wait()

    for o in range(1, n):
        whole(snd.at[0], ts.at[o]).wait()
        whole(sig.at[:, :, :, 0], ss.at[1, o]).wait()

    @pl.loop(0, halves * subs * SPIN)
    def _(d):
        at = d // (subs * SPIN), d // SPIN % subs, d % SPIN
        firsts(*at).end()
        lasts(*at).end()

    guesses.end()
    for sub in range(subs):
        for s in range(SPIN):
            store(sub, s).wait()


def share_step(n, start, guess, ordering, coupling, slab_owner, expiring):
    local_k = start.shape[0]
    quarter, rows = local_k // n, PANEL // n
    halves, subs = rows // SUBLANES, quarter // SUBLANES
    pieces, chunks = halves * n * subs * SPIN, rows // CHUNK
    spreads, far = 1 + 2 * halves * subs * SPIN, max(n // 2 - 1, 1)
    half_rows = n * SUBLANES
    f32, bf16 = jnp.float32, jnp.bfloat16
    dma = pltpu.SemaphoreType.DMA
    vmem = pl.BlockSpec(memory_space=pltpu.VMEM)
    moved = pltpu.VMEM((n, rows, SPIN, n, quarter, LANES), f32)
    grid = pltpu.VMEM((rows, SPIN, n, n, quarter, LANES), f32)
    square = (local_k, SPIN, halves, half_rows, LANES)
    stack = pltpu.VMEM((local_k, SPIN, 2, 2, halves, half_rows, LANES), bf16)
    return pl.pallas_call(
        functools.partial(share_kernel, n),
        out_shape=jax.ShapeDtypeStruct(start.shape, f32),
        in_specs=[vmem, pl.BlockSpec(memory_space=pl.ANY)] + [vmem] * 4,
        out_specs=pl.BlockSpec(memory_space=pl.ANY),
        scratch_shapes=[
            pltpu.VMEM(start.shape, f32), dma((subs * SPIN,)),
            moved, grid, grid, moved, moved,
            stack, stack, pltpu.VMEM((1, LANES), f32),
            pltpu.VMEM(square, f32), pltpu.VMEM(square, f32),
            pltpu.VMEM((PASSES, quarter) + square[1:], f32),
            pltpu.VMEM((n,) + guess.shape, f32),
            pltpu.VMEM((2, 2 * K, K), bf16),
            pltpu.VMEM((2, K, 2 * K), bf16),
            dma((n,)), dma((chunks,)), dma((n,)), dma((halves,)),
            dma((PASSES, n)), dma((PASSES, halves)), dma((n,)), dma((halves,)),
            dma((PASSES, max(n, halves))), dma((pieces,)), dma((PASSES, max(n, halves))), dma((pieces,)),
            pltpu.SemaphoreType.REGULAR((halves, 2)), pltpu.SemaphoreType.REGULAR,
            dma((spreads,)), dma((spreads,)), dma((spreads,)),
            dma((spreads, far)), dma((spreads, far)), dma((spreads, far)), dma((spreads, far)),
        ],
        compiler_params=pltpu.CompilerParams(
            collective_id=0, has_side_effects=True, vmem_limit_bytes=63 * 1024 * 1024),
        name="share_step",
    )(start, guess, ordering, coupling, slab_owner, expiring)


def body(panel_start, block_guess, coupling, slab_owner, expiring, ordering):
    slab_count = lax.axis_size("tm")
    n_mom = lax.axis_size("mom")
    local_k = panel_start.shape[0]
    unit = SUBLANES * slab_count
    if n_mom == slab_count and local_k % unit == 0 and PANEL % unit == 0:
        return share_step(
            n_mom, panel_start, block_guess, ordering[None, :], coupling[None, :], slab_owner[None, :], expiring[None, :])
    own_index = lax.axis_index("tm")
    blocks = jnp.arange(slab_count, dtype=jnp.int32)
    slab_mine = jnp.sum(blocks * (slab_owner == own_index).astype(jnp.int32))
    position = (slab_mine - expiring[0]) % slab_count
    window = slab_count * PANEL
    times = position * PANEL + jnp.arange(PANEL, dtype=jnp.int32)
    weights = jnp.exp(-1.5 * (window - 1 - times).astype(jnp.float32) / window) / math.sqrt(window)
    strength = coupling[0] * coupling[0]
    wvec = (strength * jnp.concatenate([weights, weights]))[None, :]
    owner_expiring = jnp.sum(slab_owner * (blocks == expiring[0]).astype(jnp.int32))
    chosen = jnp.broadcast_to((own_index == owner_expiring).astype(jnp.float32), (1, LANES))
    start = panel_start.reshape(local_k, SPIN, CHUNKS, PANEL // CHUNKS, LANES)
    result = panel_step(n_mom, slab_count, start, block_guess, ordering[None, :], wvec, chosen)
    return result.reshape(panel_start.shape)


def solution(mesh):
    return jax.shard_map(
        body,
        mesh=mesh,
        in_specs=(
            P("mom", "groups", None, "tm"),
            P("mom", "groups", "tm", None),
            P("groups"),
            P("groups"),
            P("groups"),
            P(),
        ),
        out_specs=P("mom", "groups", None, "tm"),
        check_vma=False,
    )
```
